32 devices in a mesh: seq: 4 (over y, core), fsdp: 8 (over z, x).
Axes of the slice: x: 2, y: 2, z: 4, core: 2. Of those that a mesh axis runs over, the one named last changes fastest.
Arguments:
- latents: bfloat16 [8, 1536, 1536], P('fsdp', 'seq'), may hold values from -48 to 48
- qkv_weight: bfloat16 [1536, 768], P('fsdp'), may hold values from -1 to 1
- out_weight: bfloat16 [256, 1536], P('fsdp'), may hold values from -0.375 to 0.375
- tile_mask: int32 [4, 4], replicated, may hold values from 0 to 1, as said below
- tile_counts: int32 [4], replicated, may hold values from 64 to 384, as said below
Outputs:
- layer_out: bfloat16 [8, 1536, 1536], P('fsdp', 'seq')
The draws below stay inside these ranges and needn't reach their ends.
Inputs may be any that keep to these rules, and one draw needn't show every extreme that they name: `tile_mask`: tiles are numbered frame first, then 2 along the height, then 2 along the width. Row q marks a box of whole tiles that contains tile q, of at most 4 tiles; row 0 marks exactly 4. `tile_counts`: the real tokens of a tile fill its first slots. Only tiles on the last frame index may be partial; a partial tile holds k * 64 tokens for some k of 1 to 6, the first tile of the last frame index is full, and the last tile is partial with k of 1 to 5.
All inputs are finite; a program needn't handle non-finite values.
Results may differ from the reference program's by a relative error of at most 0.0074.
Values may be sent and summed in bfloat16 or wider, within the bound.
No kernel may reach another device: no remote copies, remote signals or barrier semaphores. Data moves between devices by JAX's collectives and lax.ppermute only.
A program may use at most 64 MiB of HBM per device.

```python
import jax
import jax.numpy as jnp
from jax import lax

D = 1536
E = 64
TILE = 384
TILE_H = 2
TILE_W = 2
WINDOW = 4
HEADS = 4
NT = 4
TF = 1
L = 1536
BATCH = 8


def tile_coords():
    tiles = jnp.arange(NT, dtype=jnp.int32)
    frame = tiles // (TILE_H * TILE_W)
    height = tiles // TILE_W % TILE_H
    across = tiles % TILE_W
    return (tiles, frame, height, across)


def draw_latents(key, part):
    base = jnp.clip(jax.random.normal(jax.random.fold_in(key, 1), (BATCH, L, D), jnp.float32), -6.0, 6.0)
    return base.astype(jnp.bfloat16)


def draw_qkv_weight(key, part):
    base = jnp.clip(jax.random.normal(jax.random.fold_in(key, 5), (D, 3 * HEADS * E), jnp.float32), -6.0, 6.0) * float(D) ** (-0.5)
    return base.astype(jnp.bfloat16)


def draw_tile_mask(key, part):
    tiles, frame, height, across = tile_coords()
    extra = jax.random.randint(jax.random.fold_in(key, 11), (3, NT), 0, 2)
    ext_f = jnp.minimum(1 + extra[0], TF)
    ext_h = jnp.minimum(1 + extra[1], TILE_H)
    ext_w = jnp.minimum(1 + extra[2], TILE_W)
    too_many = ext_f * ext_h * ext_w > WINDOW
    ext_f = jnp.where(too_many, 1, ext_f)
    first_tile = tiles == 0
    ext_f = jnp.where(first_tile, 1, ext_f)
    ext_h = jnp.where(first_tile, 2, ext_h)
    ext_w = jnp.where(first_tile, 2, ext_w)
    shifts = jax.random.randint(jax.random.fold_in(key, 12), (3, NT), 0, 2)
    start_f = jnp.clip(frame - shifts[0] % ext_f, 0, TF - ext_f)
    start_h = jnp.clip(height - shifts[1] % ext_h, 0, TILE_H - ext_h)
    start_w = jnp.clip(across - shifts[2] % ext_w, 0, TILE_W - ext_w)
    inside_f = (frame[None, :] >= start_f[:, None]) & (frame[None, :] < (start_f + ext_f)[:, None])
    inside_h = (height[None, :] >= start_h[:, None]) & (height[None, :] < (start_h + ext_h)[:, None])
    inside_w = (across[None, :] >= start_w[:, None]) & (across[None, :] < (start_w + ext_w)[:, None])
    return (inside_f & inside_h & inside_w).astype(jnp.int32)


def draw_tile_counts(key, part):
    tiles, frame, height, across = tile_coords()
    last_frame = frame == TF - 1
    full_one = last_frame & (height == 0) & (across == 0)
    kept_frames = jax.random.randint(jax.random.fold_in(key, 21), (NT,), 1, 7)
    last_kept = jax.random.randint(jax.random.fold_in(key, 22), (NT,), 1, 6)
    kept_frames = jnp.where(tiles == NT - 1, last_kept, kept_frames)
    partial_counts = kept_frames * TILE // 6
    ragged = last_frame & jnp.logical_not(full_one)
    return jnp.where(ragged, partial_counts, TILE).astype(jnp.int32)


def steps_of(own_key, extent, shards, smallest, largest):
    factor_of = 1.0
    for position, parts in shards:
        heights = jax.random.uniform(jax.random.fold_in(jax.random.fold_in(own_key, 6), position), (parts,), jnp.float32, smallest / len(shards), largest / len(shards))
        factor_of = factor_of * jnp.repeat(jnp.exp(heights), extent[position] // parts).reshape((-1,) + (1,) * (len(extent) - 1 - position))
    return factor_of


def bell_draw(rng, extent, scale, reach, pieces=(), kind=jnp.bfloat16):
    factor_of = steps_of(rng, extent, pieces, -0.22, 0.18) if pieces else 1.0
    array = jax.random.normal(rng, extent, jnp.float32) * scale * factor_of
    return jnp.minimum(jnp.maximum(array, -reach), reach).astype(kind)


def setup_inputs(seed: int = 0) -> dict:
    key_of = jax.random.split(jax.random.key(seed), 6)
    return {
        "latents": draw_latents(jax.random.fold_in(key_of[5], 71), 0),
        "qkv_weight": draw_qkv_weight(jax.random.fold_in(key_of[5], 71), 0),
        "out_weight": bell_draw(key_of[2], (HEADS * E, D), (HEADS * E) ** -0.5, 0.375, ((0, 8),)),
        "tile_mask": draw_tile_mask(jax.random.fold_in(key_of[5], 71), 0),
        "tile_counts": draw_tile_counts(jax.random.fold_in(key_of[5], 71), 0),
    }


def reference(latents, qkv_weight, out_weight, tile_mask, tile_counts):
    score_scale = float(E) ** -0.5
    token_live = (jnp.arange(TILE, dtype=jnp.int32)[None, :] < tile_counts[:, None]).reshape(L)

    def one_video(video_rows):
        projected = jnp.dot(video_rows, qkv_weight, preferred_element_type=jnp.float32).astype(jnp.bfloat16)
        projected = projected.reshape(L, 3, HEADS, E)

        def one_head(head_index):
            queries = projected[:, 0, head_index]
            keys = projected[:, 1, head_index]
            values = projected[:, 2, head_index]

            def one_tile(tile_index):
                start = (tile_index * TILE).astype(jnp.int32)
                query_block = lax.dynamic_slice_in_dim(queries, start, TILE, 0)
                scores = lax.dot_general(query_block, keys, (((1,), (1,)), ((), ())), preferred_element_type=jnp.float32) * score_scale
                allowed = jnp.repeat(tile_mask[tile_index] > 0, TILE)[None, :] & token_live[None, :]
                masked = jnp.where(allowed, scores, -1e30)
                row_max = jnp.max(masked, axis=1, keepdims=True)
                numerators = jnp.where(allowed, jnp.exp(masked - row_max), 0.0)
                denominator = jnp.sum(numerators, axis=1, keepdims=True)
                softmax_top = numerators.astype(jnp.bfloat16)
                summed = jnp.dot(softmax_top, values, preferred_element_type=jnp.float32) / denominator
                query_live = lax.dynamic_slice_in_dim(token_live, start, TILE, 0)
                return jnp.where(query_live[:, None], summed, 0.0).astype(jnp.bfloat16)

            return lax.map(one_tile, jnp.arange(NT, dtype=jnp.int32)).reshape(L, E)

        head_outputs = lax.map(one_head, jnp.arange(HEADS, dtype=jnp.int32))
        attended = jnp.transpose(head_outputs, (1, 0, 2)).reshape(L, HEADS * E)
        return jnp.dot(attended, out_weight, preferred_element_type=jnp.float32).astype(jnp.bfloat16)

    return lax.map(one_video, latents)
```

```python
import jax
import jax.numpy as jnp
from jax import lax
from jax.experimental import pallas as pl
from jax.experimental.pallas import tpu as pltpu
from jax.sharding import PartitionSpec as P

E = 64
TILE = 384
LANES = 128
CORES = 2
NEG = -1e30

VMEM = pl.BlockSpec(memory_space=pltpu.VMEM)
SMEM = pl.BlockSpec(memory_space=pltpu.SMEM)


def grid_of(fsdp_count):
    x_count = 1
    while (2 * x_count) ** 2 <= fsdp_count and fsdp_count % (2 * x_count) == 0:
        x_count *= 2
    return fsdp_count // x_count, x_count


def z_rotation(z_count, x_count, step):
    return [(z * x_count + x, (z + step) % z_count * x_count + x) for z in range(z_count) for x in range(x_count)]


def x_rotation(z_count, x_count, step):
    return [(z * x_count + x, z * x_count + (x + step) % x_count) for z in range(z_count) for x in range(x_count)]


def core_swap(seq_count):
    return [(s, s ^ 1) for s in range(seq_count)]


def y_rotation(seq_count, step):
    return [(s, (s + CORES * step) % seq_count) for s in range(seq_count)]


def call(kernel, out_shape, in_specs, out_specs, scratch_shapes=(), name=None):
    return pl.pallas_call(
        kernel,
        out_shape=out_shape,
        in_specs=in_specs,
        out_specs=out_specs,
        scratch_shapes=scratch_shapes,
        name=name,
    )


def halves(qkv_weight, out_weight, core):
    rows, columns = qkv_weight.shape
    head_columns = columns // 3
    own_columns = head_columns // CORES
    out_rows, width = out_weight.shape
    own_width = width // CORES

    def kernel(core_ref, qkv_ref, out_ref, qkv_half_ref, out_half_ref):
        which = core_ref[0]
        for part in range(3):
            start = pl.multiple_of(part * head_columns + which * own_columns, LANES)
            qkv_half_ref[:, part * own_columns : (part + 1) * own_columns] = qkv_ref[:, pl.ds(start, own_columns)]
        out_half_ref[...] = out_ref[:, pl.ds(pl.multiple_of(which * own_width, LANES), own_width)]

    return call(
        kernel,
        (
            jax.ShapeDtypeStruct((rows, 3 * own_columns), qkv_weight.dtype),
            jax.ShapeDtypeStruct((out_rows, own_width), out_weight.dtype),
        ),
        [SMEM, VMEM, VMEM],
        (VMEM, VMEM),
        name="halves",
    )(core, qkv_weight, out_weight)


def project(positions, core, blocks, latents_own, latents_other):
    count = len(blocks)
    rows, columns = blocks[0].shape
    depth = count * rows
    own_columns = columns // 3
    row_count = latents_own.shape[0]
    dtype = latents_own.dtype

    def kernel(position_ref, core_ref, *refs):
        block_refs = refs[:count]
        own_ref, other_ref, queries_own_ref, queries_other_ref, key_value_ref, weight_ref = refs[count:]
        for block, block_ref in enumerate(block_refs):
            start = pl.multiple_of(position_ref[block] * rows, 16)
            weight_ref[pl.ds(start, rows), :] = block_ref[...]
        which = core_ref[0]
        weight = weight_ref[...]
        for latents_ref, queries_ref, place in ((own_ref, queries_own_ref, which), (other_ref, queries_other_ref, 1 - which)):
            projected = jnp.dot(latents_ref[...], weight, preferred_element_type=jnp.float32).astype(dtype)
            queries_ref[...] = projected[:, :own_columns]
            key_value_ref[pl.ds(pl.multiple_of(place * row_count, 16), row_count), :] = projected[:, own_columns:]

    return call(
        kernel,
        (
            jax.ShapeDtypeStruct((row_count, own_columns), dtype),
            jax.ShapeDtypeStruct((row_count, own_columns), dtype),
            jax.ShapeDtypeStruct((CORES * row_count, 2 * own_columns), dtype),
        ),
        [SMEM, SMEM] + [VMEM] * (count + 2),
        (VMEM, VMEM, VMEM),
        [pltpu.VMEM((depth, columns), dtype)],
        name="project",
    )(positions, core, *blocks, latents_own, latents_other)


def attend(place, tile_mask, tile_counts, queries_own, queries_other, key_values):
    chips = len(key_values)
    row_count, own_columns = queries_own.shape
    dtype = queries_own.dtype
    per_group = LANES // E
    scale = float(E) ** -0.5
    rows = row_count // 2

    def kernel(place_ref, mask_ref, count_ref, own_ref, other_ref, *refs):
        key_value_refs = refs[:chips]
        attended_own_ref, attended_other_ref = refs[chips:]
        chip = place_ref[0]
        which = place_ref[1]
        slot = lax.broadcasted_iota(jnp.int32, (1, row_count), 1)
        lane = lax.broadcasted_iota(jnp.int32, (1, LANES), 1)
        for queries_ref, attended_ref, member in ((own_ref, attended_own_ref, which), (other_ref, attended_other_ref, 1 - which)):
            tile = CORES * chip + member
            biases = []
            for step in range(chips):
                key_chip = lax.rem(chip + chips - step, chips)
                for key_member in range(CORES):
                    key_tile = CORES * key_chip + key_member
                    live = jnp.where(mask_ref[tile, key_tile] > 0, count_ref[key_tile], 0)
                    biases.append(jnp.where(slot < live, 0.0, NEG))
            bias = jnp.concatenate(biases, axis=1)
            for group in range(own_columns // LANES):
                columns = slice(group * LANES, (group + 1) * LANES)
                value_columns = slice(own_columns + group * LANES, own_columns + (group + 1) * LANES)
                keys = jnp.concatenate([ref[:, columns] for ref in key_value_refs], axis=0)
                values = jnp.concatenate([ref[:, value_columns] for ref in key_value_refs], axis=0)
                for start in range(0, row_count, rows):
                    queries = queries_ref[start : start + rows, columns] * jnp.asarray(scale, dtype)
                    position = start + lax.broadcasted_iota(jnp.int32, (rows, 1), 0)
                    attended = jnp.zeros((rows, LANES), jnp.float32)
                    for head in range(per_group):
                        inside = (lane >= head * E) & (lane < (head + 1) * E)
                        head_queries = jnp.where(inside, queries, jnp.zeros_like(queries))
                        scores = lax.dot_general(
                            head_queries, keys, (((1,), (1,)), ((), ())), preferred_element_type=jnp.float32
                        )
                        scores = scores + bias
                        numerators = jnp.exp(scores - jnp.max(scores, axis=1, keepdims=True))
                        denominator = jnp.sum(numerators, axis=1, keepdims=True)
                        summed = jnp.dot(numerators.astype(dtype), values, preferred_element_type=jnp.float32)
                        factor = jnp.where(position < count_ref[tile], 1.0 / denominator, 0.0)
                        attended = jnp.where(inside, summed * factor, attended)
                    attended_ref[start : start + rows, columns] = attended.astype(dtype)

    shape = jax.ShapeDtypeStruct((row_count, own_columns), dtype)
    return call(
        kernel,
        (shape, shape),
        [SMEM, SMEM, SMEM] + [VMEM] * (2 + chips),
        (VMEM, VMEM),
        name="attend",
    )(place, tile_mask, tile_counts, queries_own, queries_other, *key_values)


def stack_rows(positions, blocks):
    count = len(blocks)
    rows, columns = blocks[0].shape

    def kernel(position_ref, *refs):
        stacked_ref = refs[count]
        for block in range(count):
            start = pl.multiple_of(position_ref[block] * rows, 16)
            stacked_ref[pl.ds(start, rows), :] = refs[block][...]

    return call(
        kernel,
        jax.ShapeDtypeStruct((count * rows, columns), blocks[0].dtype),
        [SMEM] + [VMEM] * count,
        VMEM,
        name="stack_rows",
    )(positions, *blocks)


def project_out(core, attended_own, attended_partner, out_own, out_partner):
    row_count, own_columns = attended_own.shape
    width = out_own.shape[1]
    dtype = attended_own.dtype

    def kernel(core_ref, own_ref, partner_ref, out_own_ref, out_partner_ref, result_ref):
        which = core_ref[0]
        own_rows = pl.ds(pl.multiple_of(which * own_columns, 16), own_columns)
        partner_rows = pl.ds(pl.multiple_of((1 - which) * own_columns, 16), own_columns)
        for weight_ref, side in ((out_own_ref, which), (out_partner_ref, 1 - which)):
            total = jnp.dot(own_ref[...], weight_ref[own_rows, :], preferred_element_type=jnp.float32)
            total += jnp.dot(partner_ref[...], weight_ref[partner_rows, :], preferred_element_type=jnp.float32)
            result_ref[:, pl.ds(pl.multiple_of(side * width, LANES), width)] = total.astype(dtype)

    return call(
        kernel,
        jax.ShapeDtypeStruct((row_count, CORES * width), dtype),
        [SMEM] + [VMEM] * 4,
        VMEM,
        name="project_out",
    )(core, attended_own, attended_partner, out_own, out_partner)


def local(latents, qkv_weight, out_weight, tile_mask, tile_counts):
    seq_count = lax.axis_size("seq")
    fsdp_count = lax.axis_size("fsdp")
    z_count, x_count = grid_of(fsdp_count)
    chips = seq_count // CORES
    seq_index = lax.axis_index("seq")
    fsdp_index = lax.axis_index("fsdp")
    chip = seq_index // CORES
    core = (seq_index % CORES)[None]
    z_index = fsdp_index // x_count
    x_index = fsdp_index % x_count
    latents_own = latents[0]

    qkv_half, out_half = halves(qkv_weight, out_weight, core)
    latents_other = lax.ppermute(latents_own, "seq", core_swap(seq_count))

    shifts = [(0, 0)]
    blocks = [qkv_half]
    for x_step in range(1, x_count):
        shifts.append((0, x_step))
        blocks.append(lax.ppermute(qkv_half, "fsdp", x_rotation(z_count, x_count, x_step)))
    for z_step in range(1, z_count):
        came = lax.ppermute(qkv_half, "fsdp", z_rotation(z_count, x_count, z_step))
        shifts.append((z_step, 0))
        blocks.append(came)
        for x_step in range(1, x_count):
            shifts.append((z_step, x_step))
            blocks.append(lax.ppermute(came, "fsdp", x_rotation(z_count, x_count, x_step)))
    positions = jnp.stack(
        [(z_index + z_count - dz) % z_count * x_count + (x_index + x_count - dx) % x_count for dz, dx in shifts]
    )
    queries_own, queries_other, key_value = project(positions, core, blocks, latents_own, latents_other)

    key_values = [key_value] + [
        lax.ppermute(key_value, "seq", y_rotation(seq_count, step)) for step in range(1, chips)
    ]
    out_half, _ = lax.optimization_barrier((out_half, key_value))
    layer = [out_half] + [
        lax.ppermute(out_half, "fsdp", x_rotation(z_count, x_count, step)) for step in range(1, x_count)
    ]
    out_positions = jnp.stack([(x_index + x_count - step) % x_count for step in range(x_count)])
    layer = stack_rows(out_positions, layer)
    layers = [layer] + [
        lax.ppermute(layer, "fsdp", z_rotation(z_count, x_count, step)) for step in range(1, z_count)
    ]
    layer_positions = jnp.stack([(z_index + z_count - step) % z_count for step in range(z_count)])
    out_own = stack_rows(layer_positions, layers)
    out_partner = lax.ppermute(out_own, "seq", core_swap(seq_count))

    place = jnp.stack([chip, seq_index % CORES])
    attended_own, attended_other = attend(place, tile_mask, tile_counts, queries_own, queries_other, key_values)
    attended_partner = lax.ppermute(attended_other, "seq", core_swap(seq_count))
    return project_out(core, attended_own, attended_partner, out_own, out_partner)[None]


def solution(mesh):
    return jax.shard_map(
        local,
        mesh=mesh,
        in_specs=(P("fsdp", "seq", None), P("fsdp", None), P("fsdp", None), P(), P()),
        out_specs=P("fsdp", "seq", None),
        check_vma=False,
    )
```

```python
import jax
import jax.numpy as jnp
from jax import lax
from jax.experimental import pallas as pl
from jax.experimental.pallas import tpu as pltpu
from jax.sharding import PartitionSpec as P

E = 64
LANES = 128
CORES = 2
NEG = -1e30
COST1 = 4_000_000_000
COST = 1_000_000_000

VMEM = pl.BlockSpec(memory_space=pltpu.VMEM)
SMEM = pl.BlockSpec(memory_space=pltpu.SMEM)
HBM = pl.BlockSpec(memory_space=pltpu.HBM)


def grid_of(fsdp_count):
    x_count = 1
    while (2 * x_count) ** 2 <= fsdp_count and fsdp_count % (2 * x_count) == 0:
        x_count *= 2
    return fsdp_count // x_count, x_count


def rotation(z_count, x_count, z_step, x_step):
    return [
        (z * x_count + x, (z + z_step) % z_count * x_count + (x + x_step) % x_count)
        for z in range(z_count)
        for x in range(x_count)
    ]


def core_swap(array, seq_count):
    return lax.ppermute(array, "seq", [(s, s ^ 1) for s in range(seq_count)])


def y_rotation(array, seq_count, step):
    return lax.ppermute(array, "seq", [(s, (s + CORES * step) % seq_count) for s in range(seq_count)])


def call(kernel, name, in_specs, out_shapes, out_specs=None, scratch_shapes=(), cost=0):
    out_specs = [VMEM] * len(out_shapes) if out_specs is None else out_specs
    shapes = [
        pltpu.VMEM(shape.shape, shape.dtype) if spec is VMEM else shape for shape, spec in zip(out_shapes, out_specs)
    ]
    inner = pl.pallas_call(
        kernel,
        out_shape=shapes,
        in_specs=in_specs,
        out_specs=out_specs,
        scratch_shapes=scratch_shapes,
        cost_estimate=pl.CostEstimate(flops=cost, bytes_accessed=0, transcendentals=0) if cost else None,
        compiler_params=pltpu.CompilerParams(vmem_limit_bytes=24 << 20),
        name=name,
    )

    def run(*args):
        return inner(
            *[
                arg if spec is SMEM else pltpu.with_memory_space_constraint(arg, spec.memory_space)
                for arg, spec in zip(args, in_specs)
            ]
        )

    return run


def shaped(shape, dtype):
    return jax.ShapeDtypeStruct(shape, dtype)


def halves(qkv_weight, out_weight):
    rows, columns = qkv_weight.shape
    head_columns = columns // 3
    own = head_columns // CORES
    out_rows, width = out_weight.shape
    side = width // CORES

    def kernel(qkv_ref, out_ref, qkv_half_ref, out_half_ref, sems):
        core = lax.rem(lax.axis_index("seq"), CORES)
        copies = []
        for part in range(3):
            start = pl.multiple_of(part * head_columns + core * own, LANES)
            copies.append(
                pltpu.make_async_copy(
                    qkv_ref.at[:, pl.ds(start, own)], qkv_half_ref.at[:, part * own : (part + 1) * own], sems.at[part]
                )
            )
        start = pl.multiple_of(core * side, LANES)
        copies.append(pltpu.make_async_copy(out_ref.at[:, pl.ds(start, side)], out_half_ref, sems.at[3]))
        for copy in copies:
            copy.start()
        for copy in copies:
            copy.wait()

    return call(
        kernel,
        "halves",
        [HBM, HBM],
        [shaped((rows, 3 * own), qkv_weight.dtype), shaped((out_rows, side), out_weight.dtype)],
        scratch_shapes=[pltpu.SemaphoreType.DMA((4,))],
    )(qkv_weight, out_weight)


def side_by_side(blocks, x_count):
    rows, columns = blocks[0].shape

    def kernel(*refs):
        x_index = lax.rem(lax.axis_index("fsdp"), x_count)
        for step in range(x_count):
            place = lax.rem(x_index + x_count - step, x_count)
            refs[x_count][pl.ds(pl.multiple_of(place * rows, 16), rows), :] = refs[step][...]

    return call(kernel, "side_by_side", [VMEM] * x_count, [shaped((x_count * rows, columns), blocks[0].dtype)])(
        *blocks
    )[0]


def lane_pick(per_head):
    lane = lax.broadcasted_iota(jnp.int32, (1, LANES), 1)
    picked = per_head[0]
    for head in range(1, len(per_head)):
        picked = jnp.where(lane >= head * E, per_head[head], picked)
    return jnp.broadcast_to(picked, (picked.shape[0], LANES))


def attend_part(queries, keys, values, bias):
    lane = lax.broadcasted_iota(jnp.int32, (1, LANES), 1)
    maxima, sums, outs = [], [], []
    for head in range(LANES // E):
        inside = (lane >= head * E) & (lane < (head + 1) * E)
        head_queries = jnp.where(inside, queries, jnp.zeros_like(queries))
        scores = lax.dot_general(head_queries, keys, (((1,), (1,)), ((), ())), preferred_element_type=jnp.float32)
        scores = scores + bias
        row_max = jnp.max(scores, axis=1, keepdims=True)
        numerators = jnp.exp(scores - row_max)
        maxima.append(row_max)
        sums.append(jnp.sum(numerators, axis=1, keepdims=True))
        outs.append(jnp.dot(numerators.astype(values.dtype), values, preferred_element_type=jnp.float32))
    return lane_pick(maxima), lane_pick(sums), lane_pick(outs)


def merge(old, new):
    top = jnp.maximum(old[0], new[0])
    keep = jnp.exp(old[0] - top)
    add = jnp.exp(new[0] - top)
    return top, old[1] * keep + new[1] * add, old[2] * keep + new[2] * add


def key_bias(mask_ref, count_ref, tile, key_tile, slots):
    slot = lax.broadcasted_iota(jnp.int32, (1, slots), 1)
    live = jnp.where(mask_ref[tile, key_tile] > 0, count_ref[key_tile], 0)
    return jnp.where(slot < live, 0.0, NEG)


def row_chunks(row_count):
    rows = row_count // 2 if row_count % 32 == 0 else row_count
    return [(start, rows) for start in range(0, row_count, rows)]


def first_part(z_count, x_count, shifts, blocks, latents_own, latents_other, tile_mask, tile_counts):
    count = len(blocks)
    rows, columns = blocks[0].shape
    depth = count * rows
    own = columns // 3
    row_count = latents_own.shape[0]
    dtype = latents_own.dtype
    scale = float(E) ** -0.5

    def kernel(mask_ref, count_ref, own_ref, other_ref, *refs):
        block_refs = refs[:count]
        queries_ref, weight_ref, state_ref, full_ref, latents_ref, key_value_ref, sem = refs[count:]
        fetch = pltpu.make_async_copy(own_ref, latents_ref, sem)
        fetch.start()
        seq_index = lax.axis_index("seq")
        fsdp_index = lax.axis_index("fsdp")
        z_index = fsdp_index // x_count
        x_index = lax.rem(fsdp_index, x_count)
        for (dz, dx), block_ref in zip(shifts, block_refs):
            place = lax.rem(z_index + z_count - dz, z_count) * x_count + lax.rem(x_index + x_count - dx, x_count)
            full_ref[pl.ds(pl.multiple_of(place * rows, 16), rows), :] = block_ref[...]
        weight_ref[...] = full_ref[:, own:]
        for member, from_ref in ((1, other_ref), (0, latents_ref)):
            if member == 0:
                fetch.wait()
            projected = jnp.dot(from_ref[...], full_ref[...], preferred_element_type=jnp.float32).astype(dtype)
            queries_ref[member] = projected[:, :own] * jnp.asarray(scale, dtype)
            key_value_ref[member * row_count : (member + 1) * row_count, :] = projected[:, own:]
        core = lax.rem(seq_index, CORES)
        chip_tile = seq_index - core
        tiles = [chip_tile + core, chip_tile + 1 - core]
        for member in range(CORES):
            bias = jnp.concatenate(
                [key_bias(mask_ref, count_ref, tiles[member], key_tile, row_count) for key_tile in tiles], axis=1
            )
            for group in range(own // LANES):
                lanes = slice(group * LANES, (group + 1) * LANES)
                value_lanes = slice(own + group * LANES, own + (group + 1) * LANES)
                for start, size in row_chunks(row_count):
                    parts = attend_part(
                        queries_ref[member, start : start + size, lanes],
                        key_value_ref[:, lanes],
                        key_value_ref[:, value_lanes],
                        bias,
                    )
                    for which, part in enumerate(parts):
                        state_ref[member, which, start : start + size, lanes] = part

    return call(
        kernel,
        "first_part",
        [SMEM, SMEM, HBM] + [VMEM] * (count + 1),
        [
            shaped((CORES, row_count, own), dtype),
            shaped((depth, 2 * own), dtype),
            shaped((CORES, 3, row_count, own), jnp.float32),
        ],
        scratch_shapes=[
            pltpu.VMEM((depth, columns), dtype),
            pltpu.VMEM((row_count, latents_own.shape[1]), dtype),
            pltpu.VMEM((CORES * row_count, 2 * own), dtype),
            pltpu.SemaphoreType.DMA(()),
        ],
        cost=COST1,
    )(tile_mask, tile_counts, latents_own, latents_other, *blocks)


def next_part(seq_count, y_step, swapped, last, weight, latents, queries, state, tile_mask, tile_counts, layers=()):
    columns = weight.shape[1]
    z_count = len(layers)
    own = columns // 2
    row_count = latents.shape[0]
    dtype = latents.dtype

    def kernel(mask_ref, count_ref, weight_ref, latents_ref, queries_ref, old_ref, *refs):
        layer_refs, refs = refs[:z_count], refs[z_count:]
        out_refs, key_value_ref = refs[:-1], refs[-1]
        if layers:
            rows = layers[0].shape[0]
            z_index = lax.axis_index("fsdp") // (lax.axis_size("fsdp") // z_count)
            for step in range(z_count):
                place = lax.rem(z_index + z_count - step, z_count)
                out_refs[-1][pl.ds(pl.multiple_of(place * rows, 16), rows), :] = layer_refs[step][...]
        seq_index = lax.axis_index("seq")
        core = lax.rem(seq_index, CORES)
        key_place = lax.rem(seq_index + seq_count - CORES * y_step, seq_count)
        key_tile = key_place + 1 - 2 * core if swapped else key_place
        chip_tile = seq_index - core
        tiles = [chip_tile + core, chip_tile + 1 - core]
        key_value_ref[...] = jnp.dot(
            latents_ref[...], weight_ref[...], preferred_element_type=jnp.float32
        ).astype(dtype)
        for member in range(CORES):
            bias = key_bias(mask_ref, count_ref, tiles[member], key_tile, row_count)
            for group in range(own // LANES):
                lanes = slice(group * LANES, (group + 1) * LANES)
                value_lanes = slice(own + group * LANES, own + (group + 1) * LANES)
                for start, size in row_chunks(row_count):
                    chunk = slice(start, start + size)
                    parts = attend_part(
                        queries_ref[member, chunk, lanes], key_value_ref[:, lanes], key_value_ref[:, value_lanes], bias
                    )
                    parts = merge([old_ref[member, which, chunk, lanes] for which in range(3)], parts)
                    if last:
                        position = start + lax.broadcasted_iota(jnp.int32, (size, 1), 0)
                        attended = jnp.where(position < count_ref[tiles[member]], parts[2] / parts[1], 0.0)
                        out_refs[member][chunk, lanes] = attended.astype(dtype)
                    else:
                        for which, part in enumerate(parts):
                            out_refs[0][member, which, chunk, lanes] = part

    if last:
        out_shapes = [shaped((row_count, own), dtype)] * 2
    else:
        out_shapes = [shaped(state.shape, state.dtype)]
    if layers:
        out_shapes.append(shaped((z_count * layers[0].shape[0], layers[0].shape[1]), layers[0].dtype))
    return call(
        kernel,
        "last_part" if last else "next_part",
        [SMEM, SMEM] + [VMEM] * (4 + z_count),
        out_shapes,
        scratch_shapes=[pltpu.VMEM((row_count, columns), dtype)],
        cost=COST,
    )(tile_mask, tile_counts, weight, latents, queries, state, *layers)


def project_out(attended_own, attended_partner, out_own, out_partner):
    row_count, own = attended_own.shape
    side = out_own.shape[1]
    dtype = attended_own.dtype

    def kernel(own_ref, partner_ref, out_own_ref, out_partner_ref, result_ref, staged_ref, sems):
        core = lax.rem(lax.axis_index("seq"), CORES)
        own_rows = pl.ds(pl.multiple_of(core * own, 16), own)
        partner_rows = pl.ds(pl.multiple_of((1 - core) * own, 16), own)
        copies = []
        for half, weight_ref in enumerate((out_own_ref, out_partner_ref)):
            total = jnp.dot(own_ref[...], weight_ref[own_rows, :], preferred_element_type=jnp.float32)
            total += jnp.dot(partner_ref[...], weight_ref[partner_rows, :], preferred_element_type=jnp.float32)
            staged_ref[half] = total.astype(dtype)
            start = pl.multiple_of((core if half == 0 else 1 - core) * side, LANES)
            copies.append(
                pltpu.make_async_copy(staged_ref.at[half], result_ref.at[:, pl.ds(start, side)], sems.at[half])
            )
            copies[-1].start()
        for copy in copies:
            copy.wait()

    return call(
        kernel,
        "project_out",
        [VMEM] * 4,
        [shaped((row_count, CORES * side), dtype)],
        [HBM],
        scratch_shapes=[pltpu.VMEM((CORES, row_count, side), dtype), pltpu.SemaphoreType.DMA((CORES,))],
    )(attended_own, attended_partner, out_own, out_partner)[0]


def local(latents, qkv_weight, out_weight, tile_mask, tile_counts):
    seq_count = lax.axis_size("seq")
    fsdp_count = lax.axis_size("fsdp")
    z_count, x_count = grid_of(fsdp_count)
    chips = seq_count // CORES
    latents_own = latents[0]

    along_y = [y_rotation(latents_own, seq_count, step) for step in range(1, chips)]
    latents_other = core_swap(latents_own, seq_count)
    qkv_half, out_half = halves(qkv_weight, out_weight)

    shifts, blocks = [(0, 0)], [qkv_half]
    for z_step in reversed(range(z_count)):
        came = qkv_half
        if z_step:
            came = lax.ppermute(qkv_half, "fsdp", rotation(z_count, x_count, z_step, 0))
            shifts.append((z_step, 0))
            blocks.append(came)
        for x_step in range(1, x_count):
            shifts.append((z_step, x_step))
            if z_step == 1:
                blocks.append(lax.ppermute(qkv_half, "fsdp", rotation(z_count, x_count, z_step, x_step)))
            else:
                blocks.append(lax.ppermute(came, "fsdp", rotation(z_count, x_count, 0, x_step)))

    layer = side_by_side(
        [out_half]
        + [lax.ppermute(out_half, "fsdp", rotation(z_count, x_count, 0, x_step)) for x_step in range(1, x_count)],
        x_count,
    )
    blocks[0], layer = lax.optimization_barrier((blocks[0], layer))
    layers = [layer] + [
        lax.ppermute(layer, "fsdp", rotation(z_count, x_count, z_step, 0)) for z_step in range(1, z_count)
    ]

    queries, weight, state = first_part(
        z_count, x_count, shifts, blocks, latents_own, latents_other, tile_mask, tile_counts
    )
    parts = [(step, swapped) for step in range(1, chips) for swapped in (False, True)]
    for step, swapped in parts:
        if not swapped:
            came, state = lax.optimization_barrier((along_y[step - 1], state))
        else:
            came = core_swap(came, seq_count)
        last = (step, swapped) == parts[-1]
        result = next_part(
            seq_count,
            step,
            swapped,
            last,
            weight,
            came,
            queries,
            state,
            tile_mask,
            tile_counts,
            layers if (step, swapped) == parts[0] else (),
        )
        if (step, swapped) == parts[0]:
            *result, out_own = result
        if last:
            attended_own, attended_other = result
        else:
            state = result[0]
    out_partner = core_swap(out_own, seq_count)
    attended_partner = core_swap(attended_other, seq_count)
    return project_out(attended_own, attended_partner, out_own, out_partner)[None]


def solution(mesh):
    return jax.shard_map(
        local,
        mesh=mesh,
        in_specs=(P("fsdp", "seq", None), P("fsdp", None), P("fsdp", None), P(), P()),
        out_specs=P("fsdp", "seq", None),
        check_vma=False,
    )
```

```python
import jax
import jax.numpy as jnp
from jax import lax
from jax.experimental import pallas as pl
from jax.experimental.pallas import tpu as pltpu
from jax.sharding import PartitionSpec as P

E = 64
LANES = 128
CORES = 2
NEG = -1e30
COST1 = 1_000_000_000
COST = 1_000_000_000

VMEM = pl.BlockSpec(memory_space=pltpu.VMEM)
SMEM = pl.BlockSpec(memory_space=pltpu.SMEM)
HBM = pl.BlockSpec(memory_space=pltpu.HBM)


def grid_of(fsdp_count):
    x_count = 1
    while (2 * x_count) ** 2 <= fsdp_count and fsdp_count % (2 * x_count) == 0:
        x_count *= 2
    return fsdp_count // x_count, x_count


def rotation(z_count, x_count, z_step, x_step):
    return [
        (z * x_count + x, (z + z_step) % z_count * x_count + (x + x_step) % x_count)
        for z in range(z_count)
        for x in range(x_count)
    ]


def core_swap(array, seq_count):
    return lax.ppermute(array, "seq", [(s, s ^ 1) for s in range(seq_count)])


def y_rotation(array, seq_count, step):
    return lax.ppermute(array, "seq", [(s, (s + CORES * step) % seq_count) for s in range(seq_count)])


def call(kernel, name, in_specs, out_shapes, out_specs=None, scratch_shapes=(), cost=0):
    out_specs = [VMEM] * len(out_shapes) if out_specs is None else out_specs
    shapes = [
        pltpu.VMEM(shape.shape, shape.dtype) if spec is VMEM else shape for shape, spec in zip(out_shapes, out_specs)
    ]
    inner = pl.pallas_call(
        kernel,
        out_shape=shapes,
        in_specs=in_specs,
        out_specs=out_specs,
        scratch_shapes=scratch_shapes,
        cost_estimate=pl.CostEstimate(flops=cost, bytes_accessed=0, transcendentals=0) if cost else None,
        compiler_params=pltpu.CompilerParams(vmem_limit_bytes=24 << 20),
        name=name,
    )

    def run(*args):
        return inner(
            *[
                pltpu.with_memory_space_constraint(arg, pltpu.HBM if spec is SMEM else spec.memory_space)
                for arg, spec in zip(args, in_specs)
            ]
        )

    return run


def shaped(shape, dtype):
    return jax.ShapeDtypeStruct(shape, dtype)


def strips(width, columns):
    strip = min(width, columns)
    return [(start, strip) for start in range(0, width, strip)]


def halves(qkv_weight, out_weight):
    rows, columns = qkv_weight.shape
    head_columns = columns // 3
    own = head_columns // CORES
    out_rows, width = out_weight.shape
    side = width // CORES
    pieces = strips(side, 3 * own)

    def kernel(qkv_ref, out_ref, half_ref, packed_ref, sems):
        core = lax.rem(lax.axis_index("seq"), CORES)
        copies = []

        def copy(source, target):
            copies.append(pltpu.make_async_copy(source, target, sems.at[len(copies)]))
            copies[-1].start()

        for part in range(3):
            source = qkv_ref.at[:, pl.ds(pl.multiple_of(part * head_columns + core * own, LANES), own)]
            lanes = slice(part * own, (part + 1) * own)
            copy(source, half_ref.at[:, lanes])
            copy(source, packed_ref.at[:rows, lanes])
        for piece, (start, strip) in enumerate(pieces):
            first = rows + piece * out_rows
            copy(
                out_ref.at[:, pl.ds(pl.multiple_of(core * side + start, LANES), strip)],
                packed_ref.at[first : first + out_rows, :strip],
            )
        for each in copies:
            each.wait()

    return call(
        kernel,
        "halves",
        [HBM, HBM],
        [
            shaped((rows, 3 * own), qkv_weight.dtype),
            shaped((rows + len(pieces) * out_rows, 3 * own), qkv_weight.dtype),
        ],
        scratch_shapes=[pltpu.SemaphoreType.DMA((6 + len(pieces),))],
    )(qkv_weight, out_weight)


def side_by_side(blocks, x_count, rows, out_rows, side):
    pieces = strips(side, blocks[0].shape[1])

    def kernel(*refs):
        x_index = lax.rem(lax.axis_index("fsdp"), x_count)
        for step in range(x_count):
            place = lax.rem(x_index + x_count - step, x_count)
            for piece, (start, strip) in enumerate(pieces):
                first = rows + piece * out_rows
                refs[x_count][pl.ds(pl.multiple_of(place * out_rows, 16), out_rows), start : start + strip] = refs[step][
                    first : first + out_rows, :strip
                ]

    return call(kernel, "side_by_side", [VMEM] * x_count, [shaped((x_count * out_rows, side), blocks[0].dtype)])(
        *blocks
    )[0]


def lane_pick(per_head):
    lane = lax.broadcasted_iota(jnp.int32, (1, LANES), 1)
    picked = per_head[0]
    for head in range(1, len(per_head)):
        picked = jnp.where(lane >= head * E, per_head[head], picked)
    return jnp.broadcast_to(picked, (picked.shape[0], LANES))


def attend_part(queries, keys, values, bias):
    lane = lax.broadcasted_iota(jnp.int32, (1, LANES), 1)
    maxima, sums, outs = [], [], []
    for head in range(LANES // E):
        inside = (lane >= head * E) & (lane < (head + 1) * E)
        head_queries = jnp.where(inside, queries, jnp.zeros_like(queries))
        scores = lax.dot_general(head_queries, keys, (((1,), (1,)), ((), ())), preferred_element_type=jnp.float32)
        scores = scores + bias
        row_max = jnp.max(scores, axis=1, keepdims=True)
        numerators = jnp.exp(scores - row_max)
        maxima.append(row_max)
        sums.append(jnp.sum(numerators, axis=1, keepdims=True))
        outs.append(jnp.dot(numerators.astype(values.dtype), values, preferred_element_type=jnp.float32))
    return lane_pick(maxima), lane_pick(sums), lane_pick(outs)


def merge(old, new):
    top = jnp.maximum(old[0], new[0])
    keep = jnp.exp(old[0] - top)
    add = jnp.exp(new[0] - top)
    return top, old[1] * keep + new[1] * add, old[2] * keep + new[2] * add


def key_bias(mask_ref, count_ref, tile, key_tile, slots):
    slot = lax.broadcasted_iota(jnp.int32, (1, slots), 1)
    live = jnp.where(mask_ref[tile, key_tile] > 0, count_ref[key_tile], 0)
    return jnp.where(slot < live, 0.0, NEG)


def row_chunks(row_count):
    rows = row_count // 2 if row_count % 32 == 0 else row_count
    return [(start, rows) for start in range(0, row_count, rows)]


def first_part(z_count, x_count, shifts, blocks, latents_own, latents_other, tile_mask, tile_counts):
    count = len(blocks)
    rows = latents_own.shape[1] // count
    columns = blocks[0].shape[1]
    depth = count * rows
    own = columns // 3
    row_count = latents_own.shape[0]
    dtype = latents_own.dtype
    scale = float(E) ** -0.5

    def kernel(mask_ref, count_ref, own_ref, other_ref, *refs):
        block_refs = refs[:count]
        queries_ref, weight_ref, state_ref, full_ref, latents_ref, key_value_ref, sem = refs[count:]
        fetch = pltpu.make_async_copy(own_ref, latents_ref, sem)
        fetch.start()
        seq_index = lax.axis_index("seq")
        fsdp_index = lax.axis_index("fsdp")
        z_index = fsdp_index // x_count
        x_index = lax.rem(fsdp_index, x_count)
        for (dz, dx), block_ref in zip(shifts, block_refs):
            place = lax.rem(z_index + z_count - dz, z_count) * x_count + lax.rem(x_index + x_count - dx, x_count)
            full_ref[pl.ds(pl.multiple_of(place * rows, 16), rows), :] = block_ref[:rows, :]
        weight_ref[...] = full_ref[:, own:]
        for member, from_ref in ((1, other_ref), (0, latents_ref)):
            if member == 0:
                fetch.wait()
            projected = jnp.dot(from_ref[...], full_ref[...], preferred_element_type=jnp.float32).astype(dtype)
            queries_ref[member] = projected[:, :own] * jnp.asarray(scale, dtype)
            key_value_ref[member * row_count : (member + 1) * row_count, :] = projected[:, own:]
        core = lax.rem(seq_index, CORES)
        chip_tile = seq_index - core
        tiles = [chip_tile + core, chip_tile + 1 - core]
        for member in range(CORES):
            bias = jnp.concatenate(
                [key_bias(mask_ref, count_ref, tiles[member], key_tile, row_count) for key_tile in tiles], axis=1
            )
            for group in range(own // LANES):
                lanes = slice(group * LANES, (group + 1) * LANES)
                value_lanes = slice(own + group * LANES, own + (group + 1) * LANES)
                for start, size in row_chunks(row_count):
                    parts = attend_part(
                        queries_ref[member, start : start + size, lanes],
                        key_value_ref[:, lanes],
                        key_value_ref[:, value_lanes],
                        bias,
                    )
                    for which, part in enumerate(parts):
                        state_ref[member, which, start : start + size, lanes] = part

    return call(
        kernel,
        "first_part",
        [SMEM, SMEM, HBM] + [VMEM] * (count + 1),
        [
            shaped((CORES, row_count, own), dtype),
            shaped((depth, 2 * own), dtype),
            shaped((CORES, 3, row_count, own), jnp.float32),
        ],
        scratch_shapes=[
            pltpu.VMEM((depth, columns), dtype),
            pltpu.VMEM((row_count, latents_own.shape[1]), dtype),
            pltpu.VMEM((CORES * row_count, 2 * own), dtype),
            pltpu.SemaphoreType.DMA(()),
        ],
        cost=COST1,
    )(tile_mask, tile_counts, latents_own, latents_other, *blocks)


def next_part(seq_count, y_step, last, weight, latents, queries, state, tile_mask, tile_counts, layers=()):
    columns = weight.shape[1]
    z_count = len(layers)
    own = columns // 2
    row_count = latents[0].shape[0]
    dtype = latents[0].dtype

    def kernel(mask_ref, count_ref, weight_ref, near_ref, far_ref, queries_ref, old_ref, *refs):
        layer_refs, refs = refs[:z_count], refs[z_count:]
        out_refs, key_value_ref = refs[:-1], refs[-1]
        if layers:
            rows = layers[0].shape[0]
            z_index = lax.axis_index("fsdp") // (lax.axis_size("fsdp") // z_count)
            for step in range(z_count):
                place = lax.rem(z_index + z_count - step, z_count)
                out_refs[-1][pl.ds(pl.multiple_of(place * rows, 16), rows), :] = layer_refs[step][...]
        seq_index = lax.axis_index("seq")
        core = lax.rem(seq_index, CORES)
        key_place = lax.rem(seq_index + seq_count - CORES * y_step, seq_count)
        chip_tile = seq_index - core
        tiles = [chip_tile + core, chip_tile + 1 - core]
        for part, latents_ref in enumerate((near_ref, far_ref)):
            key_value_ref[part * row_count : (part + 1) * row_count, :] = jnp.dot(
                latents_ref[...], weight_ref[...], preferred_element_type=jnp.float32
            ).astype(dtype)
        for member in range(CORES):
            bias = jnp.concatenate(
                [
                    key_bias(mask_ref, count_ref, tiles[member], key_tile, row_count)
                    for key_tile in (key_place, key_place + 1 - 2 * core)
                ],
                axis=1,
            )
            for group in range(own // LANES):
                lanes = slice(group * LANES, (group + 1) * LANES)
                value_lanes = slice(own + group * LANES, own + (group + 1) * LANES)
                for start, size in row_chunks(row_count):
                    chunk = slice(start, start + size)
                    parts = attend_part(
                        queries_ref[member, chunk, lanes], key_value_ref[:, lanes], key_value_ref[:, value_lanes], bias
                    )
                    parts = merge([old_ref[member, which, chunk, lanes] for which in range(3)], parts)
                    if last:
                        position = start + lax.broadcasted_iota(jnp.int32, (size, 1), 0)
                        attended = jnp.where(position < count_ref[tiles[member]], parts[2] / parts[1], 0.0)
                        out_refs[member][chunk, lanes] = attended.astype(dtype)
                    else:
                        for which, part in enumerate(parts):
                            out_refs[0][member, which, chunk, lanes] = part

    if last:
        out_shapes = [shaped((row_count, own), dtype)] * 2
    else:
        out_shapes = [shaped(state.shape, state.dtype)]
    if layers:
        out_shapes.append(shaped((z_count * layers[0].shape[0], layers[0].shape[1]), layers[0].dtype))
    return call(
        kernel,
        "last_part" if last else "next_part",
        [SMEM, SMEM] + [VMEM] * (5 + z_count),
        out_shapes,
        scratch_shapes=[pltpu.VMEM((CORES * row_count, columns), dtype)],
        cost=COST,
    )(tile_mask, tile_counts, weight, *latents, queries, state, *layers)


def project_out(attended_own, attended_partner, out_own, out_partner):
    row_count, own = attended_own.shape
    side = out_own.shape[1]
    dtype = attended_own.dtype

    def kernel(own_ref, partner_ref, out_own_ref, out_partner_ref, result_ref, staged_ref, sems):
        core = lax.rem(lax.axis_index("seq"), CORES)
        own_rows = pl.ds(pl.multiple_of(core * own, 16), own)
        partner_rows = pl.ds(pl.multiple_of((1 - core) * own, 16), own)
        copies = []
        for half, weight_ref in enumerate((out_own_ref, out_partner_ref)):
            total = jnp.dot(own_ref[...], weight_ref[own_rows, :], preferred_element_type=jnp.float32)
            total += jnp.dot(partner_ref[...], weight_ref[partner_rows, :], preferred_element_type=jnp.float32)
            staged_ref[half] = total.astype(dtype)
            start = pl.multiple_of((core if half == 0 else 1 - core) * side, LANES)
            copies.append(
                pltpu.make_async_copy(staged_ref.at[half], result_ref.at[:, pl.ds(start, side)], sems.at[half])
            )
            copies[-1].start()
        for copy in copies:
            copy.wait()

    return call(
        kernel,
        "project_out",
        [VMEM] * 4,
        [shaped((row_count, CORES * side), dtype)],
        [HBM],
        scratch_shapes=[pltpu.VMEM((CORES, row_count, side), dtype), pltpu.SemaphoreType.DMA((CORES,))],
    )(attended_own, attended_partner, out_own, out_partner)[0]


def after(array, *others):
    return lax.optimization_barrier((array, *others))[0]


def local(latents, qkv_weight, out_weight, tile_mask, tile_counts):
    seq_count = lax.axis_size("seq")
    fsdp_count = lax.axis_size("fsdp")
    z_count, x_count = grid_of(fsdp_count)
    chips = seq_count // CORES
    latents_own = latents[0]

    def hop(array, z_step, x_step):
        return lax.ppermute(array, "fsdp", rotation(z_count, x_count, z_step, x_step))

    along_y = [y_rotation(latents_own, seq_count, step) for step in range(1, chips)]
    half, packed = halves(qkv_weight, out_weight)

    came = {(0, 0): half}
    for x_step in range(1, x_count):
        came[0, x_step] = hop(packed, 0, x_step)
    order = [step for step in range(2, z_count)] + [1]
    for z_step in order:
        came[z_step, 0] = hop(half, z_step, 0)
    beside = [came[0, x_step] for x_step in range(1, x_count)]
    for x_step in range(1, x_count):
        came[1, x_step] = hop(after(half, *beside), 1, x_step)
        for z_step in order[:-1]:
            came[z_step, x_step] = hop(came[z_step, 0], 0, x_step)
    latents_other = core_swap(after(latents_own, came[order[0], x_count - 1]), seq_count)

    layer = side_by_side([packed] + beside, x_count, half.shape[0], out_weight.shape[0], out_weight.shape[1] // CORES)
    layer = after(layer, *[came[z_step, 0] for z_step in order])
    layers = [layer] + [hop(layer, z_step, 0) for z_step in range(1, z_count)]

    arrived = list(came.values())[1:]
    came[0, 0] = after(half, *along_y)
    queries, weight, state = first_part(
        z_count, x_count, list(came), list(came.values()), latents_own, latents_other, tile_mask, tile_counts
    )
    for step in range(1, chips):
        near = along_y[step - 1]
        far = core_swap(after(near, *arrived), seq_count)
        last = step == chips - 1
        result = next_part(
            seq_count,
            step,
            last,
            weight,
            (near, far),
            queries,
            state,
            tile_mask,
            tile_counts,
            layers if step == 1 else (),
        )
        if step == 1:
            *result, out_own = result
        if last:
            attended_own, attended_other = result
        else:
            state = result[0]
    out_partner = core_swap(out_own, seq_count)
    attended_partner = core_swap(attended_other, seq_count)
    return project_out(attended_own, attended_partner, out_own, out_partner)[None]


def solution(mesh):
    return jax.shard_map(
        local,
        mesh=mesh,
        in_specs=(P("fsdp", "seq", None), P("fsdp", None), P("fsdp", None), P(), P()),
        out_specs=P("fsdp", "seq", None),
        check_vma=False,
    )
```

```python
import jax
import jax.numpy as jnp
from jax import lax
from jax.experimental import pallas as pl
from jax.experimental.pallas import tpu as pltpu
from jax.sharding import PartitionSpec as P

E = 64
LANES = 128
CORES = 2
NEG = -1e30
ROWS = 192
COST1 = 1_000_000_000
COST = 1_000_000_000

VMEM = pl.BlockSpec(memory_space=pltpu.VMEM)
SMEM = pl.BlockSpec(memory_space=pltpu.SMEM)
HBM = pl.BlockSpec(memory_space=pltpu.HBM)


def grid_of(fsdp_count):
    x_count = 1
    while (2 * x_count) ** 2 <= fsdp_count and fsdp_count % (2 * x_count) == 0:
        x_count *= 2
    return fsdp_count // x_count, x_count


def rotation(z_count, x_count, z_step, x_step):
    return [
        (z * x_count + x, (z + z_step) % z_count * x_count + (x + x_step) % x_count)
        for z in range(z_count)
        for x in range(x_count)
    ]


def core_swap(array, seq_count):
    return lax.ppermute(array, "seq", [(s, s ^ 1) for s in range(seq_count)])


def y_rotation(array, seq_count, step):
    return lax.ppermute(array, "seq", [(s, (s + CORES * step) % seq_count) for s in range(seq_count)])


def call(kernel, name, in_specs, out_shapes, out_specs=None, scratch_shapes=(), cost=0):
    out_specs = [VMEM] * len(out_shapes) if out_specs is None else out_specs
    shapes = [
        pltpu.VMEM(shape.shape, shape.dtype) if spec is VMEM else shape for shape, spec in zip(out_shapes, out_specs)
    ]
    inner = pl.pallas_call(
        kernel,
        out_shape=shapes,
        in_specs=in_specs,
        out_specs=out_specs,
        scratch_shapes=scratch_shapes,
        cost_estimate=pl.CostEstimate(flops=cost, bytes_accessed=0, transcendentals=0) if cost else None,
        compiler_params=pltpu.CompilerParams(vmem_limit_bytes=24 << 20),
        name=name,
    )

    def run(*args):
        return inner(
            *[
                pltpu.with_memory_space_constraint(arg, pltpu.HBM if spec is SMEM else spec.memory_space)
                for arg, spec in zip(args, in_specs)
            ]
        )

    return run


def shaped(shape, dtype):
    return jax.ShapeDtypeStruct(shape, dtype)


def strips(width, columns):
    strip = min(width, columns)
    return [(start, strip) for start in range(0, width, strip)]


def halves(qkv_weight, out_weight):
    rows, columns = qkv_weight.shape
    head_columns = columns // 3
    own = head_columns // CORES
    out_rows, width = out_weight.shape
    side = width // CORES
    pieces = strips(side, 3 * own)

    def kernel(qkv_ref, out_ref, half_ref, packed_ref, sems):
        core = lax.rem(lax.axis_index("seq"), CORES)
        copies = []

        def copy(source, target):
            copies.append(pltpu.make_async_copy(source, target, sems.at[len(copies)]))
            copies[-1].start()

        for part in range(3):
            source = qkv_ref.at[:, pl.ds(pl.multiple_of(part * head_columns + core * own, LANES), own)]
            lanes = slice(part * own, (part + 1) * own)
            copy(source, half_ref.at[:, lanes])
            copy(source, packed_ref.at[:rows, lanes])
        for piece, (start, strip) in enumerate(pieces):
            first = rows + piece * out_rows
            copy(
                out_ref.at[:, pl.ds(pl.multiple_of(core * side + start, LANES), strip)],
                packed_ref.at[first : first + out_rows, :strip],
            )
        for each in copies:
            each.wait()

    return call(
        kernel,
        "halves",
        [HBM, HBM],
        [
            shaped((rows, 3 * own), qkv_weight.dtype),
            shaped((rows + len(pieces) * out_rows, 3 * own), qkv_weight.dtype),
        ],
        scratch_shapes=[pltpu.SemaphoreType.DMA((6 + len(pieces),))],
    )(qkv_weight, out_weight)


def side_by_side(blocks, x_count, rows, out_rows, side):
    pieces = strips(side, blocks[0].shape[1])

    def kernel(*refs):
        x_index = lax.rem(lax.axis_index("fsdp"), x_count)
        for step in range(x_count):
            place = lax.rem(x_index + x_count - step, x_count)
            for piece, (start, strip) in enumerate(pieces):
                first = rows + piece * out_rows
                refs[x_count][pl.ds(pl.multiple_of(place * out_rows, 16), out_rows), start : start + strip] = refs[step][
                    first : first + out_rows, :strip
                ]

    return call(kernel, "side_by_side", [VMEM] * x_count, [shaped((x_count * out_rows, side), blocks[0].dtype)])(
        *blocks
    )[0]


def pair_up(own, got, units, shift, x_count):
    rows, columns = own.shape
    each = rows // units

    def kernel(own_ref, got_ref, pair_ref):
        bit = lax.rem(lax.axis_index("fsdp") // (x_count * shift), 2)
        for unit in range(units):
            piece = slice(unit * each, (unit + 1) * each)
            pair_ref[pl.ds(pl.multiple_of((2 * unit + bit) * each, 16), each), :] = own_ref[piece, :]
            pair_ref[pl.ds(pl.multiple_of((2 * unit + 1 - bit) * each, 16), each), :] = got_ref[piece, :]

    return call(kernel, "pair_up", [VMEM, VMEM], [shaped((2 * rows, columns), own.dtype)])(own, got)[0]


def lane_pick(per_head):
    lane = lax.broadcasted_iota(jnp.int32, (1, LANES), 1)
    picked = per_head[0]
    for head in range(1, len(per_head)):
        picked = jnp.where(lane >= head * E, per_head[head], picked)
    return jnp.broadcast_to(picked, (picked.shape[0], LANES))


def attend_part(queries, keys, values, bias):
    lane = lax.broadcasted_iota(jnp.int32, (1, LANES), 1)
    maxima, sums, outs = [], [], []
    for head in range(LANES // E):
        inside = (lane >= head * E) & (lane < (head + 1) * E)
        head_queries = jnp.where(inside, queries, jnp.zeros_like(queries))
        scores = lax.dot_general(head_queries, keys, (((1,), (1,)), ((), ())), preferred_element_type=jnp.float32)
        scores = scores + bias
        row_max = jnp.max(scores, axis=1, keepdims=True)
        numerators = jnp.exp(scores - row_max).astype(values.dtype)
        summed = jnp.dot(numerators, values, preferred_element_type=jnp.float32)
        maxima.append(row_max)
        sums.append(summed[:, LANES:])
        outs.append(summed[:, :LANES])
    return lane_pick(maxima), lane_pick(sums), lane_pick(outs)


def merge(old, new):
    top = jnp.maximum(old[0], new[0])
    keep = jnp.exp(old[0] - top)
    add = jnp.exp(new[0] - top)
    return top, old[1] * keep + new[1] * add, old[2] * keep + new[2] * add


def key_bias(mask_ref, count_ref, tile, key_tile, slots):
    slot = lax.broadcasted_iota(jnp.int32, (1, slots), 1)
    live = jnp.where(mask_ref[tile, key_tile] > 0, count_ref[key_tile], 0)
    return jnp.where(slot < live, 0.0, NEG)


def project(z_count, x_count, shifts, blocks, latents_own, latents_other):
    count = len(blocks)
    columns = blocks[0].shape[1]
    own = columns // 3
    row_count, depth = latents_own.shape
    rows = depth // count
    dtype = latents_own.dtype
    scale = float(E) ** -0.5

    def kernel(own_ref, other_ref, *refs):
        block_refs = refs[:count]
        queries_ref, weight_ref, key_value_ref, latents_ref, sem = refs[count:]
        fetch = pltpu.make_async_copy(own_ref, latents_ref, sem)
        fetch.start()
        fsdp_index = lax.axis_index("fsdp")
        z_index = fsdp_index // x_count
        x_index = lax.rem(fsdp_index, x_count)
        for (dz, dx), block_ref in zip(shifts, block_refs):
            place = lax.rem(z_index + z_count - dz, z_count) * x_count + lax.rem(x_index + x_count - dx, x_count)
            weight_ref[pl.ds(pl.multiple_of(place * rows, 16), rows), :] = block_ref[:rows, :]
        for member, from_ref in ((1, other_ref), (0, latents_ref)):
            if member == 0:
                fetch.wait()
            projected = jnp.dot(from_ref[...], weight_ref[...], preferred_element_type=jnp.float32).astype(dtype)
            queries_ref[member] = projected[:, :own] * jnp.asarray(scale, dtype)
            key_value_ref[member * row_count : (member + 1) * row_count, :] = projected[:, own:]

    return call(
        kernel,
        "project",
        [HBM] + [VMEM] * (count + 1),
        [
            shaped((CORES, row_count, own), dtype),
            shaped((depth, columns), dtype),
            shaped((CORES * row_count, 2 * own), dtype),
        ],
        scratch_shapes=[pltpu.VMEM((row_count, depth), dtype), pltpu.SemaphoreType.DMA(())],
        cost=COST1,
    )(latents_own, latents_other, *blocks)


def attend(seq_count, sources, key_value, state, last, weight, queries, tile_mask, tile_counts):
    columns = weight.shape[1]
    own = columns // 3
    row_count = queries.shape[1]
    dtype = queries.dtype
    groups = own // LANES
    local_rows = 0 if key_value is None else CORES * row_count
    slots = local_rows + len(sources) * row_count
    given = [weight, queries] + [latents for latents, _, _ in sources]
    given += [array for array in (key_value, state) if array is not None]

    def kernel(mask_ref, count_ref, weight_ref, queries_ref, *refs):
        latents_refs, refs = refs[: len(sources)], list(refs[len(sources) :])
        key_value_ref = None if key_value is None else refs.pop(0)
        old_ref = None if state is None else refs.pop(0)
        values_ref, keys_ref = refs.pop(), refs.pop()
        seq_index = lax.axis_index("seq")
        core = lax.rem(seq_index, CORES)
        chip_tile = seq_index - core
        tiles = [chip_tile + core, chip_tile + 1 - core]
        key_tiles = list(tiles) if local_rows else []

        def place(start, keys, values):
            rows = slice(start, start + keys.shape[0])
            keys_ref[rows, :] = keys
            for group in range(groups):
                first = 2 * group * LANES
                values_ref[rows, first : first + LANES] = values[:, group * LANES : (group + 1) * LANES]
                values_ref[rows, first + LANES : first + 2 * LANES] = jnp.ones((keys.shape[0], LANES), dtype)

        if local_rows:
            place(0, key_value_ref[:, :own], key_value_ref[:, own:])
        for part, (_, y_step, swapped) in enumerate(sources):
            projected = jnp.dot(
                latents_refs[part][...], weight_ref[:, own:], preferred_element_type=jnp.float32
            ).astype(dtype)
            place(local_rows + part * row_count, projected[:, :own], projected[:, own:])
            from_same = lax.rem(seq_index + seq_count - CORES * y_step, seq_count)
            key_tiles.append(from_same + 1 - 2 * core if swapped else from_same)
        for member in range(CORES):
            bias = jnp.concatenate(
                [key_bias(mask_ref, count_ref, tiles[member], key_tile, row_count) for key_tile in key_tiles], axis=1
            )
            for group in range(groups):
                lanes = slice(group * LANES, (group + 1) * LANES)
                for start in range(0, row_count, ROWS):
                    chunk = slice(start, start + ROWS)
                    parts = attend_part(
                        queries_ref[member, chunk, lanes],
                        keys_ref[:, lanes],
                        values_ref[:, 2 * group * LANES : 2 * (group + 1) * LANES],
                        bias,
                    )
                    if old_ref is not None:
                        parts = merge([old_ref[member, which, chunk, lanes] for which in range(3)], parts)
                    if last:
                        position = start + lax.broadcasted_iota(jnp.int32, (ROWS, 1), 0)
                        attended = jnp.where(position < count_ref[tiles[member]], parts[2] / parts[1], 0.0)
                        refs[member][chunk, lanes] = attended.astype(dtype)
                    else:
                        for which, part in enumerate(parts):
                            refs[0][member, which, chunk, lanes] = part

    if last:
        out_shapes = [shaped((row_count, own), dtype)] * CORES
    else:
        out_shapes = [shaped((CORES, 3, row_count, own), jnp.float32)]
    return call(
        kernel,
        "attend_last" if last else "attend",
        [SMEM, SMEM] + [VMEM] * len(given),
        out_shapes,
        scratch_shapes=[pltpu.VMEM((slots, own), dtype), pltpu.VMEM((slots, 2 * own), dtype)],
        cost=COST,
    )(tile_mask, tile_counts, *given)


def project_out(attended_own, attended_partner, out_own, out_partner):
    row_count, own = attended_own.shape
    side = out_own.shape[1]
    dtype = attended_own.dtype

    def kernel(own_ref, partner_ref, out_own_ref, out_partner_ref, result_ref, staged_ref, sems):
        core = lax.rem(lax.axis_index("seq"), CORES)
        own_rows = pl.ds(pl.multiple_of(core * own, 16), own)
        partner_rows = pl.ds(pl.multiple_of((1 - core) * own, 16), own)
        copies = []
        for half, weight_ref in enumerate((out_own_ref, out_partner_ref)):
            total = jnp.dot(own_ref[...], weight_ref[own_rows, :], preferred_element_type=jnp.float32)
            total += jnp.dot(partner_ref[...], weight_ref[partner_rows, :], preferred_element_type=jnp.float32)
            staged_ref[half] = total.astype(dtype)
            start = pl.multiple_of((core if half == 0 else 1 - core) * side, LANES)
            copies.append(
                pltpu.make_async_copy(staged_ref.at[half], result_ref.at[:, pl.ds(start, side)], sems.at[half])
            )
            copies[-1].start()
        for copy in copies:
            copy.wait()

    return call(
        kernel,
        "project_out",
        [VMEM] * 4,
        [shaped((row_count, CORES * side), dtype)],
        [HBM],
        scratch_shapes=[pltpu.VMEM((CORES, row_count, side), dtype), pltpu.SemaphoreType.DMA((CORES,))],
    )(attended_own, attended_partner, out_own, out_partner)[0]


def after(array, *others):
    return lax.optimization_barrier((array, *others))[0]


def local(latents, qkv_weight, out_weight, tile_mask, tile_counts):
    seq_count = lax.axis_size("seq")
    fsdp_count = lax.axis_size("fsdp")
    z_count, x_count = grid_of(fsdp_count)
    chips = seq_count // CORES
    latents_own = latents[0]

    def hop(array, z_step, x_step):
        return lax.ppermute(array, "fsdp", rotation(z_count, x_count, z_step, x_step))

    def flip(array, shift):
        return lax.ppermute(array, "fsdp", [(f, f ^ (shift * x_count)) for f in range(fsdp_count)])

    along_y = [y_rotation(latents_own, seq_count, step) for step in range(1, chips)]
    latents_other = core_swap(latents_own, seq_count)
    half, packed = halves(qkv_weight, out_weight)

    came = {(0, 0): half}
    for x_step in range(1, x_count):
        came[0, x_step] = hop(after(packed, latents_other), 0, x_step)
    beside = [came[0, x_step] for x_step in range(1, x_count)]
    order = [step for step in range(2, z_count)] + [1]
    for z_step in order:
        came[z_step, 0] = hop(half, z_step, 0)
        for x_step in range(1, x_count):
            if z_step > 1:
                came[z_step, x_step] = hop(after(came[z_step, 0], came[0, 1]), 0, x_step)
            else:
                came[z_step, x_step] = hop(after(half, *beside, came[2, 0]), z_step, x_step)

    out_own = side_by_side([packed] + beside, x_count, half.shape[0], out_weight.shape[0], out_weight.shape[1] // CORES)
    units, shift = 1, z_count // 2
    while shift > 1:
        out_own = pair_up(out_own, flip(after(out_own, came[1, 0], came[2, 1]), shift), units, shift, x_count)
        units, shift = 2 * units, shift // 2
    out_got = flip(out_own, shift)

    queries, weight, key_value = project(
        z_count, x_count, list(came), list(came.values()), latents_own, latents_other
    )
    steps = [(step, swapped) for step in range(1, chips) for swapped in (False, True)]
    near, _, _ = lax.optimization_barrier((along_y, key_value, out_own))
    tokens = {(step, False): near[step - 1] for step in range(1, chips)}
    tokens.update({(step, True): core_swap(near[step - 1], seq_count) for step in range(1, chips)})
    state = None
    for first in range(-1, len(steps), 2):
        sources = [(tokens[step], *step) for step in steps[max(first, 0) : first + 2]]
        last = first + 2 > len(steps)
        result = attend(
            seq_count,
            sources,
            key_value if first < 0 else None,
            state,
            last,
            weight,
            queries,
            tile_mask,
            tile_counts,
        )
        if first < 0:
            out_own = pair_up(out_own, after(out_got, result[0]), units, shift, x_count)
            out_partner = core_swap(out_own, seq_count)
        state = None if last else result[0]
    attended_own, attended_other = result
    attended_partner = core_swap(attended_other, seq_count)
    return project_out(attended_own, attended_partner, out_own, out_partner)[None]


def solution(mesh):
    return jax.shard_map(
        local,
        mesh=mesh,
        in_specs=(P("fsdp", "seq", None), P("fsdp", None), P("fsdp", None), P(), P()),
        out_specs=P("fsdp", "seq", None),
        check_vma=False,
    )
```

```python
import jax
import jax.numpy as jnp
from jax import lax
from jax.experimental import pallas as pl
from jax.experimental.pallas import tpu as pltpu
from jax.sharding import PartitionSpec as P

E = 64
LANES = 128
CORES = 2
NEG = -1e30
ROWS = 192
COST1 = 1_000_000_000
COST = 1_000_000_000

VMEM = pl.BlockSpec(memory_space=pltpu.VMEM)
SMEM = pl.BlockSpec(memory_space=pltpu.SMEM)
HBM = pl.BlockSpec(memory_space=pltpu.HBM)


def grid_of(fsdp_count):
    x_count = 1
    while (2 * x_count) ** 2 <= fsdp_count and fsdp_count % (2 * x_count) == 0:
        x_count *= 2
    return fsdp_count // x_count, x_count


def rotation(z_count, x_count, z_step, x_step):
    return [
        (z * x_count + x, (z + z_step) % z_count * x_count + (x + x_step) % x_count)
        for z in range(z_count)
        for x in range(x_count)
    ]


def core_swap(array, seq_count):
    return lax.ppermute(array, "seq", [(s, s ^ 1) for s in range(seq_count)])


def y_rotation(array, seq_count, step):
    return lax.ppermute(array, "seq", [(s, (s + CORES * step) % seq_count) for s in range(seq_count)])


def call(kernel, name, in_specs, out_shapes, out_specs=None, scratch_shapes=(), cost=0, aliases={}):
    out_specs = [VMEM] * len(out_shapes) if out_specs is None else out_specs
    shapes = [
        pltpu.VMEM(shape.shape, shape.dtype) if spec is VMEM else shape for shape, spec in zip(out_shapes, out_specs)
    ]
    inner = pl.pallas_call(
        kernel,
        out_shape=shapes,
        in_specs=in_specs,
        out_specs=out_specs,
        scratch_shapes=scratch_shapes,
        input_output_aliases=aliases,
        cost_estimate=pl.CostEstimate(flops=cost, bytes_accessed=0, transcendentals=0) if cost else None,
        compiler_params=pltpu.CompilerParams(vmem_limit_bytes=24 << 20),
        name=name,
    )

    def run(*args):
        return inner(
            *[
                pltpu.with_memory_space_constraint(arg, pltpu.HBM if spec is SMEM else spec.memory_space)
                for arg, spec in zip(args, in_specs)
            ]
        )

    return run


def shaped(shape, dtype):
    return jax.ShapeDtypeStruct(shape, dtype)


def strips(width, columns):
    strip = min(width, columns)
    return [(start, strip) for start in range(0, width, strip)]


def halves(qkv_weight, out_weight):
    rows, columns = qkv_weight.shape
    head_columns = columns // 3
    own = head_columns // CORES
    out_rows, width = out_weight.shape
    side = width // CORES
    pieces = strips(side, 3 * own)

    def kernel(qkv_ref, out_ref, half_ref, packed_ref, sems):
        core = lax.rem(lax.axis_index("seq"), CORES)
        copies = []

        def copy(source, target):
            copies.append(pltpu.make_async_copy(source, target, sems.at[len(copies)]))
            copies[-1].start()

        for part in range(3):
            source = qkv_ref.at[:, pl.ds(pl.multiple_of(part * head_columns + core * own, LANES), own)]
            lanes = slice(part * own, (part + 1) * own)
            copy(source, half_ref.at[:, lanes])
            copy(source, packed_ref.at[:rows, lanes])
        for piece, (start, strip) in enumerate(pieces):
            first = rows + piece * out_rows
            copy(
                out_ref.at[:, pl.ds(pl.multiple_of(core * side + start, LANES), strip)],
                packed_ref.at[first : first + out_rows, :strip],
            )
        for each in copies:
            each.wait()

    return call(
        kernel,
        "halves",
        [HBM, HBM],
        [
            shaped((rows, 3 * own), qkv_weight.dtype),
            shaped((rows + len(pieces) * out_rows, 3 * own), qkv_weight.dtype),
        ],
        scratch_shapes=[pltpu.SemaphoreType.DMA((6 + len(pieces),))],
    )(qkv_weight, out_weight)


def collect(blocks, x_count, z_count, rows, out_rows, side):
    pieces = strips(side, blocks[0][0].shape[1])
    flat = [(half, step) for half in range(len(blocks)) for step in range(x_count)]

    def kernel(*refs):
        fsdp_index = lax.axis_index("fsdp")
        x_index = lax.rem(fsdp_index, x_count)
        bit = lax.rem(fsdp_index // (x_count * (z_count // 2)), 2)
        for (half, step), ref in zip(flat, refs):
            place = (1 - bit if half else bit) * x_count + lax.rem(x_index + x_count - step, x_count)
            for piece, (start, strip) in enumerate(pieces):
                first = rows + piece * out_rows
                refs[-1][pl.ds(pl.multiple_of(place * out_rows, 16), out_rows), start : start + strip] = ref[
                    first : first + out_rows, :strip
                ]

    return call(
        kernel, "collect", [VMEM] * len(flat), [shaped((len(flat) * out_rows, side), blocks[0][0].dtype)]
    )(*[blocks[half][step] for half, step in flat])[0]


def pair_up(own, got, units, shift, x_count):
    rows, columns = own.shape
    each = rows // units

    def kernel(own_ref, got_ref, pair_ref):
        bit = lax.rem(lax.axis_index("fsdp") // (x_count * shift), 2)
        for unit in range(units):
            piece = slice(unit * each, (unit + 1) * each)
            pair_ref[pl.ds(pl.multiple_of((2 * unit + bit) * each, 16), each), :] = own_ref[piece, :]
            pair_ref[pl.ds(pl.multiple_of((2 * unit + 1 - bit) * each, 16), each), :] = got_ref[piece, :]

    return call(kernel, "pair_up", [VMEM, VMEM], [shaped((2 * rows, columns), own.dtype)])(own, got)[0]


def lane_pick(per_head):
    lane = lax.broadcasted_iota(jnp.int32, (1, LANES), 1)
    picked = per_head[0]
    for head in range(1, len(per_head)):
        picked = jnp.where(lane >= head * E, per_head[head], picked)
    return jnp.broadcast_to(picked, (picked.shape[0], LANES))


def attend_part(queries, keys, values, bias):
    lane = lax.broadcasted_iota(jnp.int32, (1, LANES), 1)
    rows = queries.shape[0]
    heads = LANES // E
    zero = jnp.zeros_like(queries)
    stacked = jnp.concatenate(
        [jnp.where((lane >= head * E) & (lane < (head + 1) * E), queries, zero) for head in range(heads)], axis=0
    )
    scores = lax.dot_general(stacked, keys, (((1,), (1,)), ((), ())), preferred_element_type=jnp.float32) + bias
    row_max = jnp.max(scores, axis=1, keepdims=True)
    numerators = jnp.exp(scores - row_max).astype(values.dtype)
    summed = jnp.dot(numerators, values, preferred_element_type=jnp.float32)

    def pick(array):
        return lane_pick([array[head * rows : (head + 1) * rows] for head in range(heads)])

    return pick(row_max), pick(summed[:, LANES:]), pick(summed[:, :LANES])


def merge(old, new):
    top = jnp.maximum(old[0], new[0])
    keep = jnp.exp(old[0] - top)
    add = jnp.exp(new[0] - top)
    return top, old[1] * keep + new[1] * add, old[2] * keep + new[2] * add


def key_bias(mask_ref, count_ref, tile, key_tile, slots):
    slot = lax.broadcasted_iota(jnp.int32, (1, slots), 1)
    live = jnp.where(mask_ref[tile, key_tile] > 0, count_ref[key_tile], 0)
    return jnp.where(slot < live, 0.0, NEG)


def project(z_count, x_count, shifts, blocks, latents_own, latents_other):
    count = len(blocks)
    columns = blocks[0].shape[1]
    own = columns // 3
    row_count, depth = latents_own.shape
    rows = depth // count
    dtype = latents_own.dtype
    scale = float(E) ** -0.5

    def kernel(own_ref, other_ref, *refs):
        block_refs = refs[:count]
        queries_ref, weight_ref, key_value_ref, latents_ref, sem = refs[count:]
        fetch = pltpu.make_async_copy(own_ref, latents_ref, sem)
        fetch.start()
        fsdp_index = lax.axis_index("fsdp")
        z_index = fsdp_index // x_count
        x_index = lax.rem(fsdp_index, x_count)
        for (dz, dx), block_ref in zip(shifts, block_refs):
            place = lax.rem(z_index + z_count - dz, z_count) * x_count + lax.rem(x_index + x_count - dx, x_count)
            weight_ref[pl.ds(pl.multiple_of(place * rows, 16), rows), :] = block_ref[:rows, :]
        for member, from_ref in ((1, other_ref), (0, latents_ref)):
            if member == 0:
                fetch.wait()
            projected = jnp.dot(from_ref[...], weight_ref[...], preferred_element_type=jnp.float32).astype(dtype)
            queries_ref[member] = projected[:, :own] * jnp.asarray(scale, dtype)
            key_value_ref[member * row_count : (member + 1) * row_count, :] = projected[:, own:]

    return call(
        kernel,
        "project",
        [HBM] + [VMEM] * (count + 1),
        [
            shaped((CORES, row_count, own), dtype),
            shaped((depth, columns), dtype),
            shaped((CORES * row_count, 2 * own), dtype),
        ],
        scratch_shapes=[pltpu.VMEM((row_count, depth), dtype), pltpu.SemaphoreType.DMA(())],
        cost=COST1,
    )(latents_own, latents_other, *blocks)


def attend(seq_count, sources, key_value, state, last, weight, queries, tile_mask, tile_counts):
    columns = weight.shape[1]
    own = columns // 3
    row_count = queries.shape[1]
    dtype = queries.dtype
    groups = own // LANES
    local_rows = 0 if key_value is None else CORES * row_count
    slots = local_rows + len(sources) * row_count
    given = [weight, queries] + [latents for latents, _, _ in sources]
    given += [array for array in (key_value, state) if array is not None]

    def kernel(mask_ref, count_ref, weight_ref, queries_ref, *refs):
        latents_refs, refs = refs[: len(sources)], list(refs[len(sources) :])
        key_value_ref = None if key_value is None else refs.pop(0)
        old_ref = None if state is None else refs.pop(0)
        values_ref, keys_ref = refs.pop(), refs.pop()
        seq_index = lax.axis_index("seq")
        core = lax.rem(seq_index, CORES)
        chip_tile = seq_index - core
        tiles = [chip_tile + core, chip_tile + 1 - core]
        key_tiles = list(tiles) if local_rows else []

        def place(start, keys, values):
            rows = slice(start, start + keys.shape[0])
            keys_ref[rows, :] = keys
            for group in range(groups):
                first = 2 * group * LANES
                values_ref[rows, first : first + LANES] = values[:, group * LANES : (group + 1) * LANES]
                values_ref[rows, first + LANES : first + 2 * LANES] = jnp.ones((keys.shape[0], LANES), dtype)

        if local_rows:
            place(0, key_value_ref[:, :own], key_value_ref[:, own:])
        for part, (_, y_step, swapped) in enumerate(sources):
            projected = jnp.dot(
                latents_refs[part][...], weight_ref[:, own:], preferred_element_type=jnp.float32
            ).astype(dtype)
            place(local_rows + part * row_count, projected[:, :own], projected[:, own:])
            from_same = lax.rem(seq_index + seq_count - CORES * y_step, seq_count)
            key_tiles.append(from_same + 1 - 2 * core if swapped else from_same)
        for member in range(CORES):
            bias = jnp.concatenate(
                [key_bias(mask_ref, count_ref, tiles[member], key_tile, row_count) for key_tile in key_tiles], axis=1
            )
            for group in range(groups):
                lanes = slice(group * LANES, (group + 1) * LANES)
                for start in range(0, row_count, ROWS):
                    chunk = slice(start, start + ROWS)
                    parts = attend_part(
                        queries_ref[member, chunk, lanes],
                        keys_ref[:, lanes],
                        values_ref[:, 2 * group * LANES : 2 * (group + 1) * LANES],
                        bias,
                    )
                    if old_ref is not None:
                        parts = merge([old_ref[member, which, chunk, lanes] for which in range(3)], parts)
                    if last:
                        position = start + lax.broadcasted_iota(jnp.int32, (ROWS, 1), 0)
                        attended = jnp.where(position < count_ref[tiles[member]], parts[2] / parts[1], 0.0)
                        refs[member][chunk, lanes] = attended.astype(dtype)
                    else:
                        for which, part in enumerate(parts):
                            refs[0][member, which, chunk, lanes] = part

    if last:
        out_shapes = [shaped((row_count, own), dtype)] * CORES
    else:
        out_shapes = [shaped((CORES, 3, row_count, own), jnp.float32)]
    return call(
        kernel,
        "attend_last" if last else "attend",
        [SMEM, SMEM] + [VMEM] * len(given),
        out_shapes,
        scratch_shapes=[pltpu.VMEM((slots, own), dtype), pltpu.VMEM((slots, 2 * own), dtype)],
        cost=COST,
    )(tile_mask, tile_counts, *given)


def project_out(far, attended_own, attended_partner, weight, result):
    row_count, own = attended_own.shape
    side = weight.shape[1]
    dtype = attended_own.dtype
    given = [attended_own, attended_partner, weight]

    def kernel(own_ref, partner_ref, weight_ref, *refs):
        result_ref, staged_ref, sem = refs[-3:]
        core = lax.rem(lax.axis_index("seq"), CORES)
        own_rows = pl.ds(pl.multiple_of(core * own, 16), own)
        partner_rows = pl.ds(pl.multiple_of((1 - core) * own, 16), own)
        total = jnp.dot(own_ref[...], weight_ref[own_rows, :], preferred_element_type=jnp.float32)
        total += jnp.dot(partner_ref[...], weight_ref[partner_rows, :], preferred_element_type=jnp.float32)
        staged_ref[...] = total.astype(dtype)
        start = pl.multiple_of((1 - core if far else core) * side, LANES)
        copy = pltpu.make_async_copy(staged_ref, result_ref.at[:, pl.ds(start, side)], sem)
        copy.start()
        copy.wait()

    return call(
        kernel,
        "project_out",
        [VMEM] * 3 + ([HBM] if far else []),
        [shaped((row_count, CORES * side), dtype)],
        [HBM],
        scratch_shapes=[pltpu.VMEM((row_count, side), dtype), pltpu.SemaphoreType.DMA(())],
        aliases={3: 0} if far else {},
    )(*given, *([result] if far else []))[0]


def after(array, *others):
    return lax.optimization_barrier((array, *others))[0]


def local(latents, qkv_weight, out_weight, tile_mask, tile_counts):
    seq_count = lax.axis_size("seq")
    fsdp_count = lax.axis_size("fsdp")
    z_count, x_count = grid_of(fsdp_count)
    chips = seq_count // CORES
    latents_own = latents[0]

    def hop(array, z_step, x_step):
        return lax.ppermute(array, "fsdp", rotation(z_count, x_count, z_step, x_step))

    def flip(array, shift):
        return lax.ppermute(array, "fsdp", [(f, f ^ (shift * x_count)) for f in range(fsdp_count)])

    along_y = [y_rotation(latents_own, seq_count, step) for step in range(1, chips)]
    latents_other = core_swap(latents_own, seq_count)
    half, packed = halves(qkv_weight, out_weight)

    came = {(0, 0): half}
    for x_step in range(1, x_count):
        came[0, x_step] = hop(after(packed, latents_other), 0, x_step)
    beside = [came[0, x_step] for x_step in range(1, x_count)]
    order = [step for step in range(2, z_count)] + [1]
    turn = z_count // 2
    for z_step in order:
        came[z_step, 0] = hop(packed if z_step == turn else half, z_step, 0)
    for x_step in range(1, x_count):
        for z_step in order[:-1]:
            ahead = beside if z_step == turn else [came[1, 0]]
            came[z_step, x_step] = hop(after(came[z_step, 0], *ahead), 0, x_step)
        came[1, x_step] = hop(after(half, *beside, came[turn, 0]), 1, x_step)

    out_own = collect(
        [[packed] + beside, [came[turn, x_step] for x_step in range(x_count)]],
        x_count,
        z_count,
        half.shape[0],
        out_weight.shape[0],
        out_weight.shape[1] // CORES,
    )
    units, shift = 2, turn // 2
    while shift > 1:
        out_own = pair_up(out_own, flip(out_own, shift), units, shift, x_count)
        units, shift = 2 * units, shift // 2
    out_got = flip(out_own, shift)

    queries, weight, key_value = project(
        z_count, x_count, list(came), list(came.values()), latents_own, latents_other
    )
    steps = [(step, swapped) for step in range(1, chips) for swapped in (False, True)]
    near, _, _ = lax.optimization_barrier((along_y, key_value, out_own))
    tokens = {(step, False): near[step - 1] for step in range(1, chips)}
    tokens.update({(step, True): core_swap(near[step - 1], seq_count) for step in range(1, chips)})
    state = None
    for first in range(-1, len(steps), 2):
        sources = [(tokens[step], *step) for step in steps[max(first, 0) : first + 2]]
        last = first + 2 > len(steps)
        result = attend(
            seq_count,
            sources,
            key_value if first < 0 else None,
            state,
            last,
            weight,
            queries,
            tile_mask,
            tile_counts,
        )
        state = None if last else result[0]
    attended_own, attended_other = result
    attended_partner = core_swap(attended_other, seq_count)
    out_own = pair_up(out_own, after(out_got, attended_other), units, shift, x_count)
    out_partner = core_swap(out_own, seq_count)
    near_side = project_out(False, attended_own, attended_partner, out_own, None)
    return project_out(True, attended_own, attended_partner, out_partner, near_side)[None]


def solution(mesh):
    return jax.shard_map(
        local,
        mesh=mesh,
        in_specs=(P("fsdp", "seq", None), P("fsdp", None), P("fsdp", None), P(), P()),
        out_specs=P("fsdp", "seq", None),
        check_vma=False,
    )
```

```python
import jax
import jax.numpy as jnp
from jax import lax
from jax.experimental import pallas as pl
from jax.experimental.pallas import tpu as pltpu
from jax.sharding import PartitionSpec as P

E = 64
LANES = 128
CORES = 2
NEG = -1e30
ROWS = 192
COST1 = 1_000_000_000
COST = 1_000_000_000

VMEM = pl.BlockSpec(memory_space=pltpu.VMEM)
SMEM = pl.BlockSpec(memory_space=pltpu.SMEM)
HBM = pl.BlockSpec(memory_space=pltpu.HBM)


def grid_of(fsdp_count):
    x_count = 1
    while (2 * x_count) ** 2 <= fsdp_count and fsdp_count % (2 * x_count) == 0:
        x_count *= 2
    return fsdp_count // x_count, x_count


def rotation(z_count, x_count, z_step, x_step):
    return [
        (z * x_count + x, (z + z_step) % z_count * x_count + (x + x_step) % x_count)
        for z in range(z_count)
        for x in range(x_count)
    ]


def core_swap(array, seq_count):
    return lax.ppermute(array, "seq", [(s, s ^ 1) for s in range(seq_count)])


def y_rotation(array, seq_count, step):
    return lax.ppermute(array, "seq", [(s, (s + CORES * step) % seq_count) for s in range(seq_count)])


def call(kernel, name, in_specs, out_shapes, out_specs=None, scratch_shapes=(), cost=0, aliases={}):
    out_specs = [VMEM] * len(out_shapes) if out_specs is None else out_specs
    shapes = [
        pltpu.VMEM(shape.shape, shape.dtype) if spec is VMEM else shape for shape, spec in zip(out_shapes, out_specs)
    ]
    inner = pl.pallas_call(
        kernel,
        out_shape=shapes,
        in_specs=in_specs,
        out_specs=out_specs,
        scratch_shapes=scratch_shapes,
        input_output_aliases=aliases,
        cost_estimate=pl.CostEstimate(flops=cost, bytes_accessed=0, transcendentals=0) if cost else None,
        compiler_params=pltpu.CompilerParams(vmem_limit_bytes=24 << 20),
        name=name,
    )

    def run(*args):
        return inner(
            *[
                pltpu.with_memory_space_constraint(arg, pltpu.HBM if spec is SMEM else spec.memory_space)
                for arg, spec in zip(args, in_specs)
            ]
        )

    return run


def shaped(shape, dtype):
    return jax.ShapeDtypeStruct(shape, dtype)


def strips(width, columns):
    strip = min(width, columns)
    return [(start, strip) for start in range(0, width, strip)]


def halves(qkv_weight, out_weight):
    rows, columns = qkv_weight.shape
    head_columns = columns // 3
    own = head_columns // CORES
    out_rows, width = out_weight.shape
    side = width // CORES
    pieces = strips(side, 3 * own)

    def kernel(qkv_ref, out_ref, half_ref, packed_ref, sems):
        core = lax.rem(lax.axis_index("seq"), CORES)
        copies = []

        def copy(source, target):
            copies.append(pltpu.make_async_copy(source, target, sems.at[len(copies)]))
            copies[-1].start()

        for part in range(3):
            source = qkv_ref.at[:, pl.ds(pl.multiple_of(part * head_columns + core * own, LANES), own)]
            lanes = slice(part * own, (part + 1) * own)
            copy(source, half_ref.at[:, lanes])
            copy(source, packed_ref.at[:rows, lanes])
        for piece, (start, strip) in enumerate(pieces):
            first = rows + piece * out_rows
            copy(
                out_ref.at[:, pl.ds(pl.multiple_of(core * side + start, LANES), strip)],
                packed_ref.at[first : first + out_rows, :strip],
            )
        for each in copies:
            each.wait()

    return call(
        kernel,
        "halves",
        [HBM, HBM],
        [
            shaped((rows, 3 * own), qkv_weight.dtype),
            shaped((rows + len(pieces) * out_rows, 3 * own), qkv_weight.dtype),
        ],
        scratch_shapes=[pltpu.SemaphoreType.DMA((6 + len(pieces),))],
    )(qkv_weight, out_weight)


def collect(blocks, x_count, z_count, rows, out_rows, side):
    pieces = strips(side, blocks[0][0].shape[1])
    flat = [(half, step) for half in range(len(blocks)) for step in range(x_count)]

    def kernel(*refs):
        fsdp_index = lax.axis_index("fsdp")
        x_index = lax.rem(fsdp_index, x_count)
        bit = lax.rem(fsdp_index // (x_count * (z_count // 2)), 2)
        for (half, step), ref in zip(flat, refs):
            place = (1 - bit if half else bit) * x_count + lax.rem(x_index + x_count - step, x_count)
            for piece, (start, strip) in enumerate(pieces):
                first = rows + piece * out_rows
                refs[-1][pl.ds(pl.multiple_of(place * out_rows, 16), out_rows), start : start + strip] = ref[
                    first : first + out_rows, :strip
                ]

    return call(
        kernel, "collect", [VMEM] * len(flat), [shaped((len(flat) * out_rows, side), blocks[0][0].dtype)]
    )(*[blocks[half][step] for half, step in flat])[0]


def pair_up(own, got, units, shift, x_count):
    rows, columns = own.shape
    each = rows // units

    def kernel(own_ref, got_ref, pair_ref):
        bit = lax.rem(lax.axis_index("fsdp") // (x_count * shift), 2)
        for unit in range(units):
            piece = slice(unit * each, (unit + 1) * each)
            pair_ref[pl.ds(pl.multiple_of((2 * unit + bit) * each, 16), each), :] = own_ref[piece, :]
            pair_ref[pl.ds(pl.multiple_of((2 * unit + 1 - bit) * each, 16), each), :] = got_ref[piece, :]

    return call(kernel, "pair_up", [VMEM, VMEM], [shaped((2 * rows, columns), own.dtype)])(own, got)[0]


def lane_pick(per_head):
    lane = lax.broadcasted_iota(jnp.int32, (1, LANES), 1)
    picked = per_head[0]
    for head in range(1, len(per_head)):
        picked = jnp.where(lane >= head * E, per_head[head], picked)
    return jnp.broadcast_to(picked, (picked.shape[0], LANES))


def attend_part(queries, keys, values, bias):
    lane = lax.broadcasted_iota(jnp.int32, (1, LANES), 1)
    rows = queries.shape[0]
    heads = LANES // E
    zero = jnp.zeros_like(queries)
    stacked = jnp.concatenate(
        [jnp.where((lane >= head * E) & (lane < (head + 1) * E), queries, zero) for head in range(heads)], axis=0
    )
    scores = lax.dot_general(stacked, keys, (((1,), (1,)), ((), ())), preferred_element_type=jnp.float32) + bias
    row_max = jnp.max(scores, axis=1, keepdims=True)
    numerators = jnp.exp(scores - row_max).astype(values.dtype)
    summed = jnp.dot(numerators, values, preferred_element_type=jnp.float32)

    def pick(array):
        return lane_pick([array[head * rows : (head + 1) * rows] for head in range(heads)])

    return pick(row_max), pick(summed[:, LANES:]), pick(summed[:, :LANES])


def merge(old, new):
    top = jnp.maximum(old[0], new[0])
    keep = jnp.exp(old[0] - top)
    add = jnp.exp(new[0] - top)
    return top, old[1] * keep + new[1] * add, old[2] * keep + new[2] * add


def key_bias(mask_ref, count_ref, tile, key_tile, slots):
    slot = lax.broadcasted_iota(jnp.int32, (1, slots), 1)
    live = jnp.where(mask_ref[tile, key_tile] > 0, count_ref[key_tile], 0)
    return jnp.where(slot < live, 0.0, NEG)


def project(z_count, x_count, shifts, blocks, latents_own, latents_other):
    count = len(blocks)
    columns = blocks[0].shape[1]
    own = columns // 3
    row_count, depth = latents_own.shape
    rows = depth // count
    dtype = latents_own.dtype
    scale = float(E) ** -0.5

    def kernel(own_ref, other_ref, *refs):
        block_refs = refs[:count]
        queries_ref, weight_ref, key_value_ref, latents_ref, sem = refs[count:]
        fetch = pltpu.make_async_copy(own_ref, latents_ref, sem)
        fetch.start()
        fsdp_index = lax.axis_index("fsdp")
        z_index = fsdp_index // x_count
        x_index = lax.rem(fsdp_index, x_count)
        for (dz, dx), block_ref in zip(shifts, block_refs):
            place = lax.rem(z_index + z_count - dz, z_count) * x_count + lax.rem(x_index + x_count - dx, x_count)
            weight_ref[pl.ds(pl.multiple_of(place * rows, 16), rows), :] = block_ref[:rows, :]
        for member, from_ref in ((1, other_ref), (0, latents_ref)):
            if member == 0:
                fetch.wait()
            projected = jnp.dot(from_ref[...], weight_ref[...], preferred_element_type=jnp.float32).astype(dtype)
            queries_ref[member] = projected[:, :own] * jnp.asarray(scale, dtype)
            key_value_ref[member * row_count : (member + 1) * row_count, :] = projected[:, own:]

    return call(
        kernel,
        "project",
        [HBM] + [VMEM] * (count + 1),
        [
            shaped((CORES, row_count, own), dtype),
            shaped((depth, columns), dtype),
            shaped((CORES * row_count, 2 * own), dtype),
        ],
        scratch_shapes=[pltpu.VMEM((row_count, depth), dtype), pltpu.SemaphoreType.DMA(())],
        cost=COST1,
    )(latents_own, latents_other, *blocks)


def attend(seq_count, sources, key_value, state, last, weight, queries, tile_mask, tile_counts):
    columns = weight.shape[1]
    own = columns // 3
    row_count = queries.shape[1]
    dtype = queries.dtype
    groups = own // LANES
    local_rows = 0 if key_value is None else CORES * row_count
    slots = local_rows + len(sources) * row_count
    given = [weight, queries] + [latents for latents, _, _ in sources]
    given += [array for array in (key_value, state) if array is not None]

    def kernel(mask_ref, count_ref, weight_ref, queries_ref, *refs):
        latents_refs, refs = refs[: len(sources)], list(refs[len(sources) :])
        key_value_ref = None if key_value is None else refs.pop(0)
        old_ref = None if state is None else refs.pop(0)
        values_ref, keys_ref = refs.pop(), refs.pop()
        seq_index = lax.axis_index("seq")
        core = lax.rem(seq_index, CORES)
        chip_tile = seq_index - core
        tiles = [chip_tile + core, chip_tile + 1 - core]
        key_tiles = list(tiles) if local_rows else []

        def place(start, keys, values):
            rows = slice(start, start + keys.shape[0])
            keys_ref[rows, :] = keys
            for group in range(groups):
                first = 2 * group * LANES
                values_ref[rows, first : first + LANES] = values[:, group * LANES : (group + 1) * LANES]
                values_ref[rows, first + LANES : first + 2 * LANES] = jnp.ones((keys.shape[0], LANES), dtype)

        if local_rows:
            place(0, key_value_ref[:, :own], key_value_ref[:, own:])
        for part, (_, y_step, swapped) in enumerate(sources):
            projected = jnp.dot(
                latents_refs[part][...], weight_ref[:, own:], preferred_element_type=jnp.float32
            ).astype(dtype)
            place(local_rows + part * row_count, projected[:, :own], projected[:, own:])
            from_same = lax.rem(seq_index + seq_count - CORES * y_step, seq_count)
            key_tiles.append(from_same + 1 - 2 * core if swapped else from_same)
        for member in range(CORES):
            bias = jnp.concatenate(
                [key_bias(mask_ref, count_ref, tiles[member], key_tile, row_count) for key_tile in key_tiles], axis=1
            )
            for group in range(groups):
                lanes = slice(group * LANES, (group + 1) * LANES)
                for start in range(0, row_count, ROWS):
                    chunk = slice(start, start + ROWS)
                    parts = attend_part(
                        queries_ref[member, chunk, lanes],
                        keys_ref[:, lanes],
                        values_ref[:, 2 * group * LANES : 2 * (group + 1) * LANES],
                        bias,
                    )
                    if old_ref is not None:
                        parts = merge([old_ref[member, which, chunk, lanes] for which in range(3)], parts)
                    if last:
                        position = start + lax.broadcasted_iota(jnp.int32, (ROWS, 1), 0)
                        attended = jnp.where(position < count_ref[tiles[member]], parts[2] / parts[1], 0.0)
                        refs[member][chunk, lanes] = attended.astype(dtype)
                    else:
                        for which, part in enumerate(parts):
                            refs[0][member, which, chunk, lanes] = part

    if last:
        out_shapes = [shaped((row_count, own), dtype)] * CORES
    else:
        out_shapes = [shaped((CORES, 3, row_count, own), jnp.float32)]
    return call(
        kernel,
        "attend_last" if last else "attend",
        [SMEM, SMEM] + [VMEM] * len(given),
        out_shapes,
        scratch_shapes=[pltpu.VMEM((slots, own), dtype), pltpu.VMEM((slots, 2 * own), dtype)],
        cost=COST,
    )(tile_mask, tile_counts, *given)


def project_out(attended_own, attended_partner, out_own, out_partner):
    row_count, own = attended_own.shape
    side = out_own.shape[1]
    dtype = attended_own.dtype

    def kernel(own_ref, partner_ref, out_own_ref, out_partner_ref, result_ref, staged_ref, sems):
        core = lax.rem(lax.axis_index("seq"), CORES)
        own_rows = pl.ds(pl.multiple_of(core * own, 16), own)
        partner_rows = pl.ds(pl.multiple_of((1 - core) * own, 16), own)
        copies = []
        for half, weight_ref in enumerate((out_own_ref, out_partner_ref)):
            total = jnp.dot(own_ref[...], weight_ref[own_rows, :], preferred_element_type=jnp.float32)
            total += jnp.dot(partner_ref[...], weight_ref[partner_rows, :], preferred_element_type=jnp.float32)
            staged_ref[half] = total.astype(dtype)
            start = pl.multiple_of((core if half == 0 else 1 - core) * side, LANES)
            copies.append(
                pltpu.make_async_copy(staged_ref.at[half], result_ref.at[:, pl.ds(start, side)], sems.at[half])
            )
            copies[-1].start()
        for copy in copies:
            copy.wait()

    return call(
        kernel,
        "project_out",
        [VMEM] * 4,
        [shaped((row_count, CORES * side), dtype)],
        [HBM],
        scratch_shapes=[pltpu.VMEM((CORES, row_count, side), dtype), pltpu.SemaphoreType.DMA((CORES,))],
    )(attended_own, attended_partner, out_own, out_partner)[0]


def after(array, *others):
    return lax.optimization_barrier((array, *others))[0]


def local(latents, qkv_weight, out_weight, tile_mask, tile_counts):
    seq_count = lax.axis_size("seq")
    fsdp_count = lax.axis_size("fsdp")
    z_count, x_count = grid_of(fsdp_count)
    chips = seq_count // CORES
    latents_own = latents[0]

    def hop(array, z_step, x_step):
        return lax.ppermute(array, "fsdp", rotation(z_count, x_count, z_step, x_step))

    def flip(array, shift):
        return lax.ppermute(array, "fsdp", [(f, f ^ (shift * x_count)) for f in range(fsdp_count)])

    along_y = [y_rotation(latents_own, seq_count, step) for step in range(1, chips)]
    latents_other = core_swap(latents_own, seq_count)
    half, packed = halves(qkv_weight, out_weight)

    came = {(0, 0): half}
    for x_step in range(1, x_count):
        came[0, x_step] = hop(after(packed, latents_other), 0, x_step)
    beside = [came[0, x_step] for x_step in range(1, x_count)]
    turn = z_count // 2
    for z_step in (turn, 1):
        came[z_step, 0] = hop(packed if z_step == turn else half, z_step, 0)
    second = after(half, came[1, 0], *beside)
    third = after(half, came[turn, 0])
    for x_step in range(1, x_count):
        came[turn, x_step] = hop(came[turn, 0], 0, x_step)
        came[1, x_step] = hop(second, 1, x_step)
    for z_step in range(2, z_count):
        if z_step != turn:
            came[z_step, 0] = hop(second, z_step, 0)
            for x_step in range(1, x_count):
                came[z_step, x_step] = hop(third, z_step, x_step)

    out_own = collect(
        [[packed] + beside, [came[turn, x_step] for x_step in range(x_count)]],
        x_count,
        z_count,
        half.shape[0],
        out_weight.shape[0],
        out_weight.shape[1] // CORES,
    )
    units, shift = 2, turn // 2
    while shift > 1:
        out_own = pair_up(out_own, flip(out_own, shift), units, shift, x_count)
        units, shift = 2 * units, shift // 2
    out_got = flip(out_own, shift)

    near = after(along_y, out_own, *list(came.values())[1:])
    far = [core_swap(array, seq_count) for array in near]
    came[0, 0] = after(half, *near)
    queries, weight, key_value = project(
        z_count, x_count, list(came), list(came.values()), latents_own, latents_other
    )
    state = None
    for step in range(1, chips):
        last = step == chips - 1
        result = attend(
            seq_count,
            [(near[step - 1], step, False), (far[step - 1], step, True)],
            key_value if step == 1 else None,
            state,
            last,
            weight,
            queries,
            tile_mask,
            tile_counts,
        )
        state = None if last else result[0]
    attended_own, attended_other = result
    attended_partner = core_swap(attended_other, seq_count)
    out_own = pair_up(out_own, after(out_got, attended_other), units, shift, x_count)
    out_partner = core_swap(out_own, seq_count)
    return project_out(attended_own, attended_partner, out_own, out_partner)[None]


def solution(mesh):
    return jax.shard_map(
        local,
        mesh=mesh,
        in_specs=(P("fsdp", "seq", None), P("fsdp", None), P("fsdp", None), P(), P()),
        out_specs=P("fsdp", "seq", None),
        check_vma=False,
    )
```

```python
import jax
import jax.numpy as jnp
from jax import lax
from jax.experimental import pallas as pl
from jax.experimental.pallas import tpu as pltpu
from jax.sharding import PartitionSpec as P

E = 64
LANES = 128
CORES = 2
NEG = -1e30
ROWS = 192
COST1 = 1_000_000_000
COST = 1_000_000_000

VMEM = pl.BlockSpec(memory_space=pltpu.VMEM)
SMEM = pl.BlockSpec(memory_space=pltpu.SMEM)
HBM = pl.BlockSpec(memory_space=pltpu.HBM)


def grid_of(fsdp_count):
    x_count = 1
    while (2 * x_count) ** 2 <= fsdp_count and fsdp_count % (2 * x_count) == 0:
        x_count *= 2
    return fsdp_count // x_count, x_count


def rotation(z_count, x_count, z_step, x_step):
    return [
        (z * x_count + x, (z + z_step) % z_count * x_count + (x + x_step) % x_count)
        for z in range(z_count)
        for x in range(x_count)
    ]


def core_swap(array, seq_count):
    return lax.ppermute(array, "seq", [(s, s ^ 1) for s in range(seq_count)])


def y_rotation(array, seq_count, step):
    return lax.ppermute(array, "seq", [(s, (s + CORES * step) % seq_count) for s in range(seq_count)])


def call(kernel, name, in_specs, out_shapes, out_specs=None, scratch_shapes=(), cost=0, aliases={}):
    out_specs = [VMEM] * len(out_shapes) if out_specs is None else out_specs
    shapes = [
        pltpu.VMEM(shape.shape, shape.dtype) if spec is VMEM else shape for shape, spec in zip(out_shapes, out_specs)
    ]
    inner = pl.pallas_call(
        kernel,
        out_shape=shapes,
        in_specs=in_specs,
        out_specs=out_specs,
        scratch_shapes=scratch_shapes,
        input_output_aliases=aliases,
        cost_estimate=pl.CostEstimate(flops=cost, bytes_accessed=0, transcendentals=0) if cost else None,
        compiler_params=pltpu.CompilerParams(vmem_limit_bytes=24 << 20),
        name=name,
    )

    def run(*args):
        return inner(
            *[
                pltpu.with_memory_space_constraint(arg, pltpu.HBM if spec is SMEM else spec.memory_space)
                for arg, spec in zip(args, in_specs)
            ]
        )

    return run


def shaped(shape, dtype):
    return jax.ShapeDtypeStruct(shape, dtype)


def strips(width, columns):
    strip = min(width, columns)
    return [(start, strip) for start in range(0, width, strip)]


def halves(qkv_weight, out_weight):
    rows, columns = qkv_weight.shape
    head_columns = columns // 3
    own = head_columns // CORES
    out_rows, width = out_weight.shape
    side = width // CORES
    pieces = strips(side, 3 * own)

    def kernel(qkv_ref, out_ref, half_ref, packed_ref, sems):
        core = lax.rem(lax.axis_index("seq"), CORES)
        copies = []

        def copy(source, target):
            copies.append(pltpu.make_async_copy(source, target, sems.at[len(copies)]))
            copies[-1].start()

        for part in range(3):
            source = qkv_ref.at[:, pl.ds(pl.multiple_of(part * head_columns + core * own, LANES), own)]
            lanes = slice(part * own, (part + 1) * own)
            copy(source, half_ref.at[:, lanes])
            copy(source, packed_ref.at[:rows, lanes])
        for piece, (start, strip) in enumerate(pieces):
            first = rows + piece * out_rows
            copy(
                out_ref.at[:, pl.ds(pl.multiple_of(core * side + start, LANES), strip)],
                packed_ref.at[first : first + out_rows, :strip],
            )
        for each in copies:
            each.wait()

    return call(
        kernel,
        "halves",
        [HBM, HBM],
        [
            shaped((rows, 3 * own), qkv_weight.dtype),
            shaped((rows + len(pieces) * out_rows, 3 * own), qkv_weight.dtype),
        ],
        scratch_shapes=[pltpu.SemaphoreType.DMA((6 + len(pieces),))],
    )(qkv_weight, out_weight)


def collect(blocks, x_count, z_count, rows, out_rows, side):
    pieces = strips(side, blocks[0][0].shape[1])
    flat = [(half, step) for half in range(len(blocks)) for step in range(x_count)]

    def kernel(*refs):
        fsdp_index = lax.axis_index("fsdp")
        x_index = lax.rem(fsdp_index, x_count)
        bit = lax.rem(fsdp_index // (x_count * (z_count // 2)), 2)
        for (half, step), ref in zip(flat, refs):
            place = (1 - bit if half else bit) * x_count + lax.rem(x_index + x_count - step, x_count)
            for piece, (start, strip) in enumerate(pieces):
                first = rows + piece * out_rows
                refs[-1][pl.ds(pl.multiple_of(place * out_rows, 16), out_rows), start : start + strip] = ref[
                    first : first + out_rows, :strip
                ]

    return call(
        kernel, "collect", [VMEM] * len(flat), [shaped((len(flat) * out_rows, side), blocks[0][0].dtype)]
    )(*[blocks[half][step] for half, step in flat])[0]


def pair_up(own, got, units, shift, x_count):
    rows, columns = own.shape
    each = rows // units

    def kernel(own_ref, got_ref, pair_ref):
        bit = lax.rem(lax.axis_index("fsdp") // (x_count * shift), 2)
        for unit in range(units):
            piece = slice(unit * each, (unit + 1) * each)
            pair_ref[pl.ds(pl.multiple_of((2 * unit + bit) * each, 16), each), :] = own_ref[piece, :]
            pair_ref[pl.ds(pl.multiple_of((2 * unit + 1 - bit) * each, 16), each), :] = got_ref[piece, :]

    return call(kernel, "pair_up", [VMEM, VMEM], [shaped((2 * rows, columns), own.dtype)])(own, got)[0]


def lane_pick(per_head):
    lane = lax.broadcasted_iota(jnp.int32, (1, LANES), 1)
    picked = per_head[0]
    for head in range(1, len(per_head)):
        picked = jnp.where(lane >= head * E, per_head[head], picked)
    return jnp.broadcast_to(picked, (picked.shape[0], LANES))


def attend_part(queries, keys, values, bias):
    lane = lax.broadcasted_iota(jnp.int32, (1, LANES), 1)
    rows = queries.shape[0]
    heads = LANES // E
    zero = jnp.zeros_like(queries)
    stacked = jnp.concatenate(
        [jnp.where((lane >= head * E) & (lane < (head + 1) * E), queries, zero) for head in range(heads)], axis=0
    )
    scores = lax.dot_general(stacked, keys, (((1,), (1,)), ((), ())), preferred_element_type=jnp.float32) + bias
    row_max = jnp.max(scores, axis=1, keepdims=True)
    numerators = jnp.exp(scores - row_max).astype(values.dtype)
    summed = jnp.dot(numerators, values, preferred_element_type=jnp.float32)

    def pick(array):
        return lane_pick([array[head * rows : (head + 1) * rows] for head in range(heads)])

    return pick(row_max), pick(summed[:, LANES:]), pick(summed[:, :LANES])


def merge(old, new):
    top = jnp.maximum(old[0], new[0])
    keep = jnp.exp(old[0] - top)
    add = jnp.exp(new[0] - top)
    return top, old[1] * keep + new[1] * add, old[2] * keep + new[2] * add


def key_bias(mask_ref, count_ref, tile, key_tile, slots):
    slot = lax.broadcasted_iota(jnp.int32, (1, slots), 1)
    live = jnp.where(mask_ref[tile, key_tile] > 0, count_ref[key_tile], 0)
    return jnp.where(slot < live, 0.0, NEG)


def project(z_count, x_count, shifts, blocks, latents_own, latents_other):
    count = len(blocks)
    columns = blocks[0].shape[1]
    own = columns // 3
    row_count, depth = latents_own.shape
    rows = depth // count
    dtype = latents_own.dtype
    scale = float(E) ** -0.5

    def kernel(own_ref, other_ref, *refs):
        block_refs = refs[:count]
        queries_ref, weight_ref, key_value_ref, latents_ref, sem = refs[count:]
        fetch = pltpu.make_async_copy(own_ref, latents_ref, sem)
        fetch.start()
        fsdp_index = lax.axis_index("fsdp")
        z_index = fsdp_index // x_count
        x_index = lax.rem(fsdp_index, x_count)
        for (dz, dx), block_ref in zip(shifts, block_refs):
            place = lax.rem(z_index + z_count - dz, z_count) * x_count + lax.rem(x_index + x_count - dx, x_count)
            weight_ref[pl.ds(pl.multiple_of(place * rows, 16), rows), :] = block_ref[:rows, :]
        for member, from_ref in ((1, other_ref), (0, latents_ref)):
            if member == 0:
                fetch.wait()
            projected = jnp.dot(from_ref[...], weight_ref[...], preferred_element_type=jnp.float32).astype(dtype)
            queries_ref[member] = projected[:, :own] * jnp.asarray(scale, dtype)
            key_value_ref[member * row_count : (member + 1) * row_count, :] = projected[:, own:]

    return call(
        kernel,
        "project",
        [HBM] + [VMEM] * (count + 1),
        [
            shaped((CORES, row_count, own), dtype),
            shaped((depth, columns), dtype),
            shaped((CORES * row_count, 2 * own), dtype),
        ],
        scratch_shapes=[pltpu.VMEM((row_count, depth), dtype), pltpu.SemaphoreType.DMA(())],
        cost=COST1,
    )(latents_own, latents_other, *blocks)


def attend(seq_count, sources, key_value, state, last, weight, queries, tile_mask, tile_counts):
    columns = weight.shape[1]
    own = columns // 3
    row_count = queries.shape[1]
    dtype = queries.dtype
    groups = own // LANES
    local_rows = 0 if key_value is None else CORES * row_count
    slots = local_rows + len(sources) * row_count
    given = [weight, queries] + [latents for latents, _, _ in sources]
    given += [array for array in (key_value, state) if array is not None]

    def kernel(mask_ref, count_ref, weight_ref, queries_ref, *refs):
        latents_refs, refs = refs[: len(sources)], list(refs[len(sources) :])
        key_value_ref = None if key_value is None else refs.pop(0)
        old_ref = None if state is None else refs.pop(0)
        values_ref, keys_ref = refs.pop(), refs.pop()
        seq_index = lax.axis_index("seq")
        core = lax.rem(seq_index, CORES)
        chip_tile = seq_index - core
        tiles = [chip_tile + core, chip_tile + 1 - core]
        key_tiles = list(tiles) if local_rows else []

        def place(start, keys, values):
            rows = slice(start, start + keys.shape[0])
            keys_ref[rows, :] = keys
            for group in range(groups):
                first = 2 * group * LANES
                values_ref[rows, first : first + LANES] = values[:, group * LANES : (group + 1) * LANES]
                values_ref[rows, first + LANES : first + 2 * LANES] = jnp.ones((keys.shape[0], LANES), dtype)

        if local_rows:
            place(0, key_value_ref[:, :own], key_value_ref[:, own:])
        for part, (_, y_step, swapped) in enumerate(sources):
            projected = jnp.dot(
                latents_refs[part][...], weight_ref[:, own:], preferred_element_type=jnp.float32
            ).astype(dtype)
            place(local_rows + part * row_count, projected[:, :own], projected[:, own:])
            from_same = lax.rem(seq_index + seq_count - CORES * y_step, seq_count)
            key_tiles.append(from_same + 1 - 2 * core if swapped else from_same)
        for member in range(CORES):
            bias = jnp.concatenate(
                [key_bias(mask_ref, count_ref, tiles[member], key_tile, row_count) for key_tile in key_tiles], axis=1
            )
            for group in range(groups):
                lanes = slice(group * LANES, (group + 1) * LANES)
                for start in range(0, row_count, ROWS):
                    chunk = slice(start, start + ROWS)
                    parts = attend_part(
                        queries_ref[member, chunk, lanes],
                        keys_ref[:, lanes],
                        values_ref[:, 2 * group * LANES : 2 * (group + 1) * LANES],
                        bias,
                    )
                    if old_ref is not None:
                        parts = merge([old_ref[member, which, chunk, lanes] for which in range(3)], parts)
                    if last:
                        position = start + lax.broadcasted_iota(jnp.int32, (ROWS, 1), 0)
                        attended = jnp.where(position < count_ref[tiles[member]], parts[2] / parts[1], 0.0)
                        refs[member][chunk, lanes] = attended.astype(dtype)
                    else:
                        for which, part in enumerate(parts):
                            refs[0][member, which, chunk, lanes] = part

    if last:
        out_shapes = [shaped((row_count, own), dtype)] * CORES
    else:
        out_shapes = [shaped((CORES, 3, row_count, own), jnp.float32)]
    return call(
        kernel,
        "attend_last" if last else "attend",
        [SMEM, SMEM] + [VMEM] * len(given),
        out_shapes,
        scratch_shapes=[pltpu.VMEM((slots, own), dtype), pltpu.VMEM((slots, 2 * own), dtype)],
        cost=COST,
    )(tile_mask, tile_counts, *given)


def project_out(attended_own, attended_partner, out_own, out_partner):
    row_count, own = attended_own.shape
    side = out_own.shape[1]
    dtype = attended_own.dtype

    def kernel(own_ref, partner_ref, out_own_ref, out_partner_ref, result_ref, staged_ref, sems):
        core = lax.rem(lax.axis_index("seq"), CORES)
        own_rows = pl.ds(pl.multiple_of(core * own, 16), own)
        partner_rows = pl.ds(pl.multiple_of((1 - core) * own, 16), own)
        copies = []
        for half, weight_ref in enumerate((out_own_ref, out_partner_ref)):
            total = jnp.dot(own_ref[...], weight_ref[own_rows, :], preferred_element_type=jnp.float32)
            total += jnp.dot(partner_ref[...], weight_ref[partner_rows, :], preferred_element_type=jnp.float32)
            staged_ref[half] = total.astype(dtype)
            start = pl.multiple_of((core if half == 0 else 1 - core) * side, LANES)
            copies.append(
                pltpu.make_async_copy(staged_ref.at[half], result_ref.at[:, pl.ds(start, side)], sems.at[half])
            )
            copies[-1].start()
        for copy in copies:
            copy.wait()

    return call(
        kernel,
        "project_out",
        [VMEM] * 4,
        [shaped((row_count, CORES * side), dtype)],
        [HBM],
        scratch_shapes=[pltpu.VMEM((CORES, row_count, side), dtype), pltpu.SemaphoreType.DMA((CORES,))],
    )(attended_own, attended_partner, out_own, out_partner)[0]


def after(array, *others):
    return lax.optimization_barrier((array, *others))[0]


def local(latents, qkv_weight, out_weight, tile_mask, tile_counts):
    seq_count = lax.axis_size("seq")
    fsdp_count = lax.axis_size("fsdp")
    z_count, x_count = grid_of(fsdp_count)
    chips = seq_count // CORES
    latents_own = latents[0]

    def hop(array, z_step, x_step):
        return lax.ppermute(array, "fsdp", rotation(z_count, x_count, z_step, x_step))

    def flip(array, shift):
        return lax.ppermute(array, "fsdp", [(f, f ^ (shift * x_count)) for f in range(fsdp_count)])

    along_y = [y_rotation(latents_own, seq_count, step) for step in range(1, chips)]
    latents_other = core_swap(latents_own, seq_count)
    half, packed = halves(qkv_weight, out_weight)

    came = {(0, 0): half}
    for x_step in range(1, x_count):
        came[0, x_step] = hop(after(packed, latents_other), 0, x_step)
    beside = [came[0, x_step] for x_step in range(1, x_count)]
    turn = z_count // 2
    for z_step in (turn, 1):
        came[z_step, 0] = hop(packed if z_step == turn else half, z_step, 0)
    second = after(half, came[1, 0], *beside)
    for x_step in range(1, x_count):
        came[turn, x_step] = hop(after(came[turn, 0], came[1, 0]), 0, x_step)
        came[1, x_step] = hop(second, 1, x_step)
    for z_step in range(2, z_count):
        if z_step != turn:
            came[z_step, 0] = hop(second, z_step, 0)
            for x_step in range(1, x_count):
                came[z_step, x_step] = hop(second, z_step, x_step)

    out_own = collect(
        [[packed] + beside, [came[turn, x_step] for x_step in range(x_count)]],
        x_count,
        z_count,
        half.shape[0],
        out_weight.shape[0],
        out_weight.shape[1] // CORES,
    )
    units, shift = 2, turn // 2
    while shift > 1:
        out_own = pair_up(out_own, flip(out_own, shift), units, shift, x_count)
        units, shift = 2 * units, shift // 2
    out_got = flip(out_own, shift)

    near = after(along_y, out_own, *list(came.values())[1:])
    far = [core_swap(array, seq_count) for array in near]
    came[0, 0] = after(half, *near)
    queries, weight, key_value = project(
        z_count, x_count, list(came), list(came.values()), latents_own, latents_other
    )
    state = None
    for step in range(1, chips):
        last = step == chips - 1
        result = attend(
            seq_count,
            [(near[step - 1], step, False), (far[step - 1], step, True)],
            key_value if step == 1 else None,
            state,
            last,
            weight,
            queries,
            tile_mask,
            tile_counts,
        )
        state = None if last else result[0]
    attended_own, attended_other = result
    attended_partner = core_swap(attended_other, seq_count)
    out_own = pair_up(out_own, after(out_got, attended_other), units, shift, x_count)
    out_partner = core_swap(out_own, seq_count)
    return project_out(attended_own, attended_partner, out_own, out_partner)[None]


def solution(mesh):
    return jax.shard_map(
        local,
        mesh=mesh,
        in_specs=(P("fsdp", "seq", None), P("fsdp", None), P("fsdp", None), P(), P()),
        out_specs=P("fsdp", "seq", None),
        check_vma=False,
    )
```

```python
import jax
import jax.numpy as jnp
from jax import lax
from jax.experimental import pallas as pl
from jax.experimental.pallas import tpu as pltpu
from jax.sharding import PartitionSpec as P

E = 64
LANES = 128
CORES = 2
NEG = -1e30
ROWS = 192
BLOCK = 256
GRAIN = 64
COST1 = 1_000_000_000
COST = 1_000_000_000

VMEM = pl.BlockSpec(memory_space=pltpu.VMEM)
SMEM = pl.BlockSpec(memory_space=pltpu.SMEM)
HBM = pl.BlockSpec(memory_space=pltpu.HBM)


def grid_of(fsdp_count):
    x_count = 1
    while (2 * x_count) ** 2 <= fsdp_count and fsdp_count % (2 * x_count) == 0:
        x_count *= 2
    return fsdp_count // x_count, x_count


def rotation(z_count, x_count, z_step, x_step):
    return [
        (z * x_count + x, (z + z_step) % z_count * x_count + (x + x_step) % x_count)
        for z in range(z_count)
        for x in range(x_count)
    ]


def core_swap(array, seq_count):
    return lax.ppermute(array, "seq", [(s, s ^ 1) for s in range(seq_count)])


def y_rotation(array, seq_count, step):
    return lax.ppermute(array, "seq", [(s, (s + CORES * step) % seq_count) for s in range(seq_count)])


def call(kernel, name, in_specs, out_shapes, out_specs=None, scratch_shapes=(), cost=0, aliases={}):
    out_specs = [VMEM] * len(out_shapes) if out_specs is None else out_specs
    shapes = [
        pltpu.VMEM(shape.shape, shape.dtype) if spec is VMEM else shape for shape, spec in zip(out_shapes, out_specs)
    ]
    inner = pl.pallas_call(
        kernel,
        out_shape=shapes,
        in_specs=in_specs,
        out_specs=out_specs,
        scratch_shapes=scratch_shapes,
        input_output_aliases=aliases,
        cost_estimate=pl.CostEstimate(flops=cost, bytes_accessed=0, transcendentals=0) if cost else None,
        compiler_params=pltpu.CompilerParams(vmem_limit_bytes=24 << 20),
        name=name,
    )

    def run(*args):
        return inner(
            *[
                pltpu.with_memory_space_constraint(arg, pltpu.HBM if spec is SMEM else spec.memory_space)
                for arg, spec in zip(args, in_specs)
            ]
        )

    return run


def shaped(shape, dtype):
    return jax.ShapeDtypeStruct(shape, dtype)


def strips(width, columns):
    strip = min(width, columns)
    return [(start, strip) for start in range(0, width, strip)]


def halves(qkv_weight, out_weight):
    rows, columns = qkv_weight.shape
    head_columns = columns // 3
    own = head_columns // CORES
    out_rows, width = out_weight.shape
    side = width // CORES
    pieces = strips(side, 3 * own)

    def kernel(qkv_ref, out_ref, half_ref, packed_ref, sems):
        core = lax.rem(lax.axis_index("seq"), CORES)
        copies = []

        def copy(source, target):
            copies.append(pltpu.make_async_copy(source, target, sems.at[len(copies)]))
            copies[-1].start()

        for part in range(3):
            source = qkv_ref.at[:, pl.ds(pl.multiple_of(part * head_columns + core * own, LANES), own)]
            lanes = slice(part * own, (part + 1) * own)
            copy(source, half_ref.at[:, lanes])
            copy(source, packed_ref.at[:rows, lanes])
        for piece, (start, strip) in enumerate(pieces):
            first = rows + piece * out_rows
            copy(
                out_ref.at[:, pl.ds(pl.multiple_of(core * side + start, LANES), strip)],
                packed_ref.at[first : first + out_rows, :strip],
            )
        for each in copies:
            each.wait()

    return call(
        kernel,
        "halves",
        [HBM, HBM],
        [
            shaped((rows, 3 * own), qkv_weight.dtype),
            shaped((rows + len(pieces) * out_rows, 3 * own), qkv_weight.dtype),
        ],
        scratch_shapes=[pltpu.SemaphoreType.DMA((6 + len(pieces),))],
    )(qkv_weight, out_weight)


def collect(blocks, x_count, z_count, rows, out_rows, side):
    pieces = strips(side, blocks[0][0].shape[1])
    flat = [(half, step) for half in range(len(blocks)) for step in range(x_count)]

    def kernel(*refs):
        fsdp_index = lax.axis_index("fsdp")
        x_index = lax.rem(fsdp_index, x_count)
        bit = lax.rem(fsdp_index // (x_count * (z_count // 2)), 2)
        for (half, step), ref in zip(flat, refs):
            place = (1 - bit if half else bit) * x_count + lax.rem(x_index + x_count - step, x_count)
            for piece, (start, strip) in enumerate(pieces):
                first = rows + piece * out_rows
                refs[-1][pl.ds(pl.multiple_of(place * out_rows, 16), out_rows), start : start + strip] = ref[
                    first : first + out_rows, :strip
                ]

    return call(
        kernel, "collect", [VMEM] * len(flat), [shaped((len(flat) * out_rows, side), blocks[0][0].dtype)]
    )(*[blocks[half][step] for half, step in flat])[0]


def pair_up(own, got, units, shift, x_count):
    rows, columns = own.shape
    each = rows // units

    def kernel(own_ref, got_ref, pair_ref):
        bit = lax.rem(lax.axis_index("fsdp") // (x_count * shift), 2)
        for unit in range(units):
            piece = slice(unit * each, (unit + 1) * each)
            pair_ref[pl.ds(pl.multiple_of((2 * unit + bit) * each, 16), each), :] = own_ref[piece, :]
            pair_ref[pl.ds(pl.multiple_of((2 * unit + 1 - bit) * each, 16), each), :] = got_ref[piece, :]

    return call(kernel, "pair_up", [VMEM, VMEM], [shaped((2 * rows, columns), own.dtype)])(own, got)[0]


def lane_pick(per_head):
    lane = lax.broadcasted_iota(jnp.int32, (1, LANES), 1)
    picked = per_head[0]
    for head in range(1, len(per_head)):
        picked = jnp.where(lane >= head * E, per_head[head], picked)
    return jnp.broadcast_to(picked, (picked.shape[0], LANES))


def attend_part(queries, keys, values, bias):
    lane = lax.broadcasted_iota(jnp.int32, (1, LANES), 1)
    rows = queries.shape[0]
    heads = LANES // E
    zero = jnp.zeros_like(queries)
    stacked = jnp.concatenate(
        [jnp.where((lane >= head * E) & (lane < (head + 1) * E), queries, zero) for head in range(heads)], axis=0
    )
    scores = lax.dot_general(stacked, keys, (((1,), (1,)), ((), ())), preferred_element_type=jnp.float32) + bias
    row_max = jnp.max(scores, axis=1, keepdims=True)
    numerators = jnp.exp(scores - row_max).astype(values.dtype)
    summed = jnp.dot(numerators, values, preferred_element_type=jnp.float32)

    def pick(array):
        return lane_pick([array[head * rows : (head + 1) * rows] for head in range(heads)])

    return pick(row_max), pick(summed[:, LANES:]), pick(summed[:, :LANES])


def merge(old, new):
    top = jnp.maximum(old[0], new[0])
    keep = jnp.exp(old[0] - top)
    add = jnp.exp(new[0] - top)
    return top, old[1] * keep + new[1] * add, old[2] * keep + new[2] * add


def project(z_count, x_count, shifts, blocks, latents_own, latents_other):
    count = len(blocks)
    columns = blocks[0].shape[1]
    own = columns // 3
    row_count, depth = latents_own.shape
    rows = depth // count
    dtype = latents_own.dtype
    scale = float(E) ** -0.5

    def kernel(own_ref, other_ref, *refs):
        block_refs = refs[:count]
        queries_ref, weight_ref, key_value_ref, latents_ref, sem = refs[count:]
        fetch = pltpu.make_async_copy(own_ref, latents_ref, sem)
        fetch.start()
        fsdp_index = lax.axis_index("fsdp")
        z_index = fsdp_index // x_count
        x_index = lax.rem(fsdp_index, x_count)
        for (dz, dx), block_ref in zip(shifts, block_refs):
            place = lax.rem(z_index + z_count - dz, z_count) * x_count + lax.rem(x_index + x_count - dx, x_count)
            weight_ref[pl.ds(pl.multiple_of(place * rows, 16), rows), :] = block_ref[:rows, :]
        for member, from_ref in ((1, other_ref), (0, latents_ref)):
            if member == 0:
                fetch.wait()
            projected = jnp.dot(from_ref[...], weight_ref[...], preferred_element_type=jnp.float32).astype(dtype)
            queries_ref[member] = projected[:, :own] * jnp.asarray(scale, dtype)
            key_value_ref[member * row_count : (member + 1) * row_count, :] = projected[:, own:]

    return call(
        kernel,
        "project",
        [HBM] + [VMEM] * (count + 1),
        [
            shaped((CORES, row_count, own), dtype),
            shaped((depth, columns), dtype),
            shaped((CORES * row_count, 2 * own), dtype),
        ],
        scratch_shapes=[pltpu.VMEM((row_count, depth), dtype), pltpu.SemaphoreType.DMA(())],
        cost=COST1,
    )(latents_own, latents_other, *blocks)


def attend(seq_count, sources, key_value, state, last, weight, queries, tile_mask, tile_counts):
    columns = weight.shape[1]
    own = columns // 3
    row_count = queries.shape[1]
    dtype = queries.dtype
    groups = own // LANES
    local_rows = 0 if key_value is None else CORES * row_count
    slots = local_rows + len(sources) * row_count
    given = [weight, queries] + [latents for latents, _, _ in sources]
    given += [array for array in (key_value, state) if array is not None]

    def kernel(mask_ref, count_ref, weight_ref, queries_ref, *refs):
        latents_refs, refs = refs[: len(sources)], list(refs[len(sources) :])
        key_value_ref = None if key_value is None else refs.pop(0)
        old_ref = None if state is None else refs.pop(0)
        values_ref, keys_ref = refs.pop(), refs.pop()
        seq_index = lax.axis_index("seq")
        core = lax.rem(seq_index, CORES)
        chip_tile = seq_index - core
        tiles = [chip_tile + core, chip_tile + 1 - core]
        ends = [jnp.int32(0)]
        spans = []

        def place(key_tile, keys, values):
            rows = pl.ds(pl.multiple_of(ends[-1], GRAIN), keys.shape[0])
            keys_ref[rows, :] = keys
            for group in range(groups):
                first = 2 * group * LANES
                values_ref[rows, first : first + LANES] = values[:, group * LANES : (group + 1) * LANES]
            spans.append((key_tile, ends[-1]))
            ends.append(ends[-1] + count_ref[key_tile])

        for member in range(CORES if local_rows else 0):
            rows = slice(member * row_count, (member + 1) * row_count)
            place(tiles[member], key_value_ref[rows, :own], key_value_ref[rows, own:])
        for part, (_, y_step, swapped) in enumerate(sources):
            projected = jnp.dot(
                latents_refs[part][...], weight_ref[:, own:], preferred_element_type=jnp.float32
            ).astype(dtype)
            from_same = lax.rem(seq_index + seq_count - CORES * y_step, seq_count)
            place(from_same + 1 - 2 * core if swapped else from_same, projected[:, :own], projected[:, own:])
        rest = pl.ds(pl.multiple_of(spans[-1][1] + row_count, GRAIN), BLOCK)
        keys_ref[rest, :] = jnp.zeros((BLOCK, own), dtype)
        values_ref[rest, :] = jnp.zeros((BLOCK, 2 * own), dtype)
        for group in range(groups):
            first = (2 * group + 1) * LANES
            values_ref[:, first : first + LANES] = jnp.ones((slots + BLOCK, LANES), dtype)

        def over(keys_taken):
            slot = lax.broadcasted_iota(jnp.int32, (1, keys_taken), 1)
            for member in range(CORES):
                bias = jnp.full((1, keys_taken), NEG, jnp.float32)
                for key_tile, start in spans:
                    end = start + jnp.where(mask_ref[tiles[member], key_tile] > 0, count_ref[key_tile], 0)
                    bias = jnp.where((slot >= start) & (slot < end), 0.0, bias)
                for group in range(groups):
                    lanes = slice(group * LANES, (group + 1) * LANES)
                    for start in range(0, row_count, ROWS):
                        chunk = slice(start, start + ROWS)
                        parts = attend_part(
                            queries_ref[member, chunk, lanes],
                            keys_ref[:keys_taken, lanes],
                            values_ref[:keys_taken, 2 * group * LANES : 2 * (group + 1) * LANES],
                            bias,
                        )
                        if old_ref is not None:
                            parts = merge([old_ref[member, which, chunk, lanes] for which in range(3)], parts)
                        if last:
                            position = start + lax.broadcasted_iota(jnp.int32, (ROWS, 1), 0)
                            attended = jnp.where(position < count_ref[tiles[member]], parts[2] / parts[1], 0.0)
                            refs[member][chunk, lanes] = attended.astype(dtype)
                        else:
                            for which, part in enumerate(parts):
                                refs[0][member, which, chunk, lanes] = part

        blocks = (ends[-1] + BLOCK - 1) // BLOCK
        fewest, most = max(slots // (2 * BLOCK), 1), slots // BLOCK
        for taken in range(fewest, most + 1):
            fits = blocks <= taken if taken == fewest else blocks == taken
            pl.when(fits)(lambda taken=taken: over(taken * BLOCK))

    if last:
        out_shapes = [shaped((row_count, own), dtype)] * CORES
    else:
        out_shapes = [shaped((CORES, 3, row_count, own), jnp.float32)]
    return call(
        kernel,
        "attend_last" if last else "attend",
        [SMEM, SMEM] + [VMEM] * len(given),
        out_shapes,
        scratch_shapes=[pltpu.VMEM((slots + BLOCK, own), dtype), pltpu.VMEM((slots + BLOCK, 2 * own), dtype)],
        cost=COST,
    )(tile_mask, tile_counts, *given)


def project_out(attended_own, attended_partner, out_own, out_partner):
    row_count, own = attended_own.shape
    side = out_own.shape[1]
    dtype = attended_own.dtype

    def kernel(own_ref, partner_ref, out_own_ref, out_partner_ref, result_ref, staged_ref, sems):
        core = lax.rem(lax.axis_index("seq"), CORES)
        own_rows = pl.ds(pl.multiple_of(core * own, 16), own)
        partner_rows = pl.ds(pl.multiple_of((1 - core) * own, 16), own)
        copies = []
        for half, weight_ref in enumerate((out_own_ref, out_partner_ref)):
            total = jnp.dot(own_ref[...], weight_ref[own_rows, :], preferred_element_type=jnp.float32)
            total += jnp.dot(partner_ref[...], weight_ref[partner_rows, :], preferred_element_type=jnp.float32)
            staged_ref[half] = total.astype(dtype)
            start = pl.multiple_of((core if half == 0 else 1 - core) * side, LANES)
            copies.append(
                pltpu.make_async_copy(staged_ref.at[half], result_ref.at[:, pl.ds(start, side)], sems.at[half])
            )
            copies[-1].start()
        for copy in copies:
            copy.wait()

    return call(
        kernel,
        "project_out",
        [VMEM] * 4,
        [shaped((row_count, CORES * side), dtype)],
        [HBM],
        scratch_shapes=[pltpu.VMEM((CORES, row_count, side), dtype), pltpu.SemaphoreType.DMA((CORES,))],
    )(attended_own, attended_partner, out_own, out_partner)[0]


def after(array, *others):
    return lax.optimization_barrier((array, *others))[0]


def local(latents, qkv_weight, out_weight, tile_mask, tile_counts):
    seq_count = lax.axis_size("seq")
    fsdp_count = lax.axis_size("fsdp")
    z_count, x_count = grid_of(fsdp_count)
    chips = seq_count // CORES
    latents_own = latents[0]

    def hop(array, z_step, x_step):
        return lax.ppermute(array, "fsdp", rotation(z_count, x_count, z_step, x_step))

    def flip(array, shift):
        return lax.ppermute(array, "fsdp", [(f, f ^ (shift * x_count)) for f in range(fsdp_count)])

    along_y = [y_rotation(latents_own, seq_count, step) for step in range(1, chips)]
    latents_other = core_swap(latents_own, seq_count)
    half, packed = halves(qkv_weight, out_weight)

    came = {(0, 0): half}
    for x_step in range(1, x_count):
        came[0, x_step] = hop(after(packed, latents_other), 0, x_step)
    beside = [came[0, x_step] for x_step in range(1, x_count)]
    turn = z_count // 2
    for z_step in (turn, 1):
        came[z_step, 0] = hop(packed if z_step == turn else half, z_step, 0)
    second = after(half, came[1, 0], *beside)
    third = after(half, came[turn, 0])
    for x_step in range(1, x_count):
        came[turn, x_step] = hop(came[turn, 0], 0, x_step)
        came[1, x_step] = hop(second, 1, x_step)
    for z_step in range(2, z_count):
        if z_step != turn:
            came[z_step, 0] = hop(second, z_step, 0)
            for x_step in range(1, x_count):
                came[z_step, x_step] = hop(third, z_step, x_step)

    out_own = collect(
        [[packed] + beside, [came[turn, x_step] for x_step in range(x_count)]],
        x_count,
        z_count,
        half.shape[0],
        out_weight.shape[0],
        out_weight.shape[1] // CORES,
    )
    units, shift = 2, turn // 2
    while shift > 1:
        out_own = pair_up(out_own, flip(out_own, shift), units, shift, x_count)
        units, shift = 2 * units, shift // 2
    out_got = flip(out_own, shift)

    near = after(along_y, out_own, *list(came.values())[1:])
    far = [core_swap(array, seq_count) for array in near]
    came[0, 0] = after(half, *near)
    queries, weight, key_value = project(
        z_count, x_count, list(came), list(came.values()), latents_own, latents_other
    )
    state = None
    for step in range(1, chips):
        last = step == chips - 1
        result = attend(
            seq_count,
            [(near[step - 1], step, False), (far[step - 1], step, True)],
            key_value if step == 1 else None,
            state,
            last,
            weight,
            queries,
            tile_mask,
            tile_counts,
        )
        state = None if last else result[0]
    attended_own, attended_other = result
    attended_partner = core_swap(attended_other, seq_count)
    out_own = pair_up(out_own, after(out_got, attended_other), units, shift, x_count)
    out_partner = core_swap(out_own, seq_count)
    return project_out(attended_own, attended_partner, out_own, out_partner)[None]


def solution(mesh):
    return jax.shard_map(
        local,
        mesh=mesh,
        in_specs=(P("fsdp", "seq", None), P("fsdp", None), P("fsdp", None), P(), P()),
        out_specs=P("fsdp", "seq", None),
        check_vma=False,
    )
```

```python
import jax
import jax.numpy as jnp
from jax import lax
from jax.experimental import pallas as pl
from jax.experimental.pallas import tpu as pltpu
from jax.sharding import PartitionSpec as P

E = 64
LANES = 128
CORES = 2
NEG = -1e30
ROWS = 192
BLOCK = 256
GRAIN = 64
COST1 = 1_000_000_000
COST = 1_000_000_000

VMEM = pl.BlockSpec(memory_space=pltpu.VMEM)
SMEM = pl.BlockSpec(memory_space=pltpu.SMEM)
HBM = pl.BlockSpec(memory_space=pltpu.HBM)


def grid_of(fsdp_count):
    x_count = 1
    while (2 * x_count) ** 2 <= fsdp_count and fsdp_count % (2 * x_count) == 0:
        x_count *= 2
    return fsdp_count // x_count, x_count


def rotation(z_count, x_count, z_step, x_step):
    return [
        (z * x_count + x, (z + z_step) % z_count * x_count + (x + x_step) % x_count)
        for z in range(z_count)
        for x in range(x_count)
    ]


def core_swap(array, seq_count):
    return lax.ppermute(array, "seq", [(s, s ^ 1) for s in range(seq_count)])


def y_rotation(array, seq_count, step):
    return lax.ppermute(array, "seq", [(s, (s + CORES * step) % seq_count) for s in range(seq_count)])


def call(kernel, name, in_specs, out_shapes, out_specs=None, scratch_shapes=(), cost=0, aliases={}):
    out_specs = [VMEM] * len(out_shapes) if out_specs is None else out_specs
    shapes = [
        pltpu.VMEM(shape.shape, shape.dtype) if spec is VMEM else shape for shape, spec in zip(out_shapes, out_specs)
    ]
    inner = pl.pallas_call(
        kernel,
        out_shape=shapes,
        in_specs=in_specs,
        out_specs=out_specs,
        scratch_shapes=scratch_shapes,
        input_output_aliases=aliases,
        cost_estimate=pl.CostEstimate(flops=cost, bytes_accessed=0, transcendentals=0) if cost else None,
        compiler_params=pltpu.CompilerParams(vmem_limit_bytes=24 << 20),
        name=name,
    )

    def run(*args):
        return inner(
            *[
                pltpu.with_memory_space_constraint(arg, pltpu.HBM if spec is SMEM else spec.memory_space)
                for arg, spec in zip(args, in_specs)
            ]
        )

    return run


def shaped(shape, dtype):
    return jax.ShapeDtypeStruct(shape, dtype)


def strips(width, columns):
    strip = min(width, columns)
    return [(start, strip) for start in range(0, width, strip)]


def halves(qkv_weight, out_weight):
    rows, columns = qkv_weight.shape
    head_columns = columns // 3
    own = head_columns // CORES
    out_rows, width = out_weight.shape
    side = width // CORES
    pieces = strips(side, 3 * own)

    def kernel(qkv_ref, out_ref, half_ref, packed_ref, sems):
        core = lax.rem(lax.axis_index("seq"), CORES)
        copies = []

        def copy(source, target):
            copies.append(pltpu.make_async_copy(source, target, sems.at[len(copies)]))
            copies[-1].start()

        for part in range(3):
            source = qkv_ref.at[:, pl.ds(pl.multiple_of(part * head_columns + core * own, LANES), own)]
            lanes = slice(part * own, (part + 1) * own)
            copy(source, half_ref.at[:, lanes])
            copy(source, packed_ref.at[:rows, lanes])
        for piece, (start, strip) in enumerate(pieces):
            first = rows + piece * out_rows
            copy(
                out_ref.at[:, pl.ds(pl.multiple_of(core * side + start, LANES), strip)],
                packed_ref.at[first : first + out_rows, :strip],
            )
        for each in copies:
            each.wait()

    return call(
        kernel,
        "halves",
        [HBM, HBM],
        [
            shaped((rows, 3 * own), qkv_weight.dtype),
            shaped((rows + len(pieces) * out_rows, 3 * own), qkv_weight.dtype),
        ],
        scratch_shapes=[pltpu.SemaphoreType.DMA((6 + len(pieces),))],
    )(qkv_weight, out_weight)


def collect(blocks, x_count, z_count, rows, out_rows, side):
    pieces = strips(side, blocks[0][0].shape[1])
    flat = [(half, step) for half in range(len(blocks)) for step in range(x_count)]

    def kernel(*refs):
        fsdp_index = lax.axis_index("fsdp")
        x_index = lax.rem(fsdp_index, x_count)
        bit = lax.rem(fsdp_index // (x_count * (z_count // 2)), 2)
        for (half, step), ref in zip(flat, refs):
            place = (1 - bit if half else bit) * x_count + lax.rem(x_index + x_count - step, x_count)
            for piece, (start, strip) in enumerate(pieces):
                first = rows + piece * out_rows
                refs[-1][pl.ds(pl.multiple_of(place * out_rows, 16), out_rows), start : start + strip] = ref[
                    first : first + out_rows, :strip
                ]

    return call(
        kernel, "collect", [VMEM] * len(flat), [shaped((len(flat) * out_rows, side), blocks[0][0].dtype)]
    )(*[blocks[half][step] for half, step in flat])[0]


def pair_up(own, got, units, shift, x_count):
    rows, columns = own.shape
    each = rows // units

    def kernel(own_ref, got_ref, pair_ref):
        bit = lax.rem(lax.axis_index("fsdp") // (x_count * shift), 2)
        for unit in range(units):
            piece = slice(unit * each, (unit + 1) * each)
            pair_ref[pl.ds(pl.multiple_of((2 * unit + bit) * each, 16), each), :] = own_ref[piece, :]
            pair_ref[pl.ds(pl.multiple_of((2 * unit + 1 - bit) * each, 16), each), :] = got_ref[piece, :]

    return call(kernel, "pair_up", [VMEM, VMEM], [shaped((2 * rows, columns), own.dtype)])(own, got)[0]


def lane_pick(per_head):
    lane = lax.broadcasted_iota(jnp.int32, (1, LANES), 1)
    picked = per_head[0]
    for head in range(1, len(per_head)):
        picked = jnp.where(lane >= head * E, per_head[head], picked)
    return jnp.broadcast_to(picked, (picked.shape[0], LANES))


def attend_part(queries, keys, values, bias):
    lane = lax.broadcasted_iota(jnp.int32, (1, LANES), 1)
    rows = queries.shape[0]
    heads = LANES // E
    zero = jnp.zeros_like(queries)
    stacked = jnp.concatenate(
        [jnp.where((lane >= head * E) & (lane < (head + 1) * E), queries, zero) for head in range(heads)], axis=0
    )
    scores = lax.dot_general(stacked, keys, (((1,), (1,)), ((), ())), preferred_element_type=jnp.float32) + bias
    row_max = jnp.max(scores, axis=1, keepdims=True)
    numerators = jnp.exp(scores - row_max).astype(values.dtype)
    summed = jnp.dot(numerators, values, preferred_element_type=jnp.float32)

    def pick(array):
        return lane_pick([array[head * rows : (head + 1) * rows] for head in range(heads)])

    return pick(row_max), pick(summed[:, LANES:]), pick(summed[:, :LANES])


def merge(old, new):
    top = jnp.maximum(old[0], new[0])
    keep = jnp.exp(old[0] - top)
    add = jnp.exp(new[0] - top)
    return top, old[1] * keep + new[1] * add, old[2] * keep + new[2] * add


def project(z_count, x_count, shifts, blocks, latents_own, latents_other, early=None):
    count = len(blocks)
    columns = blocks[0].shape[1]
    own = columns // 3
    row_count, depth = latents_own.shape
    rows = depth // (z_count * x_count)
    band = x_count * rows
    steps = sorted({dz for dz, _ in shifts})
    dtype = latents_own.dtype
    scale = float(E) ** -0.5

    def assemble(block_refs, weight_ref):
        fsdp_index = lax.axis_index("fsdp")
        z_index = fsdp_index // x_count
        x_index = lax.rem(fsdp_index, x_count)
        for (dz, dx), block_ref in zip(shifts, block_refs):
            place = lax.rem(z_index + z_count - dz, z_count) * x_count + lax.rem(x_index + x_count - dx, x_count)
            weight_ref[pl.ds(pl.multiple_of(place * rows, 16), rows), :] = block_ref[:rows, :]
        starts = [pl.multiple_of(lax.rem(z_index + z_count - dz, z_count) * band, LANES) for dz in steps]
        return starts, jnp.concatenate([weight_ref[pl.ds(start, band), :] for start in starts], axis=0)

    def partial(latents_ref, starts, weight):
        latents = jnp.concatenate([latents_ref[:, pl.ds(start, band)] for start in starts], axis=1)
        return jnp.dot(latents, weight, preferred_element_type=jnp.float32)

    def first(own_ref, other_ref, *refs):
        block_refs = refs[:count]
        latents_ref, weight_ref, total_ref, sem = refs[count:]
        fetch = pltpu.make_async_copy(own_ref, latents_ref, sem)
        fetch.start()
        starts, weight = assemble(block_refs, weight_ref)
        total_ref[1] = partial(other_ref, starts, weight)
        fetch.wait()
        total_ref[0] = partial(latents_ref, starts, weight)

    def rest(own_ref, other_ref, old_weight_ref, total_ref, *refs):
        block_refs = refs[:count]
        queries_ref, weight_ref, key_value_ref = refs[count:]
        starts, weight = assemble(block_refs, weight_ref)
        for member, from_ref in enumerate((own_ref, other_ref)):
            projected = (total_ref[member] + partial(from_ref, starts, weight)).astype(dtype)
            queries_ref[member] = projected[:, :own] * jnp.asarray(scale, dtype)
            key_value_ref[member * row_count : (member + 1) * row_count, :] = projected[:, own:]

    weight_shape = shaped((depth, columns), dtype)
    if early is None:
        return call(
            first,
            "project_first",
            [HBM] + [VMEM] * (count + 1),
            [shaped((row_count, depth), dtype), weight_shape, shaped((CORES, row_count, columns), jnp.float32)],
            scratch_shapes=[pltpu.SemaphoreType.DMA(())],
            cost=COST1,
        )(latents_own, latents_other, *blocks)
    own_tile, weight, total = early
    return call(
        rest,
        "project",
        [VMEM] * (count + 4),
        [
            shaped((CORES, row_count, own), dtype),
            weight_shape,
            shaped((CORES * row_count, 2 * own), dtype),
        ],
        cost=COST1,
        aliases={2: 1},
    )(own_tile, latents_other, weight, total, *blocks)


def project_whole(z_count, x_count, shifts, blocks, latents_own, latents_other):
    count = len(blocks)
    columns = blocks[0].shape[1]
    own = columns // 3
    row_count, depth = latents_own.shape
    rows = depth // count
    dtype = latents_own.dtype
    scale = float(E) ** -0.5

    def kernel(own_ref, other_ref, *refs):
        block_refs = refs[:count]
        queries_ref, weight_ref, key_value_ref, latents_ref, sem = refs[count:]
        fetch = pltpu.make_async_copy(own_ref, latents_ref, sem)
        fetch.start()
        fsdp_index = lax.axis_index("fsdp")
        z_index = fsdp_index // x_count
        x_index = lax.rem(fsdp_index, x_count)
        for (dz, dx), block_ref in zip(shifts, block_refs):
            place = lax.rem(z_index + z_count - dz, z_count) * x_count + lax.rem(x_index + x_count - dx, x_count)
            weight_ref[pl.ds(pl.multiple_of(place * rows, 16), rows), :] = block_ref[:rows, :]
        for member, from_ref in ((1, other_ref), (0, latents_ref)):
            if member == 0:
                fetch.wait()
            projected = jnp.dot(from_ref[...], weight_ref[...], preferred_element_type=jnp.float32).astype(dtype)
            queries_ref[member] = projected[:, :own] * jnp.asarray(scale, dtype)
            key_value_ref[member * row_count : (member + 1) * row_count, :] = projected[:, own:]

    return call(
        kernel,
        "project",
        [HBM] + [VMEM] * (count + 1),
        [
            shaped((CORES, row_count, own), dtype),
            shaped((depth, columns), dtype),
            shaped((CORES * row_count, 2 * own), dtype),
        ],
        scratch_shapes=[pltpu.VMEM((row_count, depth), dtype), pltpu.SemaphoreType.DMA(())],
        cost=COST1,
    )(latents_own, latents_other, *blocks)


def attend(seq_count, sources, key_value, state, last, weight, queries, tile_mask, tile_counts):
    columns = weight.shape[1]
    own = columns // 3
    row_count = queries.shape[1]
    dtype = queries.dtype
    groups = own // LANES
    local_rows = 0 if key_value is None else CORES * row_count
    slots = local_rows + len(sources) * row_count
    given = [weight, queries] + [latents for latents, _, _ in sources]
    given += [array for array in (key_value, state) if array is not None]

    def kernel(mask_ref, count_ref, weight_ref, queries_ref, *refs):
        latents_refs, refs = refs[: len(sources)], list(refs[len(sources) :])
        key_value_ref = None if key_value is None else refs.pop(0)
        old_ref = None if state is None else refs.pop(0)
        values_ref, keys_ref = refs.pop(), refs.pop()
        seq_index = lax.axis_index("seq")
        core = lax.rem(seq_index, CORES)
        chip_tile = seq_index - core
        tiles = [chip_tile + core, chip_tile + 1 - core]
        ends = [jnp.int32(0)]
        spans = []

        def place(key_tile, keys, values):
            rows = pl.ds(pl.multiple_of(ends[-1], GRAIN), keys.shape[0])
            keys_ref[rows, :] = keys
            for group in range(groups):
                first = 2 * group * LANES
                values_ref[rows, first : first + LANES] = values[:, group * LANES : (group + 1) * LANES]
            spans.append((key_tile, ends[-1]))
            ends.append(ends[-1] + count_ref[key_tile])

        for member in range(CORES if local_rows else 0):
            rows = slice(member * row_count, (member + 1) * row_count)
            place(tiles[member], key_value_ref[rows, :own], key_value_ref[rows, own:])
        for part, (_, y_step, swapped) in enumerate(sources):
            projected = jnp.dot(
                latents_refs[part][...], weight_ref[:, own:], preferred_element_type=jnp.float32
            ).astype(dtype)
            from_same = lax.rem(seq_index + seq_count - CORES * y_step, seq_count)
            place(from_same + 1 - 2 * core if swapped else from_same, projected[:, :own], projected[:, own:])
        rest = pl.ds(pl.multiple_of(spans[-1][1] + row_count, GRAIN), BLOCK)
        keys_ref[rest, :] = jnp.zeros((BLOCK, own), dtype)
        values_ref[rest, :] = jnp.zeros((BLOCK, 2 * own), dtype)
        for group in range(groups):
            first = (2 * group + 1) * LANES
            values_ref[:, first : first + LANES] = jnp.ones((slots + BLOCK, LANES), dtype)

        def over(keys_taken):
            slot = lax.broadcasted_iota(jnp.int32, (1, keys_taken), 1)
            for member in range(CORES):
                bias = jnp.full((1, keys_taken), NEG, jnp.float32)
                for key_tile, start in spans:
                    end = start + jnp.where(mask_ref[tiles[member], key_tile] > 0, count_ref[key_tile], 0)
                    bias = jnp.where((slot >= start) & (slot < end), 0.0, bias)
                for group in range(groups):
                    lanes = slice(group * LANES, (group + 1) * LANES)
                    for start in range(0, row_count, ROWS):
                        chunk = slice(start, start + ROWS)
                        parts = attend_part(
                            queries_ref[member, chunk, lanes],
                            keys_ref[:keys_taken, lanes],
                            values_ref[:keys_taken, 2 * group * LANES : 2 * (group + 1) * LANES],
                            bias,
                        )
                        if old_ref is not None:
                            parts = merge([old_ref[member, which, chunk, lanes] for which in range(3)], parts)
                        if last:
                            position = start + lax.broadcasted_iota(jnp.int32, (ROWS, 1), 0)
                            attended = jnp.where(position < count_ref[tiles[member]], parts[2] / parts[1], 0.0)
                            refs[member][chunk, lanes] = attended.astype(dtype)
                        else:
                            for which, part in enumerate(parts):
                                refs[0][member, which, chunk, lanes] = part

        blocks = (ends[-1] + BLOCK - 1) // BLOCK
        fewest, most = max(slots // (2 * BLOCK), 1), slots // BLOCK
        for taken in range(fewest, most + 1):
            fits = blocks <= taken if taken == fewest else blocks == taken
            pl.when(fits)(lambda taken=taken: over(taken * BLOCK))

    if last:
        out_shapes = [shaped((row_count, own), dtype)] * CORES
    else:
        out_shapes = [shaped((CORES, 3, row_count, own), jnp.float32)]
    return call(
        kernel,
        "attend_last" if last else "attend",
        [SMEM, SMEM] + [VMEM] * len(given),
        out_shapes,
        scratch_shapes=[pltpu.VMEM((slots + BLOCK, own), dtype), pltpu.VMEM((slots + BLOCK, 2 * own), dtype)],
        cost=COST,
    )(tile_mask, tile_counts, *given)


def project_out(attended_own, attended_partner, out_own, out_partner):
    row_count, own = attended_own.shape
    side = out_own.shape[1]
    dtype = attended_own.dtype

    def kernel(own_ref, partner_ref, out_own_ref, out_partner_ref, result_ref, staged_ref, sems):
        core = lax.rem(lax.axis_index("seq"), CORES)
        own_rows = pl.ds(pl.multiple_of(core * own, 16), own)
        partner_rows = pl.ds(pl.multiple_of((1 - core) * own, 16), own)
        copies = []
        for half, weight_ref in enumerate((out_own_ref, out_partner_ref)):
            total = jnp.dot(own_ref[...], weight_ref[own_rows, :], preferred_element_type=jnp.float32)
            total += jnp.dot(partner_ref[...], weight_ref[partner_rows, :], preferred_element_type=jnp.float32)
            staged_ref[half] = total.astype(dtype)
            start = pl.multiple_of((core if half == 0 else 1 - core) * side, LANES)
            copies.append(
                pltpu.make_async_copy(staged_ref.at[half], result_ref.at[:, pl.ds(start, side)], sems.at[half])
            )
            copies[-1].start()
        for copy in copies:
            copy.wait()

    return call(
        kernel,
        "project_out",
        [VMEM] * 4,
        [shaped((row_count, CORES * side), dtype)],
        [HBM],
        scratch_shapes=[pltpu.VMEM((CORES, row_count, side), dtype), pltpu.SemaphoreType.DMA((CORES,))],
    )(attended_own, attended_partner, out_own, out_partner)[0]


def after(array, *others):
    return lax.optimization_barrier((array, *others))[0]


def local(latents, qkv_weight, out_weight, tile_mask, tile_counts):
    seq_count = lax.axis_size("seq")
    fsdp_count = lax.axis_size("fsdp")
    z_count, x_count = grid_of(fsdp_count)
    chips = seq_count // CORES
    latents_own = latents[0]

    def hop(array, z_step, x_step):
        return lax.ppermute(array, "fsdp", rotation(z_count, x_count, z_step, x_step))

    def flip(array, shift):
        return lax.ppermute(array, "fsdp", [(f, f ^ (shift * x_count)) for f in range(fsdp_count)])

    along_y = [y_rotation(latents_own, seq_count, step) for step in range(1, chips)]
    latents_other = core_swap(latents_own, seq_count)
    half, packed = halves(qkv_weight, out_weight)

    came = {(0, 0): half}
    for x_step in range(1, x_count):
        came[0, x_step] = hop(after(packed, latents_other), 0, x_step)
    beside = [came[0, x_step] for x_step in range(1, x_count)]
    turn = z_count // 2
    for z_step in (turn, 1):
        came[z_step, 0] = hop(packed if z_step == turn else half, z_step, 0)
    second = after(half, came[1, 0], *beside)
    third = after(half, came[turn, 0])
    for x_step in range(1, x_count):
        came[turn, x_step] = hop(came[turn, 0], 0, x_step)
        came[1, x_step] = hop(second, 1, x_step)
    for z_step in range(2, z_count):
        if z_step != turn:
            came[z_step, 0] = hop(second, z_step, 0)
            for x_step in range(1, x_count):
                came[z_step, x_step] = hop(third, z_step, x_step)

    axes = (z_count, x_count)
    early = None
    if x_count * half.shape[0] % LANES == 0:
        sooner = [shift for shift in came if shift[0] in (0, turn)]
        early = project(*axes, sooner, [came[shift] for shift in sooner], latents_own, latents_other)
        packed = after(packed, early[2])

    out_own = collect(
        [[packed] + beside, [came[turn, x_step] for x_step in range(x_count)]],
        x_count,
        z_count,
        half.shape[0],
        out_weight.shape[0],
        out_weight.shape[1] // CORES,
    )
    units, shift = 2, turn // 2
    while shift > 1:
        out_own = pair_up(out_own, flip(out_own, shift), units, shift, x_count)
        units, shift = 2 * units, shift // 2
    out_got = flip(out_own, shift)

    near = after(along_y, out_own, *list(came.values())[1:])
    far = [core_swap(array, seq_count) for array in near]
    if early is not None:
        later = [shift for shift in came if shift not in sooner]
        came[later[-1]] = after(came[later[-1]], *near)
        queries, weight, key_value = project(
            *axes, later, [came[shift] for shift in later], latents_own, latents_other, early
        )
    else:
        came[0, 0] = after(half, *near)
        queries, weight, key_value = project_whole(*axes, list(came), list(came.values()), latents_own, latents_other)
    state = None
    for step in range(1, chips):
        last = step == chips - 1
        result = attend(
            seq_count,
            [(near[step - 1], step, False), (far[step - 1], step, True)],
            key_value if step == 1 else None,
            state,
            last,
            weight,
            queries,
            tile_mask,
            tile_counts,
        )
        state = None if last else result[0]
    attended_own, attended_other = result
    attended_partner = core_swap(attended_other, seq_count)
    out_own = pair_up(out_own, after(out_got, attended_other), units, shift, x_count)
    out_partner = core_swap(out_own, seq_count)
    return project_out(attended_own, attended_partner, out_own, out_partner)[None]


def solution(mesh):
    return jax.shard_map(
        local,
        mesh=mesh,
        in_specs=(P("fsdp", "seq", None), P("fsdp", None), P("fsdp", None), P(), P()),
        out_specs=P("fsdp", "seq", None),
        check_vma=False,
    )
```

```python
import jax
import jax.numpy as jnp
from jax import lax
from jax.experimental import pallas as pl
from jax.experimental.pallas import tpu as pltpu
from jax.sharding import PartitionSpec as P

E = 64
LANES = 128
CORES = 2
NEG = -1e30
ROWS = 192
BLOCK = 256
GRAIN = 64
COST1 = 1_000_000_000
COST = 1_000_000_000

VMEM = pl.BlockSpec(memory_space=pltpu.VMEM)
SMEM = pl.BlockSpec(memory_space=pltpu.SMEM)
HBM = pl.BlockSpec(memory_space=pltpu.HBM)


def grid_of(fsdp_count):
    x_count = 1
    while (2 * x_count) ** 2 <= fsdp_count and fsdp_count % (2 * x_count) == 0:
        x_count *= 2
    return fsdp_count // x_count, x_count


def rotation(z_count, x_count, z_step, x_step):
    return [
        (z * x_count + x, (z + z_step) % z_count * x_count + (x + x_step) % x_count)
        for z in range(z_count)
        for x in range(x_count)
    ]


def core_swap(array, seq_count):
    return lax.ppermute(array, "seq", [(s, s ^ 1) for s in range(seq_count)])


def y_rotation(array, seq_count, step):
    return lax.ppermute(array, "seq", [(s, (s + CORES * step) % seq_count) for s in range(seq_count)])


def call(kernel, name, in_specs, out_shapes, out_specs=None, scratch_shapes=(), cost=0, aliases={}):
    out_specs = [VMEM] * len(out_shapes) if out_specs is None else out_specs
    shapes = [
        pltpu.VMEM(shape.shape, shape.dtype) if spec is VMEM else shape for shape, spec in zip(out_shapes, out_specs)
    ]
    inner = pl.pallas_call(
        kernel,
        out_shape=shapes,
        in_specs=in_specs,
        out_specs=out_specs,
        scratch_shapes=scratch_shapes,
        input_output_aliases=aliases,
        cost_estimate=pl.CostEstimate(flops=cost, bytes_accessed=0, transcendentals=0) if cost else None,
        compiler_params=pltpu.CompilerParams(vmem_limit_bytes=24 << 20),
        name=name,
    )

    def run(*args):
        return inner(
            *[
                pltpu.with_memory_space_constraint(arg, pltpu.HBM if spec is SMEM else spec.memory_space)
                for arg, spec in zip(args, in_specs)
            ]
        )

    return run


def shaped(shape, dtype):
    return jax.ShapeDtypeStruct(shape, dtype)


def strips(width, columns):
    strip = min(width, columns)
    return [(start, strip) for start in range(0, width, strip)]


def halves(qkv_weight, out_weight):
    rows, columns = qkv_weight.shape
    head_columns = columns // 3
    own = head_columns // CORES
    out_rows, width = out_weight.shape
    side = width // CORES
    pieces = strips(side, 3 * own)

    def kernel(qkv_ref, out_ref, half_ref, packed_ref, sems):
        core = lax.rem(lax.axis_index("seq"), CORES)
        copies = []

        def copy(source, target):
            copies.append(pltpu.make_async_copy(source, target, sems.at[len(copies)]))
            copies[-1].start()

        for part in range(3):
            source = qkv_ref.at[:, pl.ds(pl.multiple_of(part * head_columns + core * own, LANES), own)]
            lanes = slice(part * own, (part + 1) * own)
            copy(source, half_ref.at[:, lanes])
            copy(source, packed_ref.at[:rows, lanes])
        for piece, (start, strip) in enumerate(pieces):
            first = rows + piece * out_rows
            copy(
                out_ref.at[:, pl.ds(pl.multiple_of(core * side + start, LANES), strip)],
                packed_ref.at[first : first + out_rows, :strip],
            )
        for each in copies:
            each.wait()

    return call(
        kernel,
        "halves",
        [HBM, HBM],
        [
            shaped((rows, 3 * own), qkv_weight.dtype),
            shaped((rows + len(pieces) * out_rows, 3 * own), qkv_weight.dtype),
        ],
        scratch_shapes=[pltpu.SemaphoreType.DMA((6 + len(pieces),))],
    )(qkv_weight, out_weight)


def collect(blocks, x_count, z_count, rows, out_rows, side):
    pieces = strips(side, blocks[0][0].shape[1])
    flat = [(half, step) for half in range(len(blocks)) for step in range(x_count)]

    def kernel(*refs):
        fsdp_index = lax.axis_index("fsdp")
        x_index = lax.rem(fsdp_index, x_count)
        bit = lax.rem(fsdp_index // (x_count * (z_count // 2)), 2)
        for (half, step), ref in zip(flat, refs):
            place = (1 - bit if half else bit) * x_count + lax.rem(x_index + x_count - step, x_count)
            for piece, (start, strip) in enumerate(pieces):
                first = rows + piece * out_rows
                refs[-1][pl.ds(pl.multiple_of(place * out_rows, 16), out_rows), start : start + strip] = ref[
                    first : first + out_rows, :strip
                ]

    return call(
        kernel, "collect", [VMEM] * len(flat), [shaped((len(flat) * out_rows, side), blocks[0][0].dtype)]
    )(*[blocks[half][step] for half, step in flat])[0]


def pair_up(own, got, units, shift, x_count):
    rows, columns = own.shape
    each = rows // units

    def kernel(own_ref, got_ref, pair_ref):
        bit = lax.rem(lax.axis_index("fsdp") // (x_count * shift), 2)
        for unit in range(units):
            piece = slice(unit * each, (unit + 1) * each)
            pair_ref[pl.ds(pl.multiple_of((2 * unit + bit) * each, 16), each), :] = own_ref[piece, :]
            pair_ref[pl.ds(pl.multiple_of((2 * unit + 1 - bit) * each, 16), each), :] = got_ref[piece, :]

    return call(kernel, "pair_up", [VMEM, VMEM], [shaped((2 * rows, columns), own.dtype)])(own, got)[0]


def lane_pick(per_head):
    lane = lax.broadcasted_iota(jnp.int32, (1, LANES), 1)
    picked = per_head[0]
    for head in range(1, len(per_head)):
        picked = jnp.where(lane >= head * E, per_head[head], picked)
    return jnp.broadcast_to(picked, (picked.shape[0], LANES))


def attend_part(queries, keys, values, bias):
    lane = lax.broadcasted_iota(jnp.int32, (1, LANES), 1)
    rows = queries.shape[0]
    heads = LANES // E
    zero = jnp.zeros_like(queries)
    stacked = jnp.concatenate(
        [jnp.where((lane >= head * E) & (lane < (head + 1) * E), queries, zero) for head in range(heads)], axis=0
    )
    scores = lax.dot_general(stacked, keys, (((1,), (1,)), ((), ())), preferred_element_type=jnp.float32) + bias
    row_max = jnp.max(scores, axis=1, keepdims=True)
    numerators = jnp.exp(scores - row_max).astype(values.dtype)
    summed = jnp.dot(numerators, values, preferred_element_type=jnp.float32)

    def pick(array):
        return lane_pick([array[head * rows : (head + 1) * rows] for head in range(heads)])

    return pick(row_max), pick(summed[:, LANES:]), pick(summed[:, :LANES])


def merge(old, new):
    top = jnp.maximum(old[0], new[0])
    keep = jnp.exp(old[0] - top)
    add = jnp.exp(new[0] - top)
    return top, old[1] * keep + new[1] * add, old[2] * keep + new[2] * add


def project(z_count, x_count, shifts, blocks, latents_own, latents_other, near=None, early=None):
    count = len(blocks)
    columns = blocks[0].shape[1]
    own = columns // 3
    row_count, depth = latents_own.shape
    rows = depth // (z_count * x_count)
    band = x_count * rows
    steps = sorted({dz for dz, _ in shifts})
    dtype = latents_own.dtype
    scale = float(E) ** -0.5

    def assemble(block_refs, weight_ref):
        fsdp_index = lax.axis_index("fsdp")
        z_index = fsdp_index // x_count
        x_index = lax.rem(fsdp_index, x_count)
        for (dz, dx), block_ref in zip(shifts, block_refs):
            place = lax.rem(z_index + z_count - dz, z_count) * x_count + lax.rem(x_index + x_count - dx, x_count)
            weight_ref[pl.ds(pl.multiple_of(place * rows, 16), rows), :] = block_ref[:rows, :]
        starts = [pl.multiple_of(lax.rem(z_index + z_count - dz, z_count) * band, LANES) for dz in steps]
        return starts, jnp.concatenate([weight_ref[pl.ds(start, band), :] for start in starts], axis=0)

    def partial(latents_ref, starts, weight):
        latents = jnp.concatenate([latents_ref[:, pl.ds(start, band)] for start in starts], axis=1)
        return jnp.dot(latents, weight, preferred_element_type=jnp.float32)

    def first(own_ref, other_ref, *refs):
        block_refs = refs[:count]
        latents_ref, weight_ref, total_ref, sem = refs[count:]
        fetch = pltpu.make_async_copy(own_ref, latents_ref, sem)
        fetch.start()
        starts, weight = assemble(block_refs, weight_ref)
        total_ref[1] = partial(other_ref, starts, weight)
        fetch.wait()
        total_ref[0] = partial(latents_ref, starts, weight)

    def rest(own_ref, other_ref, old_weight_ref, total_ref, near_ref, *refs):
        block_refs = refs[:count]
        queries_ref, weight_ref, key_value_ref = refs[count:]
        starts, weight = assemble(block_refs, weight_ref)
        for member, from_ref in enumerate((own_ref, other_ref)):
            projected = (total_ref[member] + partial(from_ref, starts, weight)).astype(dtype)
            queries_ref[member] = projected[:, :own] * jnp.asarray(scale, dtype)
            key_value_ref[member * row_count : (member + 1) * row_count, :] = projected[:, own:]
        key_value_ref[CORES * row_count :, :] = jnp.dot(
            near_ref[...], weight_ref[:, own:], preferred_element_type=jnp.float32
        ).astype(dtype)

    weight_shape = shaped((depth, columns), dtype)
    if early is None:
        return call(
            first,
            "project_first",
            [HBM] + [VMEM] * (count + 1),
            [shaped((row_count, depth), dtype), weight_shape, shaped((CORES, row_count, columns), jnp.float32)],
            scratch_shapes=[pltpu.SemaphoreType.DMA(())],
            cost=COST1,
        )(latents_own, latents_other, *blocks)
    own_tile, weight, total = early
    return call(
        rest,
        "project",
        [VMEM] * (count + 5),
        [
            shaped((CORES, row_count, own), dtype),
            weight_shape,
            shaped(((CORES + 1) * row_count, 2 * own), dtype),
        ],
        cost=COST1,
        aliases={2: 1},
    )(own_tile, latents_other, weight, total, near, *blocks)


def project_whole(z_count, x_count, shifts, blocks, latents_own, latents_other, near):
    count = len(blocks)
    columns = blocks[0].shape[1]
    own = columns // 3
    row_count, depth = latents_own.shape
    rows = depth // count
    dtype = latents_own.dtype
    scale = float(E) ** -0.5

    def kernel(own_ref, other_ref, near_ref, *refs):
        block_refs = refs[:count]
        queries_ref, weight_ref, key_value_ref, latents_ref, sem = refs[count:]
        fetch = pltpu.make_async_copy(own_ref, latents_ref, sem)
        fetch.start()
        fsdp_index = lax.axis_index("fsdp")
        z_index = fsdp_index // x_count
        x_index = lax.rem(fsdp_index, x_count)
        for (dz, dx), block_ref in zip(shifts, block_refs):
            place = lax.rem(z_index + z_count - dz, z_count) * x_count + lax.rem(x_index + x_count - dx, x_count)
            weight_ref[pl.ds(pl.multiple_of(place * rows, 16), rows), :] = block_ref[:rows, :]
        for member, from_ref in ((1, other_ref), (0, latents_ref)):
            if member == 0:
                fetch.wait()
            projected = jnp.dot(from_ref[...], weight_ref[...], preferred_element_type=jnp.float32).astype(dtype)
            queries_ref[member] = projected[:, :own] * jnp.asarray(scale, dtype)
            key_value_ref[member * row_count : (member + 1) * row_count, :] = projected[:, own:]
        key_value_ref[CORES * row_count :, :] = jnp.dot(
            near_ref[...], weight_ref[:, own:], preferred_element_type=jnp.float32
        ).astype(dtype)

    return call(
        kernel,
        "project",
        [HBM] + [VMEM] * (count + 2),
        [
            shaped((CORES, row_count, own), dtype),
            shaped((depth, columns), dtype),
            shaped(((CORES + 1) * row_count, 2 * own), dtype),
        ],
        scratch_shapes=[pltpu.VMEM((row_count, depth), dtype), pltpu.SemaphoreType.DMA(())],
        cost=COST1,
    )(latents_own, latents_other, near, *blocks)


def attend(seq_count, sources, key_value, state, last, weight, queries, tile_mask, tile_counts):
    columns = weight.shape[1]
    own = columns // 3
    row_count = queries.shape[1]
    dtype = queries.dtype
    groups = own // LANES
    local_rows = 0 if key_value is None else key_value.shape[0]
    slots = local_rows + len(sources) * row_count
    given = [weight, queries] + [latents for latents, _, _ in sources]
    given += [array for array in (key_value, state) if array is not None]

    def kernel(mask_ref, count_ref, weight_ref, queries_ref, *refs):
        latents_refs, refs = refs[: len(sources)], list(refs[len(sources) :])
        key_value_ref = None if key_value is None else refs.pop(0)
        old_ref = None if state is None else refs.pop(0)
        values_ref, keys_ref = refs.pop(), refs.pop()
        seq_index = lax.axis_index("seq")
        core = lax.rem(seq_index, CORES)
        chip_tile = seq_index - core
        tiles = [chip_tile + core, chip_tile + 1 - core]
        ends = [jnp.int32(0)]
        spans = []

        def place(key_tile, keys, values):
            rows = pl.ds(pl.multiple_of(ends[-1], GRAIN), keys.shape[0])
            keys_ref[rows, :] = keys
            for group in range(groups):
                first = 2 * group * LANES
                values_ref[rows, first : first + LANES] = values[:, group * LANES : (group + 1) * LANES]
            spans.append((key_tile, ends[-1]))
            ends.append(ends[-1] + count_ref[key_tile])

        def tile_of(y_step, swapped):
            from_same = lax.rem(seq_index + seq_count - CORES * y_step, seq_count)
            return from_same + 1 - 2 * core if swapped else from_same

        for index, key_tile in enumerate([*tiles, tile_of(1, False)] if local_rows else []):
            rows = slice(index * row_count, (index + 1) * row_count)
            place(key_tile, key_value_ref[rows, :own], key_value_ref[rows, own:])
        for part, (_, y_step, swapped) in enumerate(sources):
            projected = jnp.dot(
                latents_refs[part][...], weight_ref[:, own:], preferred_element_type=jnp.float32
            ).astype(dtype)
            place(tile_of(y_step, swapped), projected[:, :own], projected[:, own:])
        rest = pl.ds(pl.multiple_of(spans[-1][1] + row_count, GRAIN), BLOCK)
        keys_ref[rest, :] = jnp.zeros((BLOCK, own), dtype)
        values_ref[rest, :] = jnp.zeros((BLOCK, 2 * own), dtype)
        for group in range(groups):
            first = (2 * group + 1) * LANES
            values_ref[:, first : first + LANES] = jnp.ones((slots + BLOCK, LANES), dtype)

        def over(keys_taken):
            slot = lax.broadcasted_iota(jnp.int32, (1, keys_taken), 1)
            for member in range(CORES):
                bias = jnp.full((1, keys_taken), NEG, jnp.float32)
                for key_tile, start in spans:
                    end = start + jnp.where(mask_ref[tiles[member], key_tile] > 0, count_ref[key_tile], 0)
                    bias = jnp.where((slot >= start) & (slot < end), 0.0, bias)
                for group in range(groups):
                    lanes = slice(group * LANES, (group + 1) * LANES)
                    for start in range(0, row_count, ROWS):
                        chunk = slice(start, start + ROWS)
                        parts = attend_part(
                            queries_ref[member, chunk, lanes],
                            keys_ref[:keys_taken, lanes],
                            values_ref[:keys_taken, 2 * group * LANES : 2 * (group + 1) * LANES],
                            bias,
                        )
                        if old_ref is not None:
                            parts = merge([old_ref[member, which, chunk, lanes] for which in range(3)], parts)
                        if last:
                            position = start + lax.broadcasted_iota(jnp.int32, (ROWS, 1), 0)
                            attended = jnp.where(position < count_ref[tiles[member]], parts[2] / parts[1], 0.0)
                            refs[member][chunk, lanes] = attended.astype(dtype)
                        else:
                            for which, part in enumerate(parts):
                                refs[0][member, which, chunk, lanes] = part

        blocks = (ends[-1] + BLOCK - 1) // BLOCK
        fewest, most = max(slots // (2 * BLOCK), 1), slots // BLOCK
        for taken in range(fewest, most + 1):
            fits = blocks <= taken if taken == fewest else blocks == taken
            pl.when(fits)(lambda taken=taken: over(taken * BLOCK))

    if last:
        out_shapes = [shaped((row_count, own), dtype)] * CORES
    else:
        out_shapes = [shaped((CORES, 3, row_count, own), jnp.float32)]
    return call(
        kernel,
        "attend_last" if last else "attend",
        [SMEM, SMEM] + [VMEM] * len(given),
        out_shapes,
        scratch_shapes=[pltpu.VMEM((slots + BLOCK, own), dtype), pltpu.VMEM((slots + BLOCK, 2 * own), dtype)],
        cost=COST,
    )(tile_mask, tile_counts, *given)


def project_out(attended_own, attended_partner, out_own, out_partner):
    row_count, own = attended_own.shape
    side = out_own.shape[1]
    dtype = attended_own.dtype

    def kernel(own_ref, partner_ref, out_own_ref, out_partner_ref, result_ref, staged_ref, sems):
        core = lax.rem(lax.axis_index("seq"), CORES)
        own_rows = pl.ds(pl.multiple_of(core * own, 16), own)
        partner_rows = pl.ds(pl.multiple_of((1 - core) * own, 16), own)
        copies = []
        for half, weight_ref in enumerate((out_own_ref, out_partner_ref)):
            total = jnp.dot(own_ref[...], weight_ref[own_rows, :], preferred_element_type=jnp.float32)
            total += jnp.dot(partner_ref[...], weight_ref[partner_rows, :], preferred_element_type=jnp.float32)
            staged_ref[half] = total.astype(dtype)
            start = pl.multiple_of((core if half == 0 else 1 - core) * side, LANES)
            copies.append(
                pltpu.make_async_copy(staged_ref.at[half], result_ref.at[:, pl.ds(start, side)], sems.at[half])
            )
            copies[-1].start()
        for copy in copies:
            copy.wait()

    return call(
        kernel,
        "project_out",
        [VMEM] * 4,
        [shaped((row_count, CORES * side), dtype)],
        [HBM],
        scratch_shapes=[pltpu.VMEM((CORES, row_count, side), dtype), pltpu.SemaphoreType.DMA((CORES,))],
    )(attended_own, attended_partner, out_own, out_partner)[0]


def after(array, *others):
    return lax.optimization_barrier((array, *others))[0]


def local(latents, qkv_weight, out_weight, tile_mask, tile_counts):
    seq_count = lax.axis_size("seq")
    fsdp_count = lax.axis_size("fsdp")
    z_count, x_count = grid_of(fsdp_count)
    chips = seq_count // CORES
    latents_own = latents[0]

    def hop(array, z_step, x_step):
        return lax.ppermute(array, "fsdp", rotation(z_count, x_count, z_step, x_step))

    def flip(array, shift):
        return lax.ppermute(array, "fsdp", [(f, f ^ (shift * x_count)) for f in range(fsdp_count)])

    along_y = [y_rotation(latents_own, seq_count, step) for step in range(1, chips)]
    latents_other = core_swap(latents_own, seq_count)
    half, packed = halves(qkv_weight, out_weight)

    came = {(0, 0): half}
    for x_step in range(1, x_count):
        came[0, x_step] = hop(after(packed, latents_other), 0, x_step)
    beside = [came[0, x_step] for x_step in range(1, x_count)]
    turn = z_count // 2
    for z_step in (turn, 1):
        came[z_step, 0] = hop(packed if z_step == turn else half, z_step, 0)
    second = after(half, came[1, 0], *beside)
    third = after(half, came[turn, 0])
    for x_step in range(1, x_count):
        came[turn, x_step] = hop(came[turn, 0], 0, x_step)
        came[1, x_step] = hop(second, 1, x_step)
    for z_step in range(2, z_count):
        if z_step != turn:
            came[z_step, 0] = hop(second, z_step, 0)
            for x_step in range(1, x_count):
                came[z_step, x_step] = hop(third, z_step, x_step)

    axes = (z_count, x_count)
    early = None
    if x_count * half.shape[0] % LANES == 0:
        sooner = [shift for shift in came if shift[0] in (0, turn)]
        early = project(*axes, sooner, [came[shift] for shift in sooner], latents_own, latents_other)
        packed = after(packed, early[2])

    out_own = collect(
        [[packed] + beside, [came[turn, x_step] for x_step in range(x_count)]],
        x_count,
        z_count,
        half.shape[0],
        out_weight.shape[0],
        out_weight.shape[1] // CORES,
    )
    units, shift = 2, turn // 2
    while shift > 1:
        out_own = pair_up(out_own, flip(out_own, shift), units, shift, x_count)
        units, shift = 2 * units, shift // 2
    out_got = flip(out_own, shift)

    near = after(along_y, out_own, *list(came.values())[1:])
    far = [core_swap(array, seq_count) for array in near]
    if early is not None:
        later = [shift for shift in came if shift not in sooner]
        came[later[-1]] = after(came[later[-1]], *near)
        queries, weight, key_value = project(
            *axes, later, [came[shift] for shift in later], latents_own, latents_other, near[0], early
        )
    else:
        came[0, 0] = after(half, *near)
        queries, weight, key_value = project_whole(
            *axes, list(came), list(came.values()), latents_own, latents_other, near[0]
        )
    state = None
    for step in range(1, chips):
        last = step == chips - 1
        result = attend(
            seq_count,
            [(near[step - 1], step, False)] * (step > 1) + [(far[step - 1], step, True)],
            key_value if step == 1 else None,
            state,
            last,
            weight,
            queries,
            tile_mask,
            tile_counts,
        )
        state = None if last else result[0]
    attended_own, attended_other = result
    attended_partner = core_swap(attended_other, seq_count)
    out_own = pair_up(out_own, after(out_got, attended_other), units, shift, x_count)
    out_partner = core_swap(out_own, seq_count)
    return project_out(attended_own, attended_partner, out_own, out_partner)[None]


def solution(mesh):
    return jax.shard_map(
        local,
        mesh=mesh,
        in_specs=(P("fsdp", "seq", None), P("fsdp", None), P("fsdp", None), P(), P()),
        out_specs=P("fsdp", "seq", None),
        check_vma=False,
    )
```

```python
import jax
import jax.numpy as jnp
from jax import lax
from jax.experimental import pallas as pl
from jax.experimental.pallas import tpu as pltpu
from jax.sharding import PartitionSpec as P

E = 64
LANES = 128
CORES = 2
NEG = -1e30
ROWS = 192
BLOCK = 256
GRAIN = 64
COST1 = 1_000_000_000
COST = 1_000_000_000

VMEM = pl.BlockSpec(memory_space=pltpu.VMEM)
SMEM = pl.BlockSpec(memory_space=pltpu.SMEM)
HBM = pl.BlockSpec(memory_space=pltpu.HBM)


def grid_of(fsdp_count):
    x_count = 1
    while (2 * x_count) ** 2 <= fsdp_count and fsdp_count % (2 * x_count) == 0:
        x_count *= 2
    return fsdp_count // x_count, x_count


def rotation(z_count, x_count, z_step, x_step):
    return [
        (z * x_count + x, (z + z_step) % z_count * x_count + (x + x_step) % x_count)
        for z in range(z_count)
        for x in range(x_count)
    ]


def core_swap(array, seq_count):
    return lax.ppermute(array, "seq", [(s, s ^ 1) for s in range(seq_count)])


def y_rotation(array, seq_count, step):
    return lax.ppermute(array, "seq", [(s, (s + CORES * step) % seq_count) for s in range(seq_count)])


def call(kernel, name, in_specs, out_shapes, out_specs=None, scratch_shapes=(), cost=0, aliases={}):
    out_specs = [VMEM] * len(out_shapes) if out_specs is None else out_specs
    shapes = [
        pltpu.VMEM(shape.shape, shape.dtype) if spec is VMEM else shape for shape, spec in zip(out_shapes, out_specs)
    ]
    inner = pl.pallas_call(
        kernel,
        out_shape=shapes,
        in_specs=in_specs,
        out_specs=out_specs,
        scratch_shapes=scratch_shapes,
        input_output_aliases=aliases,
        cost_estimate=pl.CostEstimate(flops=cost, bytes_accessed=0, transcendentals=0) if cost else None,
        compiler_params=pltpu.CompilerParams(vmem_limit_bytes=24 << 20),
        name=name,
    )

    def run(*args):
        return inner(
            *[
                pltpu.with_memory_space_constraint(arg, pltpu.HBM if spec is SMEM else spec.memory_space)
                for arg, spec in zip(args, in_specs)
            ]
        )

    return run


def shaped(shape, dtype):
    return jax.ShapeDtypeStruct(shape, dtype)


def strips(width, columns):
    strip = min(width, columns)
    return [(start, strip) for start in range(0, width, strip)]


def halves(qkv_weight, out_weight):
    rows, columns = qkv_weight.shape
    head_columns = columns // 3
    own = head_columns // CORES
    out_rows, width = out_weight.shape
    side = width // CORES
    pieces = strips(side, 3 * own)

    def kernel(qkv_ref, out_ref, half_ref, packed_ref, sems):
        core = lax.rem(lax.axis_index("seq"), CORES)
        copies = []

        def copy(source, target):
            copies.append(pltpu.make_async_copy(source, target, sems.at[len(copies)]))
            copies[-1].start()

        for part in range(3):
            source = qkv_ref.at[:, pl.ds(pl.multiple_of(part * head_columns + core * own, LANES), own)]
            lanes = slice(part * own, (part + 1) * own)
            copy(source, half_ref.at[:, lanes])
            copy(source, packed_ref.at[:rows, lanes])
        for piece, (start, strip) in enumerate(pieces):
            first = rows + piece * out_rows
            copy(
                out_ref.at[:, pl.ds(pl.multiple_of(core * side + start, LANES), strip)],
                packed_ref.at[first : first + out_rows, :strip],
            )
        for each in copies:
            each.wait()

    return call(
        kernel,
        "halves",
        [HBM, HBM],
        [
            shaped((rows, 3 * own), qkv_weight.dtype),
            shaped((rows + len(pieces) * out_rows, 3 * own), qkv_weight.dtype),
        ],
        scratch_shapes=[pltpu.SemaphoreType.DMA((6 + len(pieces),))],
    )(qkv_weight, out_weight)


def collect(blocks, x_count, z_count, rows, out_rows, side):
    pieces = strips(side, blocks[0][0].shape[1])
    flat = [(half, step) for half in range(len(blocks)) for step in range(x_count)]

    def kernel(*refs):
        fsdp_index = lax.axis_index("fsdp")
        x_index = lax.rem(fsdp_index, x_count)
        bit = lax.rem(fsdp_index // (x_count * (z_count // 2)), 2)
        for (half, step), ref in zip(flat, refs):
            place = (1 - bit if half else bit) * x_count + lax.rem(x_index + x_count - step, x_count)
            for piece, (start, strip) in enumerate(pieces):
                first = rows + piece * out_rows
                refs[-1][pl.ds(pl.multiple_of(place * out_rows, 16), out_rows), start : start + strip] = ref[
                    first : first + out_rows, :strip
                ]

    return call(
        kernel, "collect", [VMEM] * len(flat), [shaped((len(flat) * out_rows, side), blocks[0][0].dtype)]
    )(*[blocks[half][step] for half, step in flat])[0]


def pair_up(own, got, units, shift, x_count):
    rows, columns = own.shape
    each = rows // units

    def kernel(own_ref, got_ref, pair_ref):
        bit = lax.rem(lax.axis_index("fsdp") // (x_count * shift), 2)
        for unit in range(units):
            piece = slice(unit * each, (unit + 1) * each)
            pair_ref[pl.ds(pl.multiple_of((2 * unit + bit) * each, 16), each), :] = own_ref[piece, :]
            pair_ref[pl.ds(pl.multiple_of((2 * unit + 1 - bit) * each, 16), each), :] = got_ref[piece, :]

    return call(kernel, "pair_up", [VMEM, VMEM], [shaped((2 * rows, columns), own.dtype)])(own, got)[0]


def lane_pick(per_head):
    lane = lax.broadcasted_iota(jnp.int32, (1, LANES), 1)
    picked = per_head[0]
    for head in range(1, len(per_head)):
        picked = jnp.where(lane >= head * E, per_head[head], picked)
    return jnp.broadcast_to(picked, (picked.shape[0], LANES))


def attend_part(queries, keys, values, bias):
    lane = lax.broadcasted_iota(jnp.int32, (1, LANES), 1)
    rows = queries.shape[0]
    heads = LANES // E
    zero = jnp.zeros_like(queries)
    stacked = jnp.concatenate(
        [jnp.where((lane >= head * E) & (lane < (head + 1) * E), queries, zero) for head in range(heads)], axis=0
    )
    scores = lax.dot_general(stacked, keys, (((1,), (1,)), ((), ())), preferred_element_type=jnp.float32) + bias
    row_max = jnp.max(scores, axis=1, keepdims=True)
    numerators = jnp.exp(scores - row_max).astype(values.dtype)
    summed = jnp.dot(numerators, values, preferred_element_type=jnp.float32)

    def pick(array):
        return lane_pick([array[head * rows : (head + 1) * rows] for head in range(heads)])

    return pick(row_max), pick(summed[:, LANES:]), pick(summed[:, :LANES])


def merge(old, new):
    top = jnp.maximum(old[0], new[0])
    keep = jnp.exp(old[0] - top)
    add = jnp.exp(new[0] - top)
    return top, old[1] * keep + new[1] * add, old[2] * keep + new[2] * add


def project(z_count, x_count, shifts, blocks, latents_own, latents_other, near=None, early=None):
    count = len(blocks)
    columns = blocks[0].shape[1]
    own = columns // 3
    row_count, depth = latents_own.shape
    rows = depth // (z_count * x_count)
    band = x_count * rows
    steps = sorted({dz for dz, _ in shifts})
    dtype = latents_own.dtype
    scale = float(E) ** -0.5

    def assemble(block_refs, weight_ref):
        fsdp_index = lax.axis_index("fsdp")
        z_index = fsdp_index // x_count
        x_index = lax.rem(fsdp_index, x_count)
        for (dz, dx), block_ref in zip(shifts, block_refs):
            place = lax.rem(z_index + z_count - dz, z_count) * x_count + lax.rem(x_index + x_count - dx, x_count)
            weight_ref[pl.ds(pl.multiple_of(place * rows, 16), rows), :] = block_ref[:rows, :]
        starts = [pl.multiple_of(lax.rem(z_index + z_count - dz, z_count) * band, LANES) for dz in steps]
        return starts, jnp.concatenate([weight_ref[pl.ds(start, band), :] for start in starts], axis=0)

    def partial(latents_ref, starts, weight):
        latents = jnp.concatenate([latents_ref[:, pl.ds(start, band)] for start in starts], axis=1)
        return jnp.dot(latents, weight, preferred_element_type=jnp.float32)

    def first(own_ref, other_ref, *refs):
        block_refs = refs[:count]
        latents_ref, weight_ref, total_ref, sem = refs[count:]
        fetch = pltpu.make_async_copy(own_ref, latents_ref, sem)
        fetch.start()
        starts, weight = assemble(block_refs, weight_ref)
        total_ref[1] = partial(other_ref, starts, weight)
        fetch.wait()
        total_ref[0] = partial(latents_ref, starts, weight)

    def rest(own_ref, other_ref, old_weight_ref, total_ref, near_ref, *refs):
        block_refs = refs[:count]
        queries_ref, weight_ref, key_value_ref = refs[count:]
        starts, weight = assemble(block_refs, weight_ref)
        for member, from_ref in enumerate((own_ref, other_ref)):
            projected = (total_ref[member] + partial(from_ref, starts, weight)).astype(dtype)
            queries_ref[member] = projected[:, :own] * jnp.asarray(scale, dtype)
            key_value_ref[member * row_count : (member + 1) * row_count, :] = projected[:, own:]
        key_value_ref[CORES * row_count :, :] = jnp.dot(
            near_ref[...], weight_ref[:, own:], preferred_element_type=jnp.float32
        ).astype(dtype)

    weight_shape = shaped((depth, columns), dtype)
    if early is None:
        return call(
            first,
            "project_first",
            [HBM] + [VMEM] * (count + 1),
            [shaped((row_count, depth), dtype), weight_shape, shaped((CORES, row_count, columns), jnp.float32)],
            scratch_shapes=[pltpu.SemaphoreType.DMA(())],
            cost=COST1,
        )(latents_own, latents_other, *blocks)
    own_tile, weight, total = early
    return call(
        rest,
        "project",
        [VMEM] * (count + 5),
        [
            shaped((CORES, row_count, own), dtype),
            weight_shape,
            shaped(((CORES + 1) * row_count, 2 * own), dtype),
        ],
        cost=COST1,
        aliases={2: 1},
    )(own_tile, latents_other, weight, total, near, *blocks)


def project_whole(z_count, x_count, shifts, blocks, latents_own, latents_other, near):
    count = len(blocks)
    columns = blocks[0].shape[1]
    own = columns // 3
    row_count, depth = latents_own.shape
    rows = depth // count
    dtype = latents_own.dtype
    scale = float(E) ** -0.5

    def kernel(own_ref, other_ref, near_ref, *refs):
        block_refs = refs[:count]
        queries_ref, weight_ref, key_value_ref, latents_ref, sem = refs[count:]
        fetch = pltpu.make_async_copy(own_ref, latents_ref, sem)
        fetch.start()
        fsdp_index = lax.axis_index("fsdp")
        z_index = fsdp_index // x_count
        x_index = lax.rem(fsdp_index, x_count)
        for (dz, dx), block_ref in zip(shifts, block_refs):
            place = lax.rem(z_index + z_count - dz, z_count) * x_count + lax.rem(x_index + x_count - dx, x_count)
            weight_ref[pl.ds(pl.multiple_of(place * rows, 16), rows), :] = block_ref[:rows, :]
        for member, from_ref in ((1, other_ref), (0, latents_ref)):
            if member == 0:
                fetch.wait()
            projected = jnp.dot(from_ref[...], weight_ref[...], preferred_element_type=jnp.float32).astype(dtype)
            queries_ref[member] = projected[:, :own] * jnp.asarray(scale, dtype)
            key_value_ref[member * row_count : (member + 1) * row_count, :] = projected[:, own:]
        key_value_ref[CORES * row_count :, :] = jnp.dot(
            near_ref[...], weight_ref[:, own:], preferred_element_type=jnp.float32
        ).astype(dtype)

    return call(
        kernel,
        "project",
        [HBM] + [VMEM] * (count + 2),
        [
            shaped((CORES, row_count, own), dtype),
            shaped((depth, columns), dtype),
            shaped(((CORES + 1) * row_count, 2 * own), dtype),
        ],
        scratch_shapes=[pltpu.VMEM((row_count, depth), dtype), pltpu.SemaphoreType.DMA(())],
        cost=COST1,
    )(latents_own, latents_other, near, *blocks)


def attend(seq_count, sources, key_value, state, last, weight, queries, tile_mask, tile_counts):
    columns = weight.shape[1]
    own = columns // 3
    row_count = queries.shape[1]
    dtype = queries.dtype
    groups = own // LANES
    local_rows = 0 if key_value is None else key_value.shape[0]
    slots = local_rows + len(sources) * row_count
    given = [weight, queries] + [latents for latents, _, _ in sources]
    given += [array for array in (key_value, state) if array is not None]

    def kernel(mask_ref, count_ref, weight_ref, queries_ref, *refs):
        latents_refs, refs = refs[: len(sources)], list(refs[len(sources) :])
        key_value_ref = None if key_value is None else refs.pop(0)
        old_ref = None if state is None else refs.pop(0)
        values_ref, keys_ref = refs.pop(), refs.pop()
        seq_index = lax.axis_index("seq")
        core = lax.rem(seq_index, CORES)
        chip_tile = seq_index - core
        tiles = [chip_tile + core, chip_tile + 1 - core]
        ends = [jnp.int32(0)]
        spans = []

        def place(key_tile, keys, values):
            rows = pl.ds(pl.multiple_of(ends[-1], GRAIN), keys.shape[0])
            keys_ref[rows, :] = keys
            for group in range(groups):
                first = 2 * group * LANES
                values_ref[rows, first : first + LANES] = values[:, group * LANES : (group + 1) * LANES]
            spans.append((key_tile, ends[-1]))
            ends.append(ends[-1] + count_ref[key_tile])

        def tile_of(y_step, swapped):
            from_same = lax.rem(seq_index + seq_count - CORES * y_step, seq_count)
            return from_same + 1 - 2 * core if swapped else from_same

        for index, key_tile in enumerate([*tiles, tile_of(1, False)] if local_rows else []):
            rows = slice(index * row_count, (index + 1) * row_count)
            place(key_tile, key_value_ref[rows, :own], key_value_ref[rows, own:])
        for part, (_, y_step, swapped) in enumerate(sources):
            projected = jnp.dot(
                latents_refs[part][...], weight_ref[:, own:], preferred_element_type=jnp.float32
            ).astype(dtype)
            place(tile_of(y_step, swapped), projected[:, :own], projected[:, own:])
        rest = pl.ds(pl.multiple_of(spans[-1][1] + row_count, GRAIN), BLOCK)
        keys_ref[rest, :] = jnp.zeros((BLOCK, own), dtype)
        values_ref[rest, :] = jnp.zeros((BLOCK, 2 * own), dtype)
        for group in range(groups):
            first = (2 * group + 1) * LANES
            values_ref[:, first : first + LANES] = jnp.ones((slots + BLOCK, LANES), dtype)

        def over(keys_taken):
            slot = lax.broadcasted_iota(jnp.int32, (1, keys_taken), 1)
            for member in range(CORES):
                bias = jnp.full((1, keys_taken), NEG, jnp.float32)
                for key_tile, start in spans:
                    end = start + jnp.where(mask_ref[tiles[member], key_tile] > 0, count_ref[key_tile], 0)
                    bias = jnp.where((slot >= start) & (slot < end), 0.0, bias)
                for group in range(groups):
                    lanes = slice(group * LANES, (group + 1) * LANES)
                    for start in range(0, row_count, ROWS):
                        chunk = slice(start, start + ROWS)
                        parts = attend_part(
                            queries_ref[member, chunk, lanes],
                            keys_ref[:keys_taken, lanes],
                            values_ref[:keys_taken, 2 * group * LANES : 2 * (group + 1) * LANES],
                            bias,
                        )
                        if old_ref is not None:
                            parts = merge([old_ref[member, which, chunk, lanes] for which in range(3)], parts)
                        if last:
                            position = start + lax.broadcasted_iota(jnp.int32, (ROWS, 1), 0)
                            attended = jnp.where(position < count_ref[tiles[member]], parts[2] / parts[1], 0.0)
                            refs[member][chunk, lanes] = attended.astype(dtype)
                        else:
                            for which, part in enumerate(parts):
                                refs[0][member, which, chunk, lanes] = part

        blocks = (ends[-1] + BLOCK - 1) // BLOCK
        fewest, most = max(slots // (2 * BLOCK), 1), slots // BLOCK
        for taken in range(fewest, most + 1):
            fits = blocks <= taken if taken == fewest else blocks == taken
            pl.when(fits)(lambda taken=taken: over(taken * BLOCK))

    if last:
        out_shapes = [shaped((row_count, own), dtype)] * CORES
    else:
        out_shapes = [shaped((CORES, 3, row_count, own), jnp.float32)]
    return call(
        kernel,
        "attend_last" if last else "attend",
        [SMEM, SMEM] + [VMEM] * len(given),
        out_shapes,
        scratch_shapes=[pltpu.VMEM((slots + BLOCK, own), dtype), pltpu.VMEM((slots + BLOCK, 2 * own), dtype)],
        cost=COST,
    )(tile_mask, tile_counts, *given)


def project_out(attended_own, attended_partner, out_own, out_partner):
    row_count, own = attended_own.shape
    side = out_own.shape[1]
    strip = side // 3 if side % (3 * BLOCK) == 0 else side
    dtype = attended_own.dtype

    def kernel(own_ref, partner_ref, out_own_ref, out_partner_ref, result_ref, staged_ref, sems):
        core = lax.rem(lax.axis_index("seq"), CORES)
        own_rows = pl.ds(pl.multiple_of(core * own, 16), own)
        partner_rows = pl.ds(pl.multiple_of((1 - core) * own, 16), own)
        copies = []
        for half, weight_ref in enumerate((out_own_ref, out_partner_ref)):
            for first in range(0, side, strip):
                columns = slice(first, first + strip)
                total = jnp.dot(own_ref[...], weight_ref[own_rows, columns], preferred_element_type=jnp.float32)
                total += jnp.dot(partner_ref[...], weight_ref[partner_rows, columns], preferred_element_type=jnp.float32)
                staged_ref[half, :, columns] = total.astype(dtype)
                start = pl.multiple_of((core if half == 0 else 1 - core) * side + first, LANES)
                copies.append(
                    pltpu.make_async_copy(
                        staged_ref.at[half, :, columns], result_ref.at[:, pl.ds(start, strip)], sems.at[len(copies)]
                    )
                )
                copies[-1].start()
        for copy in copies:
            copy.wait()

    return call(
        kernel,
        "project_out",
        [VMEM] * 4,
        [shaped((row_count, CORES * side), dtype)],
        [HBM],
        scratch_shapes=[pltpu.VMEM((CORES, row_count, side), dtype), pltpu.SemaphoreType.DMA((CORES * side // strip,))],
    )(attended_own, attended_partner, out_own, out_partner)[0]


def after(array, *others):
    return lax.optimization_barrier((array, *others))[0]


def local(latents, qkv_weight, out_weight, tile_mask, tile_counts):
    seq_count = lax.axis_size("seq")
    fsdp_count = lax.axis_size("fsdp")
    z_count, x_count = grid_of(fsdp_count)
    chips = seq_count // CORES
    latents_own = latents[0]

    def hop(array, z_step, x_step):
        return lax.ppermute(array, "fsdp", rotation(z_count, x_count, z_step, x_step))

    def flip(array, shift):
        return lax.ppermute(array, "fsdp", [(f, f ^ (shift * x_count)) for f in range(fsdp_count)])

    along_y = [y_rotation(latents_own, seq_count, step) for step in range(1, chips)]
    latents_other = core_swap(latents_own, seq_count)
    half, packed = halves(qkv_weight, out_weight)

    came = {(0, 0): half}
    for x_step in range(1, x_count):
        came[0, x_step] = hop(after(packed, latents_other), 0, x_step)
    beside = [came[0, x_step] for x_step in range(1, x_count)]
    turn = z_count // 2
    for z_step in (turn, 1):
        came[z_step, 0] = hop(packed if z_step == turn else half, z_step, 0)
    second = after(half, came[1, 0], *beside)
    third = after(half, came[turn, 0])
    for x_step in range(1, x_count):
        came[turn, x_step] = hop(came[turn, 0], 0, x_step)
        came[1, x_step] = hop(second, 1, x_step)
    for z_step in range(2, z_count):
        if z_step != turn:
            came[z_step, 0] = hop(second, z_step, 0)
            for x_step in range(1, x_count):
                came[z_step, x_step] = hop(third, z_step, x_step)

    axes = (z_count, x_count)
    early = None
    if x_count * half.shape[0] % LANES == 0:
        sooner = [shift for shift in came if shift[0] in (0, turn)]
        early = project(*axes, sooner, [came[shift] for shift in sooner], latents_own, latents_other)
        packed = after(packed, early[2])

    out_own = collect(
        [[packed] + beside, [came[turn, x_step] for x_step in range(x_count)]],
        x_count,
        z_count,
        half.shape[0],
        out_weight.shape[0],
        out_weight.shape[1] // CORES,
    )
    units, shift = 2, turn // 2
    while shift > 1:
        out_own = pair_up(out_own, flip(out_own, shift), units, shift, x_count)
        units, shift = 2 * units, shift // 2
    out_got = flip(out_own, shift)

    near = after(along_y, out_own, *list(came.values())[1:])
    far = [core_swap(array, seq_count) for array in near]
    if early is not None:
        later = [shift for shift in came if shift not in sooner]
        came[later[-1]] = after(came[later[-1]], *near)
        queries, weight, key_value = project(
            *axes, later, [came[shift] for shift in later], latents_own, latents_other, near[0], early
        )
    else:
        came[0, 0] = after(half, *near)
        queries, weight, key_value = project_whole(
            *axes, list(came), list(came.values()), latents_own, latents_other, near[0]
        )
    state = None
    for step in range(1, chips):
        last = step == chips - 1
        result = attend(
            seq_count,
            [(near[step - 1], step, False)] * (step > 1) + [(far[step - 1], step, True)],
            key_value if step == 1 else None,
            state,
            last,
            weight,
            queries,
            tile_mask,
            tile_counts,
        )
        state = None if last else result[0]
    attended_own, attended_other = result
    attended_partner = core_swap(attended_other, seq_count)
    out_own = pair_up(out_own, after(out_got, attended_other), units, shift, x_count)
    out_partner = core_swap(out_own, seq_count)
    return project_out(attended_own, attended_partner, out_own, out_partner)[None]


def solution(mesh):
    return jax.shard_map(
        local,
        mesh=mesh,
        in_specs=(P("fsdp", "seq", None), P("fsdp", None), P("fsdp", None), P(), P()),
        out_specs=P("fsdp", "seq", None),
        check_vma=False,
    )
```

```python
import jax
import jax.numpy as jnp
from jax import lax
from jax.experimental import pallas as pl
from jax.experimental.pallas import tpu as pltpu
from jax.sharding import PartitionSpec as P

E = 64
LANES = 128
CORES = 2
NEG = -1e30
ROWS = 192
BLOCK = 256
GRAIN = 64
COST1 = 1_000_000_000
COST = 1_000_000_000

VMEM = pl.BlockSpec(memory_space=pltpu.VMEM)
SMEM = pl.BlockSpec(memory_space=pltpu.SMEM)
HBM = pl.BlockSpec(memory_space=pltpu.HBM)


def grid_of(fsdp_count):
    x_count = 1
    while (2 * x_count) ** 2 <= fsdp_count and fsdp_count % (2 * x_count) == 0:
        x_count *= 2
    return fsdp_count // x_count, x_count


def rotation(z_count, x_count, z_step, x_step):
    return [
        (z * x_count + x, (z + z_step) % z_count * x_count + (x + x_step) % x_count)
        for z in range(z_count)
        for x in range(x_count)
    ]


def core_swap(array, seq_count):
    return lax.ppermute(array, "seq", [(s, s ^ 1) for s in range(seq_count)])


def y_rotation(array, seq_count, step):
    return lax.ppermute(array, "seq", [(s, (s + CORES * step) % seq_count) for s in range(seq_count)])


def call(kernel, name, in_specs, out_shapes, out_specs=None, scratch_shapes=(), cost=0, aliases={}):
    out_specs = [VMEM] * len(out_shapes) if out_specs is None else out_specs
    shapes = [
        pltpu.VMEM(shape.shape, shape.dtype) if spec is VMEM else shape for shape, spec in zip(out_shapes, out_specs)
    ]
    inner = pl.pallas_call(
        kernel,
        out_shape=shapes,
        in_specs=in_specs,
        out_specs=out_specs,
        scratch_shapes=scratch_shapes,
        input_output_aliases=aliases,
        cost_estimate=pl.CostEstimate(flops=cost, bytes_accessed=0, transcendentals=0) if cost else None,
        compiler_params=pltpu.CompilerParams(vmem_limit_bytes=24 << 20),
        name=name,
    )

    def run(*args):
        return inner(
            *[
                pltpu.with_memory_space_constraint(arg, pltpu.HBM if spec is SMEM else spec.memory_space)
                for arg, spec in zip(args, in_specs)
            ]
        )

    return run


def shaped(shape, dtype):
    return jax.ShapeDtypeStruct(shape, dtype)


def strips(width, columns):
    strip = min(width, columns)
    return [(start, strip) for start in range(0, width, strip)]


def halves(qkv_weight, out_weight):
    rows, columns = qkv_weight.shape
    head_columns = columns // 3
    own = head_columns // CORES
    out_rows, width = out_weight.shape
    side = width // CORES
    pieces = strips(side, 3 * own)

    def kernel(qkv_ref, out_ref, half_ref, packed_ref, sems):
        core = lax.rem(lax.axis_index("seq"), CORES)
        copies = []

        def copy(source, target):
            copies.append(pltpu.make_async_copy(source, target, sems.at[len(copies)]))
            copies[-1].start()

        for part in range(3):
            source = qkv_ref.at[:, pl.ds(pl.multiple_of(part * head_columns + core * own, LANES), own)]
            lanes = slice(part * own, (part + 1) * own)
            copy(source, half_ref.at[:, lanes])
            copy(source, packed_ref.at[:rows, lanes])
        for piece, (start, strip) in enumerate(pieces):
            first = rows + piece * out_rows
            copy(
                out_ref.at[:, pl.ds(pl.multiple_of(core * side + start, LANES), strip)],
                packed_ref.at[first : first + out_rows, :strip],
            )
        for each in copies:
            each.wait()

    return call(
        kernel,
        "halves",
        [HBM, HBM],
        [
            shaped((rows, 3 * own), qkv_weight.dtype),
            shaped((rows + len(pieces) * out_rows, 3 * own), qkv_weight.dtype),
        ],
        scratch_shapes=[pltpu.SemaphoreType.DMA((6 + len(pieces),))],
    )(qkv_weight, out_weight)


def collect(blocks, x_count, z_count, rows, out_rows, side):
    pieces = strips(side, blocks[0][0].shape[1])
    flat = [(half, step) for half in range(len(blocks)) for step in range(x_count)]

    def kernel(*refs):
        fsdp_index = lax.axis_index("fsdp")
        x_index = lax.rem(fsdp_index, x_count)
        bit = lax.rem(fsdp_index // (x_count * (z_count // 2)), 2)
        for (half, step), ref in zip(flat, refs):
            place = (1 - bit if half else bit) * x_count + lax.rem(x_index + x_count - step, x_count)
            for piece, (start, strip) in enumerate(pieces):
                first = rows + piece * out_rows
                refs[-1][pl.ds(pl.multiple_of(place * out_rows, 16), out_rows), start : start + strip] = ref[
                    first : first + out_rows, :strip
                ]

    return call(
        kernel, "collect", [VMEM] * len(flat), [shaped((len(flat) * out_rows, side), blocks[0][0].dtype)]
    )(*[blocks[half][step] for half, step in flat])[0]


def pair_up(own, got, units, shift, x_count):
    rows, columns = own.shape
    each = rows // units

    def kernel(own_ref, got_ref, pair_ref):
        bit = lax.rem(lax.axis_index("fsdp") // (x_count * shift), 2)
        for unit in range(units):
            piece = slice(unit * each, (unit + 1) * each)
            pair_ref[pl.ds(pl.multiple_of((2 * unit + bit) * each, 16), each), :] = own_ref[piece, :]
            pair_ref[pl.ds(pl.multiple_of((2 * unit + 1 - bit) * each, 16), each), :] = got_ref[piece, :]

    return call(kernel, "pair_up", [VMEM, VMEM], [shaped((2 * rows, columns), own.dtype)])(own, got)[0]


def lane_pick(per_head):
    lane = lax.broadcasted_iota(jnp.int32, (1, LANES), 1)
    picked = per_head[0]
    for head in range(1, len(per_head)):
        picked = jnp.where(lane >= head * E, per_head[head], picked)
    return jnp.broadcast_to(picked, (picked.shape[0], LANES))


def attend_part(queries, keys, values, bias):
    lane = lax.broadcasted_iota(jnp.int32, (1, LANES), 1)
    rows = queries.shape[0]
    heads = LANES // E
    zero = jnp.zeros_like(queries)
    stacked = jnp.concatenate(
        [jnp.where((lane >= head * E) & (lane < (head + 1) * E), queries, zero) for head in range(heads)], axis=0
    )
    scores = lax.dot_general(stacked, keys, (((1,), (1,)), ((), ())), preferred_element_type=jnp.float32) + bias
    row_max = jnp.max(scores, axis=1, keepdims=True)
    numerators = jnp.exp(scores - row_max).astype(values.dtype)
    summed = jnp.dot(numerators, values, preferred_element_type=jnp.float32)

    def pick(array):
        return lane_pick([array[head * rows : (head + 1) * rows] for head in range(heads)])

    return pick(row_max), pick(summed[:, LANES:]), pick(summed[:, :LANES])


def merge(old, new):
    top = jnp.maximum(old[0], new[0])
    keep = jnp.exp(old[0] - top)
    add = jnp.exp(new[0] - top)
    return top, old[1] * keep + new[1] * add, old[2] * keep + new[2] * add


def project(z_count, x_count, shifts, blocks, latents_own, latents_other, near=None, early=None):
    count = len(blocks)
    columns = blocks[0].shape[1]
    own = columns // 3
    row_count, depth = latents_own.shape
    rows = depth // (z_count * x_count)
    band = x_count * rows
    steps = sorted({dz for dz, _ in shifts})
    dtype = latents_own.dtype
    scale = float(E) ** -0.5

    def assemble(block_refs, weight_ref):
        fsdp_index = lax.axis_index("fsdp")
        z_index = fsdp_index // x_count
        x_index = lax.rem(fsdp_index, x_count)
        for (dz, dx), block_ref in zip(shifts, block_refs):
            place = lax.rem(z_index + z_count - dz, z_count) * x_count + lax.rem(x_index + x_count - dx, x_count)
            weight_ref[pl.ds(pl.multiple_of(place * rows, 16), rows), :] = block_ref[:rows, :]
        starts = [pl.multiple_of(lax.rem(z_index + z_count - dz, z_count) * band, LANES) for dz in steps]
        return starts, jnp.concatenate([weight_ref[pl.ds(start, band), :] for start in starts], axis=0)

    def partial(latents_ref, starts, weight):
        latents = jnp.concatenate([latents_ref[:, pl.ds(start, band)] for start in starts], axis=1)
        return jnp.dot(latents, weight, preferred_element_type=jnp.float32)

    def first(own_ref, other_ref, *refs):
        block_refs = refs[:count]
        latents_ref, weight_ref, total_ref, sem = refs[count:]
        fetch = pltpu.make_async_copy(own_ref, latents_ref, sem)
        fetch.start()
        starts, weight = assemble(block_refs, weight_ref)
        total_ref[1] = partial(other_ref, starts, weight)
        fetch.wait()
        total_ref[0] = partial(latents_ref, starts, weight)

    def rest(own_ref, other_ref, old_weight_ref, total_ref, near_ref, *refs):
        block_refs = refs[:count]
        queries_ref, weight_ref, key_value_ref = refs[count:]
        starts, weight = assemble(block_refs, weight_ref)
        for member, from_ref in enumerate((own_ref, other_ref)):
            projected = (total_ref[member] + partial(from_ref, starts, weight)).astype(dtype)
            queries_ref[member] = projected[:, :own] * jnp.asarray(scale, dtype)
            key_value_ref[member * row_count : (member + 1) * row_count, :] = projected[:, own:]
        key_value_ref[CORES * row_count :, :] = jnp.dot(
            near_ref[...], weight_ref[:, own:], preferred_element_type=jnp.float32
        ).astype(dtype)

    weight_shape = shaped((depth, columns), dtype)
    if early is None:
        return call(
            first,
            "project_first",
            [HBM] + [VMEM] * (count + 1),
            [shaped((row_count, depth), dtype), weight_shape, shaped((CORES, row_count, columns), jnp.float32)],
            scratch_shapes=[pltpu.SemaphoreType.DMA(())],
            cost=COST1,
        )(latents_own, latents_other, *blocks)
    own_tile, weight, total = early
    return call(
        rest,
        "project",
        [VMEM] * (count + 5),
        [
            shaped((CORES, row_count, own), dtype),
            weight_shape,
            shaped(((CORES + 1) * row_count, 2 * own), dtype),
        ],
        cost=COST1,
        aliases={2: 1},
    )(own_tile, latents_other, weight, total, near, *blocks)


def project_whole(z_count, x_count, shifts, blocks, latents_own, latents_other, near):
    count = len(blocks)
    columns = blocks[0].shape[1]
    own = columns // 3
    row_count, depth = latents_own.shape
    rows = depth // count
    dtype = latents_own.dtype
    scale = float(E) ** -0.5

    def kernel(own_ref, other_ref, near_ref, *refs):
        block_refs = refs[:count]
        queries_ref, weight_ref, key_value_ref, latents_ref, sem = refs[count:]
        fetch = pltpu.make_async_copy(own_ref, latents_ref, sem)
        fetch.start()
        fsdp_index = lax.axis_index("fsdp")
        z_index = fsdp_index // x_count
        x_index = lax.rem(fsdp_index, x_count)
        for (dz, dx), block_ref in zip(shifts, block_refs):
            place = lax.rem(z_index + z_count - dz, z_count) * x_count + lax.rem(x_index + x_count - dx, x_count)
            weight_ref[pl.ds(pl.multiple_of(place * rows, 16), rows), :] = block_ref[:rows, :]
        for member, from_ref in ((1, other_ref), (0, latents_ref)):
            if member == 0:
                fetch.wait()
            projected = jnp.dot(from_ref[...], weight_ref[...], preferred_element_type=jnp.float32).astype(dtype)
            queries_ref[member] = projected[:, :own] * jnp.asarray(scale, dtype)
            key_value_ref[member * row_count : (member + 1) * row_count, :] = projected[:, own:]
        key_value_ref[CORES * row_count :, :] = jnp.dot(
            near_ref[...], weight_ref[:, own:], preferred_element_type=jnp.float32
        ).astype(dtype)

    return call(
        kernel,
        "project",
        [HBM] + [VMEM] * (count + 2),
        [
            shaped((CORES, row_count, own), dtype),
            shaped((depth, columns), dtype),
            shaped(((CORES + 1) * row_count, 2 * own), dtype),
        ],
        scratch_shapes=[pltpu.VMEM((row_count, depth), dtype), pltpu.SemaphoreType.DMA(())],
        cost=COST1,
    )(latents_own, latents_other, near, *blocks)


def attend(seq_count, sources, key_value, state, last, weight, queries, tile_mask, tile_counts):
    columns = weight.shape[1]
    own = columns // 3
    row_count = queries.shape[1]
    dtype = queries.dtype
    groups = own // LANES
    local_rows = 0 if key_value is None else key_value.shape[0]
    slots = local_rows + len(sources) * row_count
    given = [weight, queries] + [latents for latents, _, _ in sources]
    given += [array for array in (key_value, state) if array is not None]

    def kernel(mask_ref, count_ref, weight_ref, queries_ref, *refs):
        latents_refs, refs = refs[: len(sources)], list(refs[len(sources) :])
        key_value_ref = None if key_value is None else refs.pop(0)
        old_ref = None if state is None else refs.pop(0)
        values_ref, keys_ref = refs.pop(), refs.pop()
        seq_index = lax.axis_index("seq")
        core = lax.rem(seq_index, CORES)
        chip_tile = seq_index - core
        tiles = [chip_tile + core, chip_tile + 1 - core]
        ends = [jnp.int32(0)]
        spans = []

        def place(key_tile, keys, values):
            rows = pl.ds(pl.multiple_of(ends[-1], GRAIN), keys.shape[0])
            keys_ref[rows, :] = keys
            for group in range(groups):
                first = 2 * group * LANES
                values_ref[rows, first : first + LANES] = values[:, group * LANES : (group + 1) * LANES]
            spans.append((key_tile, ends[-1]))
            ends.append(ends[-1] + count_ref[key_tile])

        def tile_of(y_step, swapped):
            from_same = lax.rem(seq_index + seq_count - CORES * y_step, seq_count)
            return from_same + 1 - 2 * core if swapped else from_same

        for index, key_tile in enumerate([*tiles, tile_of(1, False)] if local_rows else []):
            rows = slice(index * row_count, (index + 1) * row_count)
            place(key_tile, key_value_ref[rows, :own], key_value_ref[rows, own:])
        for part, (_, y_step, swapped) in enumerate(sources):
            projected = jnp.dot(
                latents_refs[part][...], weight_ref[:, own:], preferred_element_type=jnp.float32
            ).astype(dtype)
            place(tile_of(y_step, swapped), projected[:, :own], projected[:, own:])
        rest = pl.ds(pl.multiple_of(spans[-1][1] + row_count, GRAIN), BLOCK)
        keys_ref[rest, :] = jnp.zeros((BLOCK, own), dtype)
        values_ref[rest, :] = jnp.zeros((BLOCK, 2 * own), dtype)
        for group in range(groups):
            first = (2 * group + 1) * LANES
            values_ref[:, first : first + LANES] = jnp.ones((slots + BLOCK, LANES), dtype)

        def over(keys_taken):
            later = []
            slot = lax.broadcasted_iota(jnp.int32, (1, keys_taken), 1)
            for member in range(CORES):
                bias = jnp.full((1, keys_taken), NEG, jnp.float32)
                for key_tile, start in spans:
                    end = start + jnp.where(mask_ref[tiles[member], key_tile] > 0, count_ref[key_tile], 0)
                    bias = jnp.where((slot >= start) & (slot < end), 0.0, bias)
                for group in range(groups):
                    lanes = slice(group * LANES, (group + 1) * LANES)
                    for start in range(0, row_count, ROWS):
                        chunk = slice(start, start + ROWS)

                        def rows_of(member=member, group=group, lanes=lanes, start=start, chunk=chunk, bias=bias):
                            parts = attend_part(
                                queries_ref[member, chunk, lanes],
                                keys_ref[:keys_taken, lanes],
                                values_ref[:keys_taken, 2 * group * LANES : 2 * (group + 1) * LANES],
                                bias,
                            )
                            if old_ref is not None:
                                parts = merge([old_ref[member, which, chunk, lanes] for which in range(3)], parts)
                            if last:
                                position = start + lax.broadcasted_iota(jnp.int32, (ROWS, 1), 0)
                                attended = jnp.where(position < count_ref[tiles[member]], parts[2] / parts[1], 0.0)
                                refs[member][chunk, lanes] = attended.astype(dtype)
                            else:
                                for which, part in enumerate(parts):
                                    refs[0][member, which, chunk, lanes] = part

                        if last and start:
                            refs[member][chunk, lanes] = jnp.zeros((ROWS, LANES), dtype)
                            later.append((count_ref[tiles[member]] > start, rows_of))
                        else:
                            rows_of()
            for live, rows_of in later:
                pl.when(live)(rows_of)

        blocks = (ends[-1] + BLOCK - 1) // BLOCK
        fewest, most = max(slots // (2 * BLOCK), 1), slots // BLOCK
        for taken in range(fewest, most + 1):
            fits = blocks <= taken if taken == fewest else blocks == taken
            pl.when(fits)(lambda taken=taken: over(taken * BLOCK))

    if last:
        out_shapes = [shaped((row_count, own), dtype)] * CORES
    else:
        out_shapes = [shaped((CORES, 3, row_count, own), jnp.float32)]
    return call(
        kernel,
        "attend_last" if last else "attend",
        [SMEM, SMEM] + [VMEM] * len(given),
        out_shapes,
        scratch_shapes=[pltpu.VMEM((slots + BLOCK, own), dtype), pltpu.VMEM((slots + BLOCK, 2 * own), dtype)],
        cost=COST,
    )(tile_mask, tile_counts, *given)


def project_out(attended_own, attended_partner, out_own, out_partner):
    row_count, own = attended_own.shape
    side = out_own.shape[1]
    strip = side // 3 if side % (3 * BLOCK) == 0 else side
    dtype = attended_own.dtype

    def kernel(own_ref, partner_ref, out_own_ref, out_partner_ref, result_ref, staged_ref, sems):
        core = lax.rem(lax.axis_index("seq"), CORES)
        own_rows = pl.ds(pl.multiple_of(core * own, 16), own)
        partner_rows = pl.ds(pl.multiple_of((1 - core) * own, 16), own)
        copies = []
        for half, weight_ref in enumerate((out_own_ref, out_partner_ref)):
            for first in range(0, side, strip):
                columns = slice(first, first + strip)
                total = jnp.dot(own_ref[...], weight_ref[own_rows, columns], preferred_element_type=jnp.float32)
                total += jnp.dot(partner_ref[...], weight_ref[partner_rows, columns], preferred_element_type=jnp.float32)
                staged_ref[half, :, columns] = total.astype(dtype)
                start = pl.multiple_of((core if half == 0 else 1 - core) * side + first, LANES)
                copies.append(
                    pltpu.make_async_copy(
                        staged_ref.at[half, :, columns], result_ref.at[:, pl.ds(start, strip)], sems.at[len(copies)]
                    )
                )
                copies[-1].start()
        for copy in copies:
            copy.wait()

    return call(
        kernel,
        "project_out",
        [VMEM] * 4,
        [shaped((row_count, CORES * side), dtype)],
        [HBM],
        scratch_shapes=[pltpu.VMEM((CORES, row_count, side), dtype), pltpu.SemaphoreType.DMA((CORES * side // strip,))],
    )(attended_own, attended_partner, out_own, out_partner)[0]


def after(array, *others):
    return lax.optimization_barrier((array, *others))[0]


def local(latents, qkv_weight, out_weight, tile_mask, tile_counts):
    seq_count = lax.axis_size("seq")
    fsdp_count = lax.axis_size("fsdp")
    z_count, x_count = grid_of(fsdp_count)
    chips = seq_count // CORES
    latents_own = latents[0]

    def hop(array, z_step, x_step):
        return lax.ppermute(array, "fsdp", rotation(z_count, x_count, z_step, x_step))

    def flip(array, shift):
        return lax.ppermute(array, "fsdp", [(f, f ^ (shift * x_count)) for f in range(fsdp_count)])

    along_y = [y_rotation(latents_own, seq_count, step) for step in range(1, chips)]
    latents_other = core_swap(latents_own, seq_count)
    half, packed = halves(qkv_weight, out_weight)

    came = {(0, 0): half}
    for x_step in range(1, x_count):
        came[0, x_step] = hop(after(packed, latents_other), 0, x_step)
    beside = [came[0, x_step] for x_step in range(1, x_count)]
    turn = z_count // 2
    for z_step in (turn, 1):
        came[z_step, 0] = hop(packed if z_step == turn else half, z_step, 0)
    second = after(half, came[1, 0], *beside)
    third = after(half, came[turn, 0])
    for x_step in range(1, x_count):
        came[turn, x_step] = hop(came[turn, 0], 0, x_step)
        came[1, x_step] = hop(second, 1, x_step)
    for z_step in range(2, z_count):
        if z_step != turn:
            came[z_step, 0] = hop(second, z_step, 0)
            for x_step in range(1, x_count):
                came[z_step, x_step] = hop(third, z_step, x_step)

    axes = (z_count, x_count)
    early = None
    if x_count * half.shape[0] % LANES == 0:
        sooner = [shift for shift in came if shift[0] in (0, turn)]
        early = project(*axes, sooner, [came[shift] for shift in sooner], latents_own, latents_other)
        packed = after(packed, early[2])

    out_own = collect(
        [[packed] + beside, [came[turn, x_step] for x_step in range(x_count)]],
        x_count,
        z_count,
        half.shape[0],
        out_weight.shape[0],
        out_weight.shape[1] // CORES,
    )
    units, shift = 2, turn // 2
    while shift > 1:
        out_own = pair_up(out_own, flip(out_own, shift), units, shift, x_count)
        units, shift = 2 * units, shift // 2
    out_got = flip(out_own, shift)

    near = after(along_y, out_own, *list(came.values())[1:])
    far = [core_swap(array, seq_count) for array in near]
    if early is not None:
        later = [shift for shift in came if shift not in sooner]
        came[later[-1]] = after(came[later[-1]], *near)
        queries, weight, key_value = project(
            *axes, later, [came[shift] for shift in later], latents_own, latents_other, near[0], early
        )
    else:
        came[0, 0] = after(half, *near)
        queries, weight, key_value = project_whole(
            *axes, list(came), list(came.values()), latents_own, latents_other, near[0]
        )
    state = None
    for step in range(1, chips):
        last = step == chips - 1
        result = attend(
            seq_count,
            [(near[step - 1], step, False)] * (step > 1) + [(far[step - 1], step, True)],
            key_value if step == 1 else None,
            state,
            last,
            weight,
            queries,
            tile_mask,
            tile_counts,
        )
        state = None if last else result[0]
    attended_own, attended_other = result
    attended_partner = core_swap(attended_other, seq_count)
    out_own = pair_up(out_own, after(out_got, attended_other), units, shift, x_count)
    out_partner = core_swap(out_own, seq_count)
    return project_out(attended_own, attended_partner, out_own, out_partner)[None]


def solution(mesh):
    return jax.shard_map(
        local,
        mesh=mesh,
        in_specs=(P("fsdp", "seq", None), P("fsdp", None), P("fsdp", None), P(), P()),
        out_specs=P("fsdp", "seq", None),
        check_vma=False,
    )
```
